32 devices in a mesh: seq: 8 (over y, x, core), grp: 4 (over z).
Axes of the slice: x: 2, y: 2, z: 4, core: 2. Of those that a mesh axis runs over, the one named last changes fastest.
Arguments:
- hidden: bfloat16 [4, 4, 2, 1024, 768], P(None, 'grp', None, 'seq'), may hold values from -6 to 6
- lengths: int32 [4, 4, 2], P(None, 'grp'), may hold values from 128 to 1024, as said below
- query_weight: bfloat16 [768, 768], replicated, may hold values from -0.625 to 0.625
- key_weight: bfloat16 [768, 768], replicated, may hold values from -0.21875 to 0.21875
- value_weight: bfloat16 [768, 768], replicated, may hold values from -0.21875 to 0.21875
- w_rel: bfloat16 [12, 64, 64], replicated, may hold values from -0.75 to 0.75
- output_weight: bfloat16 [768, 768], replicated, may hold values from -0.875 to 0.875
- gain_attn: bfloat16 [768], replicated, may hold values from 0.099609375 to 1.8984375
- inner_weight: bfloat16 [768, 3072], replicated, may hold values from -0.21875 to 0.21875
- outer_weight: bfloat16 [3072, 768], replicated, may hold values from -0.109375 to 0.109375
- gain_ffn: bfloat16 [768], replicated, may hold values from 0.099609375 to 1.8984375
- cotangent: bfloat16 [4, 4, 2, 512, 768], P(None, 'grp', None, 'seq'), may hold values from -6 to 6
Outputs:
- pooled_out: bfloat16 [4, 4, 2, 512, 768], P(None, 'grp', None, 'seq')
- grad_hidden: bfloat16 [4, 4, 2, 1024, 768], P(None, 'grp', None, 'seq')
- grad_w_query: float32 [768, 768], P(('seq', 'grp'))
- grad_w_key: float32 [768, 768], P(('seq', 'grp'))
- grad_w_value: float32 [768, 768], P(('seq', 'grp'))
- grad_w_rel: float32 [12, 64, 64], replicated
- grad_w_out: float32 [768, 768], P(('seq', 'grp'))
- grad_gain_attn: float32 [768], replicated
- grad_w_inner: float32 [768, 3072], P(('seq', 'grp'))
- grad_w_outer: float32 [3072, 768], P(('seq', 'grp'))
- grad_gain_ffn: float32 [768], replicated
The draws below stay inside these ranges and needn't reach their ends.
Inputs may be any that keep to these rules, and one draw needn't show every extreme that they name: `lengths`: in every bucket group one sequence has 1024 positions.
All inputs are finite; a program needn't handle non-finite values.
Results may differ from the reference program's by a relative error of at most 0.022.
Values may be sent and summed in bfloat16 or wider, within the bound.
A program may use at most 256 MiB of HBM per device.

```python
import math
import jax
import jax.numpy as jnp
from jax import lax

H = 12
HD = 64
D = 768
FF = 3072
SLOT = 1024
MB = 4
SEQS = 2
GROUPS = 4


def draw_lengths(key, part):
    key_base, key_pick = jax.random.split(key)
    base_len = jax.random.randint(key_base, (MB, GROUPS, SEQS), SLOT // 8, SLOT + 1)
    chosen = jax.random.randint(key_pick, (GROUPS,), 0, MB * SEQS)
    slot_index = jnp.arange(MB, dtype=jnp.int32)[:, None, None] * SEQS + jnp.arange(SEQS, dtype=jnp.int32)[None, None, :]
    return jnp.where(slot_index == chosen[None, :, None], SLOT, base_len).astype(jnp.int32)


def level_of(rng, dims, shards, low, high):
    def one(axis_at, parts):
        draws = jax.random.uniform(jax.random.fold_in(jax.random.fold_in(rng, 6), axis_at), (parts,), jnp.float32, low / len(shards), high / len(shards))
        return jnp.repeat(jnp.exp(draws), dims[axis_at] // parts).reshape((-1,) + (1,) * (len(dims) - axis_at - 1))

    level = one(*shards[0])
    for cut in shards[1:]:
        level = level * one(*cut)
    return level


def bell_draw(stream_key, shape, scale, bound, shards=(), kind=jnp.bfloat16):
    gain = level_of(stream_key, shape, shards, -0.22, 0.18) if shards else 1.0
    values = jax.random.normal(stream_key, shape, jnp.float32) * scale * gain
    return jnp.minimum(jnp.maximum(values, -bound), bound).astype(kind)


def setup_inputs(seed: int = 0) -> dict:
    keys = jax.random.split(jax.random.key(seed), 13)
    hidden = bell_draw(keys[0], (MB, GROUPS, SEQS, SLOT, D), 1.0, 6.0, ((1, 4), (3, 8)))
    lengths = draw_lengths(jax.random.fold_in(keys[12], 71), 0)
    query_weight = bell_draw(keys[2], (D, D), (D // 8) ** -0.5, 0.625)
    key_weight = bell_draw(keys[3], (D, D), D ** -0.5, 0.21875)
    value_weight = bell_draw(keys[4], (D, D), D ** -0.5, 0.21875)
    w_rel = bell_draw(keys[5], (H, HD, HD), HD ** -0.5, 0.75)
    output_weight = bell_draw(keys[6], (D, D), (D // 16) ** -0.5, 0.875)
    gain_attn = jnp.clip(1.0 + 0.18 * jax.random.normal(keys[7], (D,), jnp.float32), 0.099609375, 1.8984375).astype(jnp.bfloat16)
    inner_weight = bell_draw(keys[8], (D, FF), D ** -0.5, 0.21875)
    outer_weight = bell_draw(keys[9], (FF, D), FF ** -0.5, 0.109375)
    gain_ffn = jnp.clip(1.0 + 0.18 * jax.random.normal(keys[10], (D,), jnp.float32), 0.099609375, 1.8984375).astype(jnp.bfloat16)
    cotangent = bell_draw(keys[11], (MB, GROUPS, SEQS, SLOT // 2, D), 1.0, 6.0, ((1, 4), (3, 8)))
    return dict(hidden=hidden, lengths=lengths, query_weight=query_weight, key_weight=key_weight, value_weight=value_weight, w_rel=w_rel, output_weight=output_weight, gain_attn=gain_attn, inner_weight=inner_weight, outer_weight=outer_weight, gain_ffn=gain_ffn, cotangent=cotangent)


@jax.custom_vjp
def low(v):
    return lax.optimization_barrier(v.astype(jnp.bfloat16)).astype(jnp.float32)

@jax.custom_vjp
def low_back(v):
    return v

def low_keep(v):
    return (low(v), None)

def low_pass(kept, grad):
    return (grad,)

def back_keep(v):
    return (v, None)

def back_low(kept, grad):
    return (low(grad),)
low.defvjp(low_keep, low_pass)
low_back.defvjp(back_keep, back_low)

def rates_of(freq_count):
    return jnp.exp(-jnp.arange(freq_count, dtype=jnp.float32) * (math.log(10000.0) / freq_count))

def features(positions, freq_count):
    angles = positions.astype(jnp.float32)[:, None] * rates_of(freq_count)[None, :]
    return jnp.concatenate([jnp.sin(angles), jnp.cos(angles)], 1)

def turning(positions, freq_count):
    angles = 2.0 * positions.astype(jnp.float32)[:, None] * rates_of(freq_count)[None, :]
    return (jnp.cos(angles), jnp.sin(angles))

def rotate(rel_proj, cosines, sine_terms, freq_count):
    sin_part = rel_proj[..., :freq_count]
    cos_part = rel_proj[..., freq_count:]
    cosines = cosines[:, None, :]
    sine_terms = sine_terms[:, None, :]
    return jnp.concatenate([sin_part * cosines + cos_part * sine_terms, cos_part * cosines - sin_part * sine_terms], -1)

def norm_rows(rows, gain_vec):
    row_mean = lax.optimization_barrier(jnp.mean(rows, -1, keepdims=True))
    centered = rows - row_mean
    variance = lax.optimization_barrier(jnp.mean(centered * centered, -1, keepdims=True))
    return centered * lax.rsqrt(variance + 1e-05) * gain_vec

def layer(params, tokens, seq_length):
    query_weight, key_weight, value_weight, w_rel, output_weight, gain_attn, inner_weight, outer_weight, gain_ffn = params
    highest = lax.Precision.HIGHEST
    half_len = SLOT // 2
    freq_count = HD // 2
    pooled = tokens.reshape(half_len, 2, D).mean(1)
    pooled_short_rows = low(pooled)
    query = low_back(low(jnp.dot(pooled_short_rows, query_weight, precision=highest)))
    query_heads = query.reshape(half_len, H, HD)
    query_pos = jnp.arange(half_len, dtype=jnp.int32)
    rel_proj = low_back(jnp.einsum('qhd,hde->qhe', query_heads, w_rel, precision=highest))
    cosines, sine_terms = turning(query_pos, freq_count)
    shifted = low(rotate(rel_proj, cosines, sine_terms, freq_count))
    keys_low = low_back(low(jnp.dot(tokens, key_weight, precision=highest))).reshape(SLOT, H, HD)
    values_low = low_back(low(jnp.dot(tokens, value_weight, precision=highest))).reshape(SLOT, H, HD)
    key_pos = jnp.arange(SLOT, dtype=jnp.int32)
    key_feat = low(features(key_pos, freq_count))
    raw_scores = jnp.einsum('qhd,khd->hqk', query_heads, keys_low, precision=highest)
    raw_scores = raw_scores + jnp.einsum('qhe,ke->hqk', shifted, key_feat, precision=highest)
    scores = low_back(raw_scores * 0.125)
    scores = jnp.where((key_pos < seq_length)[None, None, :], scores, -1e+30)
    row_max = lax.optimization_barrier(jnp.max(scores, -1, keepdims=True))
    exp_scores = jnp.exp(scores - row_max)
    probability = exp_scores / lax.optimization_barrier(jnp.sum(exp_scores, -1, keepdims=True))
    attn_out = jnp.einsum('hqk,khd->qhd', low(probability), values_low, precision=highest).reshape(half_len, D)
    attn_out = low_back(low(attn_out))
    branch = low_back(jnp.dot(attn_out, output_weight, precision=highest))
    mixed_rows = norm_rows(pooled + branch, gain_attn)
    inner_pre = low_back(jnp.dot(low(mixed_rows), inner_weight, precision=highest))
    active = low(jax.nn.gelu(inner_pre, approximate=False))
    outer_out = low_back(jnp.dot(active, outer_weight, precision=highest))
    normed = norm_rows(mixed_rows + outer_out, gain_ffn)
    return normed * (2 * query_pos < seq_length).astype(jnp.float32)[:, None]

def add_up(left_val, right_val):
    return left_val + right_val

def reference(hidden, lengths, query_weight, key_weight, value_weight, w_rel, output_weight, gain_attn, inner_weight, outer_weight, gain_ffn, cotangent):
    params = (query_weight.astype(jnp.float32), key_weight.astype(jnp.float32), value_weight.astype(jnp.float32), w_rel.astype(jnp.float32), output_weight.astype(jnp.float32), gain_attn.astype(jnp.float32), inner_weight.astype(jnp.float32), outer_weight.astype(jnp.float32), gain_ffn.astype(jnp.float32))
    seq_total = MB * GROUPS * SEQS
    tokens_all = hidden.astype(jnp.float32).reshape(seq_total, SLOT, D)
    cot_all = cotangent.astype(jnp.float32).reshape(seq_total, SLOT // 2, D)
    length_all = lengths.reshape(seq_total).astype(jnp.int32)

    def one_sequence(grad_sums, sequence):
        tokens, seq_length, cot_rows = sequence

        def forward(weights, inputs):
            return layer(weights, inputs, seq_length)
        result, pullback = jax.vjp(forward, params, tokens)
        grad_params, grad_tokens = pullback(cot_rows)
        grad_sums = jax.tree.map(add_up, grad_sums, grad_params)
        return (grad_sums, (result.astype(jnp.bfloat16), grad_tokens.astype(jnp.bfloat16)))
    zero_grads = jax.tree.map(jnp.zeros_like, params)
    grad_sums, (results, grad_inputs) = lax.scan(one_sequence, zero_grads, (tokens_all, length_all, cot_all))
    pooled_out = results.reshape(MB, GROUPS, SEQS, SLOT // 2, D)
    grad_hidden = grad_inputs.reshape(MB, GROUPS, SEQS, SLOT, D)
    return (pooled_out, grad_hidden, grad_sums[0], grad_sums[1], grad_sums[2], grad_sums[3], grad_sums[4], grad_sums[5], grad_sums[6], grad_sums[7], grad_sums[8])
```

```python
import functools
import math

import jax
import jax.numpy as jnp
from jax import lax
from jax.experimental import pallas as pl
from jax.experimental.pallas import tpu as pltpu
from jax.sharding import PartitionSpec as P

BF = jnp.bfloat16
F32 = jnp.float32
I32 = jnp.int32
MESH = pl.DeviceIdType.MESH
VMEM_LIMIT = 58 << 20
EPS = 1e-05
FFC = 512
QT = 128


def sds(shape, dtype):
    return jax.ShapeDtypeStruct(shape, dtype)


def mm(a, b):
    return lax.dot_general(a, b, (((1,), (0,)), ((), ())), preferred_element_type=F32)


def mm_nt(a, b):
    return lax.dot_general(a, b, (((1,), (1,)), ((), ())), preferred_element_type=F32)


def mm_tn(a, b):
    return lax.dot_general(a, b, (((0,), (0,)), ((), ())), preferred_element_type=F32)


def full(shape):
    zeros = (0,) * len(shape)
    return pl.BlockSpec(shape, lambda *unused: zeros)


def call(body, grid, in_specs, out_specs, out_shape, scratch, flops, moved, scalars=1):
    return pl.pallas_call(
        body,
        grid_spec=pltpu.PrefetchScalarGridSpec(
            num_scalar_prefetch=scalars,
            grid=grid,
            in_specs=in_specs,
            out_specs=out_specs,
            scratch_shapes=scratch,
        ),
        out_shape=out_shape,
        compiler_params=pltpu.CompilerParams(
            dimension_semantics=("arbitrary",) * len(grid), vmem_limit_bytes=VMEM_LIMIT
        ),
        cost_estimate=pl.CostEstimate(flops=flops, bytes_accessed=moved, transcendentals=0),
    )


def rel_of(pos, order):
    bits = len(order)
    rel = 0
    for i, mask in enumerate(order):
        if (pos >> (bits - 1 - i)) & 1:
            rel |= mask
    return rel


def split_rows(val_ref, keep_ref, send_ref, order, me, cols=None):
    count = 2 ** len(order)
    step = val_ref.shape[0] // count
    for pos in range(count):
        start = pl.multiple_of((me ^ rel_of(pos, order)) * step, step)
        rows = val_ref[pl.ds(start, step), :]
        ref = keep_ref if pos < count // 2 else send_ref
        if cols is None:
            ref[pos % (count // 2)] = rows
        else:
            ref[pos % (count // 2), :, cols] = rows


def gather_body(count, src, dst, send_sem, recv_sem, local_sem):
    me = lax.axis_index("seq")
    barrier = pltpu.get_barrier_semaphore()
    for k in range(1, count):
        pl.semaphore_signal(
            barrier, inc=1, device_id={"seq": lax.rem(me + k, count)}, device_id_type=MESH
        )
    pl.semaphore_wait(barrier, count - 1)
    own = pltpu.make_async_copy(src.at[me], dst.at[me], local_sem)
    own.start()
    copies = []
    for k in range(1, count):
        peer = lax.rem(me + k, count)
        copy = pltpu.make_async_remote_copy(
            src_ref=src.at[peer],
            dst_ref=dst.at[me],
            send_sem=send_sem.at[k],
            recv_sem=recv_sem.at[k],
            device_id={"seq": peer},
            device_id_type=MESH,
        )
        copy.start()
        copies.append(copy)
    own.wait()
    for copy in copies:
        copy.wait()


def to_sequence(blocks):
    count = blocks.shape[0]
    return pl.pallas_call(
        functools.partial(gather_body, count),
        out_shape=sds(blocks.shape, blocks.dtype),
        in_specs=[pl.BlockSpec(memory_space=pl.ANY)],
        out_specs=pl.BlockSpec(memory_space=pl.ANY),
        scratch_shapes=[
            pltpu.SemaphoreType.DMA((count,)),
            pltpu.SemaphoreType.DMA((count,)),
            pltpu.SemaphoreType.DMA,
        ],
        compiler_params=pltpu.CompilerParams(
            collective_id=0, has_side_effects=True, vmem_limit_bytes=VMEM_LIMIT
        ),
    )(blocks)


def swap(value, axis, size, mask):
    return lax.ppermute(value, axis, [(i, i ^ mask) for i in range(size)])


def assemble_body(count, sc, *refs):
    out = refs[count]
    me = sc[0]
    for k in range(count):
        out[me ^ k] = refs[k][...]


def assemble(sc, pieces):
    count = len(pieces)
    shape = (count,) + pieces[0].shape
    size = math.prod(shape) * 4
    return call(
        functools.partial(assemble_body, count),
        (1,),
        [full(p.shape) for p in pieces],
        full(shape),
        sds(shape, pieces[0].dtype),
        [],
        0,
        size,
    )(sc, *pieces)


def pool_matrix(rows):
    row = lax.broadcasted_iota(I32, (rows, 2 * rows), 0)
    col = lax.broadcasted_iota(I32, (rows, 2 * rows), 1)
    return jnp.where((col == 2 * row) | (col == 2 * row + 1), 0.5, 0.0).astype(BF)


def attend_body(
    heads, sc, x_ref, wq_ref, wk_ref, wv_ref, bd_ref, cos_ref, sin_ref, feat_ref,
    attn_ref, linv_ref, p_ref, q_ref, k_ref, v_ref, pooled_ref, xt_ref, pt_ref, sh_s,
):
    slot = x_ref.shape[0]
    half = slot // 2
    scale = 0.125 * 1.4426950408889634

    @pl.when(pl.program_id(0) == 0)
    def first():
        pool = pool_matrix(128)
        for t in range(slot // 256):
            tile = x_ref[256 * t : 256 * (t + 1), :]
            rows = mm(pool, tile)
            pooled_ref[128 * t : 128 * (t + 1), :] = rows
            xt_ref[:, 256 * t : 256 * (t + 1)] = tile.T
            pt_ref[:, 128 * t : 128 * (t + 1)] = rows.astype(BF).T

    q = mm(pooled_ref[...].astype(BF), wq_ref[...]).astype(BF)
    q_ref[...] = q
    k_ref[...] = mm(x_ref[...], wk_ref[...]).astype(BF)
    v_ref[...] = mm(x_ref[...], wv_ref[...]).astype(BF)
    rel = mm(q, bd_ref[0])
    lane = lax.broadcasted_iota(I32, (1, 128), 1)
    low = (lane % 64) < 32
    for pair in range(2):
        part = rel[:, 128 * pair : 128 * (pair + 1)]
        other = jnp.where(low, pltpu.roll(part, 96, 1), -pltpu.roll(part, 32, 1))
        sh_s[:, 128 * pair : 128 * (pair + 1)] = (
            part * cos_ref[...] + other * sin_ref[...]
        ).astype(BF)
    key_ok = lax.broadcasted_iota(I32, (1, slot), 1) < sc[1]
    ones = jnp.ones((slot, 128), BF)

    def one_pair(pair, carry):
        cols = pl.ds(pl.multiple_of(pair * 128, 128), 128)
        key_side = jnp.concatenate([k_ref[:, cols], feat_ref[...]], 1)
        value_side = jnp.concatenate([v_ref[:, cols], ones], 1)
        for t in range(half // QT):
            rows = slice(QT * t, QT * (t + 1))
            q_part = q_ref[rows, cols]
            s_part = sh_s[rows, cols]
            outs = []
            for h in range(2):
                mine = (lane < 64) if h == 0 else (lane >= 64)
                zero = jnp.zeros_like(q_part)
                left = jnp.concatenate(
                    [jnp.where(mine, q_part, zero), jnp.where(mine, s_part, zero)], 1
                )
                s = jnp.where(key_ok, mm_nt(left, key_side), -1e30)
                top = jnp.max(s, -1, keepdims=True)
                p = jnp.exp2((s - top) * scale).astype(BF)
                p_ref[pair * 2 + h, rows, :] = p
                acc = mm(p, value_side)
                inv = 1.0 / acc[:, 128:]
                outs.append((acc[:, :128] * inv, inv))
            first_head = lane < 64
            attn_ref[rows, cols] = jnp.where(first_head, outs[0][0], outs[1][0]).astype(BF)
            linv_ref[rows, cols] = jnp.where(first_head, outs[0][1], outs[1][1])
        return carry

    lax.fori_loop(0, 2, one_pair, 0)


def attend(sc, x, wq, wk, wv, bd, cosines, sines, feat):
    slot, width = x.shape
    half = slot // 2
    groups = width // 256
    heads = width // 64
    by_group = lambda rows: pl.BlockSpec((rows, 256), lambda g, s: (0, g))
    return call(
        functools.partial(attend_body, heads),
        (groups,),
        [
            full((slot, width)),
            by_group(width),
            by_group(width),
            by_group(width),
            pl.BlockSpec((1, 256, 256), lambda g, s: (g, 0, 0)),
            full((half, 128)),
            full((half, 128)),
            full((slot, 128)),
        ],
        [
            by_group(half),
            by_group(half),
            pl.BlockSpec((4, half, slot), lambda g, s: (g, 0, 0)),
            by_group(half),
            by_group(slot),
            by_group(slot),
            full((half, width)),
            full((width, slot)),
            full((width, half)),
        ],
        [
            sds((half, width), BF),
            sds((half, width), F32),
            sds((heads, half, slot), BF),
            sds((half, width), BF),
            sds((slot, width), BF),
            sds((slot, width), BF),
            sds((half, width), F32),
            sds((width, slot), BF),
            sds((width, half), BF),
        ],
        [pltpu.VMEM((half, 256), BF)],
        12_000_000_000,
        30_000_000,
    )(sc, x, wq, wk, wv, bd, cosines, sines, feat)


def norm_parts(rows):
    centered = rows - jnp.mean(rows, -1, keepdims=True)
    rstd = lax.rsqrt(jnp.mean(centered * centered, -1, keepdims=True) + EPS)
    return centered * rstd, rstd


def norm_back(grad, unit, rstd, gain):
    scaled = grad * gain
    return rstd * (
        scaled
        - jnp.mean(scaled, -1, keepdims=True)
        - unit * jnp.mean(scaled * unit, -1, keepdims=True)
    )


def feed_body(
    count, sc, attn_ref, pooled_ref, wo_ref, win_ref, wout_ref, g1_ref, g2_ref, *refs
):
    cots = refs[:count]
    outs = refs[count : 2 * count]
    (act_ref, slope_ref, gouter_ref, gtwo_ref, unit_ref, rstd_ref, mixed_ref, dgain_ref) = refs[
        2 * count : 2 * count + 8
    ]
    mixed_s, acc_s, rows_s, cot_s = refs[2 * count + 8 :]
    step = pl.program_id(0)
    me = sc[0]
    half = attn_ref.shape[0]
    block = half // count

    @pl.when(step == 0)
    def first():
        unit, rstd = norm_parts(pooled_ref[...] + mm(attn_ref[...], wo_ref[...]))
        mixed = unit * g1_ref[...]
        unit_ref[...] = unit
        rstd_ref[...] = jnp.broadcast_to(rstd, rstd_ref.shape)
        mixed_s[...] = mixed
        mixed_ref[...] = mixed.astype(BF)
        acc_s[...] = mixed
        for k in range(count):
            start = pl.multiple_of((me ^ k) * block, block)
            cot_s[pl.ds(start, block), :] = cots[k][...]

    pre = mm(mixed_ref[...], win_ref[...])
    cdf = 0.5 * (1.0 + lax.erf(pre * 0.7071067811865476))
    act = (pre * cdf).astype(BF)
    act_ref[...] = act
    slope_ref[...] = (cdf + pre * (jnp.exp(pre * pre * -0.5) * 0.3989422804014327)).astype(BF)
    acc_s[...] += mm(act, wout_ref[...])

    @pl.when(step == pl.num_programs(0) - 1)
    def last():
        unit, rstd = norm_parts(acc_s[...])
        row = lax.broadcasted_iota(I32, (half, 1), 0)
        valid = 2 * row < sc[1]
        rows_s[...] = jnp.where(valid, unit * g2_ref[...], 0.0).astype(BF)
        for k in range(count):
            start = pl.multiple_of((me ^ k) * block, block)
            outs[k][...] = rows_s[pl.ds(start, block), :]
        grad = jnp.where(valid, cot_s[...].astype(F32), 0.0)
        dgain_ref[...] = jnp.sum(grad * unit, 0, keepdims=True)
        two = norm_back(grad, unit, rstd, g2_ref[...])
        gtwo_ref[...] = two
        gouter_ref[...] = two.astype(BF)


def feed(sc, attn, pooled, wo, win, wout, g1, g2, cots):
    half, width = attn.shape
    inner = win.shape[1]
    count = len(cots)
    block = half // count
    return call(
        functools.partial(feed_body, count),
        (inner // FFC,),
        [
            full((half, width)),
            full((half, width)),
            full((width, width)),
            pl.BlockSpec((width, FFC), lambda j, s: (0, j)),
            pl.BlockSpec((FFC, width), lambda j, s: (j, 0)),
            full((1, width)),
            full((1, width)),
        ]
        + [full((block, width))] * count,
        [full((block, width))] * count
        + [
            pl.BlockSpec((half, FFC), lambda j, s: (0, j)),
            pl.BlockSpec((half, FFC), lambda j, s: (0, j)),
            full((half, width)),
            full((half, width)),
            full((half, width)),
            full((half, 128)),
            full((half, width)),
            full((1, width)),
        ],
        [sds((block, width), BF)] * count
        + [
            sds((half, inner), BF),
            sds((half, inner), BF),
            sds((half, width), BF),
            sds((half, width), F32),
            sds((half, width), F32),
            sds((half, 128), F32),
            sds((half, width), BF),
            sds((1, width), F32),
        ],
        [
            pltpu.VMEM((half, width), F32),
            pltpu.VMEM((half, width), F32),
            pltpu.VMEM((half, width), BF),
            pltpu.VMEM((half, width), BF),
        ],
        5_500_000_000,
        24_000_000,
    )(sc, attn, pooled, wo, win, wout, g1, g2, *cots)


def wouter_body(count, sc, act_ref, gouter_ref, keep_ref, send_ref):
    val = mm_tn(act_ref[...], gouter_ref[...]).astype(BF)
    pos = pl.program_id(0)

    @pl.when(pos < count // 2)
    def near():
        keep_ref[0] = val

    @pl.when(pos >= count // 2)
    def far():
        send_ref[0] = val


def wouter(sc, act, gouter, order):
    half, inner = act.shape
    width = gouter.shape[1]
    count = 2 ** len(order)
    rows = inner // count
    mid = count // 2

    def column(pos, s):
        rel = 0
        for i, mask in enumerate(order):
            rel = rel + ((pos >> (len(order) - 1 - i)) & 1) * mask
        return (0, s[0] ^ rel)

    return call(
        functools.partial(wouter_body, count),
        (count,),
        [pl.BlockSpec((half, rows), column), full((half, width))],
        [
            pl.BlockSpec((1, rows, width), lambda p, s: (jnp.minimum(p, mid - 1), 0, 0)),
            pl.BlockSpec((1, rows, width), lambda p, s: (jnp.maximum(p - mid, 0), 0, 0)),
        ],
        [sds((mid, rows, width), BF)] * 2,
        [],
        2_500_000_000,
        9_000_000,
    )(sc, act, gouter)


def back_body(
    order, sc, gouter_ref, slope_ref, wout_ref, win_ref, mixed_ref, gtwo_ref, unit_ref, rstd_ref,
    g1_ref, wo_ref, attn_ref, ga_ref, gone_ref, dgain_ref, ikeep_ref, isend_ref, okeep_ref,
    osend_ref, acc_s, mt_s, val_s,
):
    step = pl.program_id(0)
    me = sc[0]

    @pl.when(step == 0)
    def first():
        acc_s[...] = gtwo_ref[...]
        mt_s[...] = mixed_ref[...].T

    inner = (slope_ref[...].astype(F32) * mm_nt(gouter_ref[...], wout_ref[...])).astype(BF)
    acc_s[...] += mm_nt(inner, win_ref[...])
    val_s[...] = mm(mt_s[...], inner).astype(BF)
    split_rows(val_s, ikeep_ref, isend_ref, order, me)

    @pl.when(step == pl.num_programs(0) - 1)
    def last():
        grad = acc_s[...]
        unit = unit_ref[...]
        dgain_ref[...] = jnp.sum(grad * unit, 0, keepdims=True)
        one = norm_back(grad, unit, rstd_ref[:, :1], g1_ref[...])
        gone_ref[...] = one
        branch = one.astype(BF)
        ga_ref[...] = mm_nt(branch, wo_ref[...])
        at = attn_ref[...].T
        width = at.shape[0]
        for c in range(0, width, FFC):
            size = min(FFC, width - c)
            val_s[:, :size] = mm(at, branch[:, c : c + size]).astype(BF)
            split_rows(val_s.at[:, :size], okeep_ref, osend_ref, order, me, slice(c, c + size))


def back(sc, gouter, slope, wout, win, mixed, gtwo, unit, rstd, g1, wo, attn, order):
    half, width = gouter.shape
    inner = slope.shape[1]
    count = 2 ** len(order)
    mid = count // 2
    rows = width // count
    wide = pl.BlockSpec((mid, rows, FFC), lambda j, s: (0, 0, j))
    return call(
        functools.partial(back_body, order),
        (inner // FFC,),
        [
            full((half, width)),
            pl.BlockSpec((half, FFC), lambda j, s: (0, j)),
            pl.BlockSpec((FFC, width), lambda j, s: (j, 0)),
            pl.BlockSpec((width, FFC), lambda j, s: (0, j)),
            full((half, width)),
            full((half, width)),
            full((half, width)),
            full((half, 128)),
            full((1, width)),
            full((width, width)),
            full((half, width)),
        ],
        [
            full((half, width)),
            full((half, width)),
            full((1, width)),
            wide,
            wide,
            full((mid, rows, width)),
            full((mid, rows, width)),
        ],
        [
            sds((half, width), F32),
            sds((half, width), F32),
            sds((1, width), F32),
            sds((mid, rows, inner), BF),
            sds((mid, rows, inner), BF),
            sds((mid, rows, width), BF),
            sds((mid, rows, width), BF),
        ],
        [
            pltpu.VMEM((half, width), F32),
            pltpu.VMEM((width, half), BF),
            pltpu.VMEM((width, FFC), BF),
        ],
        8_400_000_000,
        30_000_000,
    )(sc, gouter, slope, wout, win, mixed, gtwo, unit, rstd, g1, wo, attn)


def unattend_body(
    order, sc, p_ref, q_ref, k_ref, v_ref, ga_ref, attn_ref, linv_ref, xt_ref, pt_ref, bd_ref,
    cos_ref, sin_ref, feat_ref, dk_ref, dv_ref, gq_ref, drel_ref, keep_ref, send_ref,
    gs_s, d_s, qt_s, gt_s, gqf_s, rel_s, ds_s, kt_s, vt_s, val_s,
):
    half = q_ref.shape[0]
    slot = k_ref.shape[0]
    me = sc[0]
    scaled = ga_ref[...] * linv_ref[...]
    d_s[...] = scaled * attn_ref[...].astype(F32)
    gs = scaled.astype(BF)
    gs_s[...] = gs
    gt_s[...] = gs.T
    qt_s[...] = q_ref[...].T
    lane = lax.broadcasted_iota(I32, (1, 128), 1)
    low = (lane % 64) < 32
    first_head = lane < 64
    ones = jnp.broadcast_to(jnp.where(lane < 2, 1.0, 0.0).astype(BF), (slot, 128))

    def one_pair(pair, carry):
        cols = pl.ds(pl.multiple_of(pair * 128, 128), 128)
        key_side = jnp.concatenate([k_ref[:, cols], feat_ref[...]], 1)
        value_side = jnp.concatenate([v_ref[:, cols], ones], 1)
        outs = [[], []]
        for h in range(2):
            mine = first_head if h == 0 else jnp.logical_not(first_head)
            head = pair * 2 + h
            for t in range(half // QT):
                rows = slice(QT * t, QT * (t + 1))
                g_part = gs_s[rows, cols]
                delta = jnp.sum(jnp.where(mine, d_s[rows, cols], 0.0), -1, keepdims=True)
                coarse = delta.astype(BF).astype(F32)
                tail = jnp.where(lane == 0, coarse, jnp.where(lane == 1, delta - coarse, 0.0))
                left = jnp.concatenate(
                    [jnp.where(mine, g_part, jnp.zeros_like(g_part)), (-tail).astype(BF)], 1
                )
                ds = (p_ref[head, rows, :].astype(F32) * mm_nt(left, value_side)).astype(BF)
                ds_s[rows, :] = ds
                outs[h].append(mm(ds, key_side))
            lines = pl.ds(pl.multiple_of(head * 64, 64), 64)
            kt_s[lines, :] = (mm(qt_s[lines, :], ds_s[...]) * 0.125).astype(BF)
            vt_s[lines, :] = mm(gt_s[lines, :], p_ref[head]).astype(BF)
        for t in range(half // QT):
            rows = slice(QT * t, QT * (t + 1))
            a, b = outs[0][t], outs[1][t]
            gqf_s[rows, cols] = jnp.where(first_head, a[:, :128], b[:, :128]) * 0.125
            shift = jnp.where(first_head, a[:, 128:], b[:, 128:]) * 0.125
            other = jnp.where(low, -pltpu.roll(shift, 96, 1), pltpu.roll(shift, 32, 1))
            rel_s[rows, cols] = (shift * cos_ref[rows, :] + other * sin_ref[rows, :]).astype(BF)
        return carry

    lax.fori_loop(0, 2, one_pair, 0)
    rel = rel_s[...]
    drel_ref[...] = mm(qt_s[...], rel)
    gq = (gqf_s[...] + mm_nt(rel, bd_ref[0])).astype(BF)
    gq_ref[...] = gq
    dk = kt_s[...].T
    dv = vt_s[...].T
    dk_ref[...] = dk
    dv_ref[...] = dv
    val_s[:, 0:256] = mm(pt_ref[...], gq).astype(BF)
    val_s[:, 256:512] = mm(xt_ref[...], dk).astype(BF)
    val_s[:, 512:768] = mm(xt_ref[...], dv).astype(BF)
    split_rows(val_s, keep_ref, send_ref, order, me)


def unattend(g, sc, p, q, k, v, ga, attn, linv, xt, pt, bd, cosines, sines, feat, order):
    half, width = q.shape
    slot = k.shape[0]
    count = 2 ** len(order)
    mid = count // 2
    rows = width // count
    col = lambda r: pl.BlockSpec((r, 256), lambda i, s: (0, g))
    return call(
        functools.partial(unattend_body, order),
        (1,),
        [
            pl.BlockSpec((4, half, slot), lambda i, s: (g, 0, 0)),
            col(half),
            col(slot),
            col(slot),
            col(half),
            col(half),
            col(half),
            full((width, slot)),
            full((width, half)),
            pl.BlockSpec((1, 256, 256), lambda i, s: (g, 0, 0)),
            full((half, 128)),
            full((half, 128)),
            full((slot, 128)),
        ],
        [
            full((slot, 256)),
            full((slot, 256)),
            full((half, 256)),
            full((256, 256)),
            full((mid, rows, 768)),
            full((mid, rows, 768)),
        ],
        [
            sds((slot, 256), BF),
            sds((slot, 256), BF),
            sds((half, 256), BF),
            sds((256, 256), F32),
            sds((mid, rows, 768), BF),
            sds((mid, rows, 768), BF),
        ],
        [
            pltpu.VMEM((half, 256), BF),
            pltpu.VMEM((half, 256), F32),
            pltpu.VMEM((256, half), BF),
            pltpu.VMEM((256, half), BF),
            pltpu.VMEM((half, 256), F32),
            pltpu.VMEM((half, 256), BF),
            pltpu.VMEM((half, slot), BF),
            pltpu.VMEM((256, slot), BF),
            pltpu.VMEM((256, slot), BF),
            pltpu.VMEM((width, 768), BF),
        ],
        7_000_000_000,
        12_000_000,
    )(sc, p, q, k, v, ga, attn, linv, xt, pt, bd, cosines, sines, feat)


def tokens_body(count, groups, sc, gone_ref, wq_ref, wk_ref, wv_ref, *refs):
    gqs = refs[:groups]
    dks = refs[groups : 2 * groups]
    dvs = refs[2 * groups : 3 * groups]
    outs = refs[3 * groups : 3 * groups + count]
    (rows_s,) = refs[3 * groups + count :]
    me = sc[0]
    slot = dks[0].shape[0]
    spread = pool_matrix(128).astype(F32).T.astype(BF)
    for t in range(slot // 256):
        small = slice(128 * t, 128 * (t + 1))
        rows = slice(256 * t, 256 * (t + 1))
        gq = jnp.concatenate([r[small, :] for r in gqs], 1)
        pooled = gone_ref[small, :] + mm_nt(gq, wq_ref[...])
        high = pooled.astype(BF)
        tail = (pooled - high.astype(F32)).astype(BF)
        acc = mm(spread, high) + mm(spread, tail)
        acc = acc + mm_nt(jnp.concatenate([r[rows, :] for r in dks], 1), wk_ref[...])
        acc = acc + mm_nt(jnp.concatenate([r[rows, :] for r in dvs], 1), wv_ref[...])
        rows_s[rows, :] = acc.astype(BF)
    block = slot // count
    for k in range(count):
        start = pl.multiple_of((me ^ k) * block, block)
        outs[k][...] = rows_s[pl.ds(start, block), :]


def tokens(sc, gone, wq, wk, wv, gqs, dks, dvs, count):
    half, width = gone.shape
    slot = 2 * half
    block = slot // count
    groups = len(gqs)
    return call(
        functools.partial(tokens_body, count, groups),
        (1,),
        [full((half, width))]
        + [full((width, width))] * 3
        + [full((half, 256))] * groups
        + [full((slot, 256))] * (2 * groups),
        [full((block, width))] * count,
        [sds((block, width), BF)] * count,
        [pltpu.VMEM((slot, width), BF)],
        3_300_000_000,
        12_000_000,
    )(sc, gone, wq, wk, wv, *gqs, *dks, *dvs)


def add_up(parts):
    total = parts[0].astype(F32)
    for part in parts[1:]:
        total = total + part.astype(F32)
    return total


def reduce_rows(keep, send, order, seq_size, grp_size):
    parts = [keep, swap(send, "seq", seq_size, order[0])]
    for mask in order[1:]:
        mid = parts[0].shape[0] // 2
        out = add_up([p[mid:] for p in parts]).astype(BF)
        parts = [p[:mid] for p in parts] + [swap(out, "seq", seq_size, mask)]
    total = add_up(parts)[0]
    rank = lax.axis_index("grp")
    rows = total.shape[0] // grp_size
    mask = 1
    while mask < grp_size:
        pairs = total.reshape(-1, 2, rows, total.shape[-1])
        bit = (rank // mask) % 2
        out = lax.dynamic_index_in_dim(pairs, 1 - bit, 1, False).astype(BF)
        held = lax.dynamic_index_in_dim(pairs, bit, 1, False)
        total = held + swap(out, "grp", grp_size, mask).astype(F32)
        mask *= 2
    return total.reshape(rows, -1)


def sum_everywhere(value, seq_size, grp_size):
    for axis, size in (("seq", seq_size), ("grp", grp_size)):
        mask = 1
        while mask < size:
            value = value + swap(value, axis, size, mask)
            mask *= 2
    return value


def local(
    seq_size, grp_size, hidden, lengths, query_weight, key_weight, value_weight, w_rel,
    output_weight, gain_attn, inner_weight, outer_weight, gain_ffn, cotangent,
):
    micro, unused, seqs, part, width = hidden.shape
    count = micro * seqs
    assert count == seq_size
    slot = part * seq_size
    half = slot // 2
    me = lax.axis_index("seq")
    heads, head_dim, unused_dim = w_rel.shape
    groups = width // 256
    limit = lax.dynamic_index_in_dim(lengths.reshape(count), me, 0, False)
    sc = jnp.stack([me.astype(I32), limit])

    x = to_sequence(hidden.reshape(count, part, width)).reshape(slot, width)
    cot_blocks = cotangent.reshape(count, part // 2, width)
    cots = []
    for k in range(count):
        piece = lax.dynamic_index_in_dim(cot_blocks, me ^ k, 0, False)
        cots.append(piece if k == 0 else swap(piece, "seq", seq_size, k))

    freq = head_dim // 2
    rates = jnp.exp(-jnp.arange(freq, dtype=F32) * (math.log(10000.0) / freq))
    turn = 2.0 * jnp.arange(half, dtype=F32)[:, None] * rates[None, :]
    cosines = jnp.tile(jnp.cos(turn), (1, 4))
    sines = jnp.tile(jnp.sin(turn), (1, 4))
    angles = jnp.arange(slot, dtype=F32)[:, None] * rates[None, :]
    feat = jnp.tile(jnp.concatenate([jnp.sin(angles), jnp.cos(angles)], 1), (1, 2)).astype(BF)
    eye = jnp.eye(4, dtype=BF)
    bd = (
        w_rel.reshape(groups, 4, head_dim, 1, head_dim) * eye[None, :, None, :, None]
    ).reshape(groups, 256, 256)

    attn, linv, p, q, k, v, pooled, xt, pt = attend(
        sc, x, query_weight, key_weight, value_weight, bd, cosines, sines, feat
    )
    g1 = gain_attn.astype(F32).reshape(1, width)
    g2 = gain_ffn.astype(F32).reshape(1, width)
    fed = feed(sc, attn, pooled, output_weight, inner_weight, outer_weight, g1, g2, cots)
    outs = fed[:count]
    act, slope, gouter, gtwo, unit, rstd, mixed, dgain_ffn = fed[count:]
    first, second = (1, 2, 4), (1, 4, 2)
    okeep, osend = wouter(sc, act, gouter, first)
    pooled_parts = [outs[0]] + [swap(outs[k], "seq", seq_size, k) for k in range(1, count)]
    ga, gone, dgain_attn, ikeep, isend, bkeep, bsend = back(
        sc, gouter, slope, outer_weight, inner_weight, mixed, gtwo, unit, rstd, g1,
        output_weight, attn, second,
    )
    d_outer = reduce_rows(okeep, osend, first, seq_size, grp_size)
    d_inner = reduce_rows(ikeep, isend, second, seq_size, grp_size)
    d_out = reduce_rows(bkeep, bsend, second, seq_size, grp_size)

    gqs, dks, dvs, rels, d_group = [], [], [], [], []
    for g in range(groups):
        order = first if g % 2 == 0 else second
        dk, dv, gq, rel, keep, send = unattend(
            g, sc, p, q, k, v, ga, attn, linv, xt, pt, bd, cosines, sines, feat, order
        )
        gqs.append(gq)
        dks.append(dk)
        dvs.append(dv)
        diagonal = jnp.stack(
            [rel[64 * a : 64 * (a + 1), 64 * a : 64 * (a + 1)] for a in range(4)]
        )
        rels.append(diagonal)
        d_group.append(reduce_rows(keep, send, order, seq_size, grp_size))
    grads = tokens(sc, gone, query_weight, key_weight, value_weight, gqs, dks, dvs, count)
    token_parts = [grads[0]] + [swap(grads[k], "seq", seq_size, k) for k in range(1, count)]

    rel_sums = [sum_everywhere(r, seq_size, grp_size) for r in rels]
    gains = sum_everywhere(
        jnp.concatenate([dgain_attn, dgain_ffn], 1), seq_size, grp_size
    )
    pooled_out = assemble(sc, pooled_parts).reshape(micro, 1, seqs, part // 2, width)
    grad_hidden = assemble(sc, token_parts).reshape(hidden.shape)
    d_query = jnp.concatenate([d[:, 0:256] for d in d_group], 1)
    d_key = jnp.concatenate([d[:, 256:512] for d in d_group], 1)
    d_value = jnp.concatenate([d[:, 512:768] for d in d_group], 1)
    return (
        pooled_out,
        grad_hidden,
        d_query,
        d_key,
        d_value,
        jnp.concatenate(rel_sums, 0),
        d_out,
        gains[0, :width],
        d_inner,
        d_outer,
        gains[0, width:],
    )


def solution(mesh):
    rows = P(None, "grp", None, "seq", None)
    spread = P(("seq", "grp"), None)
    sizes = dict(mesh.shape)
    return jax.shard_map(
        functools.partial(local, sizes["seq"], sizes["grp"]),
        mesh=mesh,
        in_specs=(rows, P(None, "grp", None)) + (P(),) * 9 + (rows,),
        out_specs=(
            rows, rows, spread, spread, spread, P(), spread, P(), spread, spread, P()
        ),
        check_vma=False,
    )
```

```python
import functools
import math
import types

import jax
import jax.numpy as jnp
from jax import lax
from jax.experimental import pallas as pl
from jax.experimental.pallas import tpu as pltpu
from jax.sharding import PartitionSpec as P

BF = jnp.bfloat16
F32 = jnp.float32
I32 = jnp.int32
MESH = pl.DeviceIdType.MESH
VMEM_LIMIT = 58 << 20
EPS = 1e-05
FFC = 512
QT = 256


def sds(shape, dtype):
    return jax.ShapeDtypeStruct(shape, dtype)


def mm(a, b):
    return lax.dot_general(a, b, (((1,), (0,)), ((), ())), preferred_element_type=F32)


def mm_nt(a, b):
    return lax.dot_general(a, b, (((1,), (1,)), ((), ())), preferred_element_type=F32)


def mm_tn(a, b):
    return lax.dot_general(a, b, (((0,), (0,)), ((), ())), preferred_element_type=F32)


def full(shape):
    zeros = (0,) * len(shape)
    return pl.BlockSpec(shape, lambda *unused: zeros)


def call(body, grid, in_specs, out_specs, out_shape, scratch, flops, moved, scalars=1):
    return pl.pallas_call(
        body,
        grid_spec=pltpu.PrefetchScalarGridSpec(
            num_scalar_prefetch=scalars,
            grid=grid,
            in_specs=in_specs,
            out_specs=out_specs,
            scratch_shapes=scratch,
        ),
        out_shape=out_shape,
        compiler_params=pltpu.CompilerParams(
            dimension_semantics=("arbitrary",) * len(grid), vmem_limit_bytes=VMEM_LIMIT
        ),
        cost_estimate=pl.CostEstimate(flops=flops, bytes_accessed=moved, transcendentals=0),
    )


def rel_of(pos, order):
    bits = len(order)
    rel = 0
    for i, mask in enumerate(order):
        if (pos >> (bits - 1 - i)) & 1:
            rel |= mask
    return rel


def split_rows(val_ref, keep_ref, send_ref, order, me, cols=None):
    count = 2 ** len(order)
    step = val_ref.shape[0] // count
    for pos in range(count):
        start = pl.multiple_of((me ^ rel_of(pos, order)) * step, step)
        rows = val_ref[pl.ds(start, step), :]
        ref = keep_ref if pos < count // 2 else send_ref
        if cols is None:
            ref[pos % (count // 2)] = rows
        else:
            ref[pos % (count // 2), :, cols] = rows


def gather_body(count, src, dst, send_sem, recv_sem, local_sem):
    me = lax.axis_index("seq")
    barrier = pltpu.get_barrier_semaphore()
    for k in range(1, count):
        pl.semaphore_signal(
            barrier, inc=1, device_id={"seq": lax.rem(me + k, count)}, device_id_type=MESH
        )
    pl.semaphore_wait(barrier, count - 1)
    own = pltpu.make_async_copy(src.at[me], dst.at[me], local_sem)
    own.start()
    copies = []
    for k in range(1, count):
        peer = lax.rem(me + k, count)
        copy = pltpu.make_async_remote_copy(
            src_ref=src.at[peer],
            dst_ref=dst.at[me],
            send_sem=send_sem.at[k],
            recv_sem=recv_sem.at[k],
            device_id={"seq": peer},
            device_id_type=MESH,
        )
        copy.start()
        copies.append(copy)
    own.wait()
    for copy in copies:
        copy.wait()


def to_sequence(blocks):
    count = blocks.shape[0]
    return pl.pallas_call(
        functools.partial(gather_body, count),
        out_shape=sds(blocks.shape, blocks.dtype),
        in_specs=[pl.BlockSpec(memory_space=pl.ANY)],
        out_specs=pl.BlockSpec(memory_space=pl.ANY),
        scratch_shapes=[
            pltpu.SemaphoreType.DMA((count,)),
            pltpu.SemaphoreType.DMA((count,)),
            pltpu.SemaphoreType.DMA,
        ],
        compiler_params=pltpu.CompilerParams(
            collective_id=0, has_side_effects=True, vmem_limit_bytes=VMEM_LIMIT
        ),
    )(blocks)


def swap(value, axis, size, mask):
    return lax.ppermute(value, axis, [(i, i ^ mask) for i in range(size)])


def assemble_body(count, sc, *refs):
    out = refs[count]
    me = sc[0]
    for k in range(count):
        out[me ^ k] = refs[k][...]


def assemble(sc, pieces):
    count = len(pieces)
    shape = (count,) + pieces[0].shape
    size = math.prod(shape) * 4
    return call(
        functools.partial(assemble_body, count),
        (1,),
        [full(p.shape) for p in pieces],
        full(shape),
        sds(shape, pieces[0].dtype),
        [],
        0,
        size,
    )(sc, *pieces)


def pool_matrix(rows):
    row = lax.broadcasted_iota(I32, (rows, 2 * rows), 0)
    col = lax.broadcasted_iota(I32, (rows, 2 * rows), 1)
    return jnp.where((col == 2 * row) | (col == 2 * row + 1), 0.5, 0.0).astype(BF)


def attend_body(
    heads, sc, x_ref, wq_ref, wk_ref, wv_ref, bd_ref, cos_ref, sin_ref, feat_ref,
    attn_ref, linv_ref, p_ref, q_ref, k_ref, v_ref, pooled_ref, xt_ref, pt_ref, sh_s,
):
    slot = x_ref.shape[0]
    half = slot // 2
    scale = 0.125 * 1.4426950408889634

    @pl.when(pl.program_id(0) == 0)
    def first():
        pool = pool_matrix(128)
        for t in range(slot // 256):
            tile = x_ref[256 * t : 256 * (t + 1), :]
            rows = mm(pool, tile)
            pooled_ref[128 * t : 128 * (t + 1), :] = rows
            xt_ref[:, 256 * t : 256 * (t + 1)] = tile.T
            pt_ref[:, 128 * t : 128 * (t + 1)] = rows.astype(BF).T

    q = mm(pooled_ref[...].astype(BF), wq_ref[...]).astype(BF)
    q_ref[...] = q
    k_ref[...] = mm(x_ref[...], wk_ref[...]).astype(BF)
    v_ref[...] = mm(x_ref[...], wv_ref[...]).astype(BF)
    rel = mm(q, bd_ref[0])
    lane = lax.broadcasted_iota(I32, (1, 128), 1)
    low = (lane % 64) < 32
    for pair in range(2):
        part = rel[:, 128 * pair : 128 * (pair + 1)]
        other = jnp.where(low, pltpu.roll(part, 96, 1), -pltpu.roll(part, 32, 1))
        sh_s[:, 128 * pair : 128 * (pair + 1)] = (
            part * cos_ref[...] + other * sin_ref[...]
        ).astype(BF)
    key_ok = lax.broadcasted_iota(I32, (1, slot), 1) < sc[1]
    ones = jnp.ones((slot, 128), BF)

    def one_pair(pair, carry):
        cols = pl.ds(pl.multiple_of(pair * 128, 128), 128)
        key_side = jnp.concatenate([k_ref[:, cols], feat_ref[...]], 1)
        value_side = jnp.concatenate([v_ref[:, cols], ones], 1)
        for t in range(half // QT):
            rows = slice(QT * t, QT * (t + 1))
            q_part = q_ref[rows, cols]
            s_part = sh_s[rows, cols]
            outs = []
            for h in range(2):
                mine = (lane < 64) if h == 0 else (lane >= 64)
                zero = jnp.zeros_like(q_part)
                left = jnp.concatenate(
                    [jnp.where(mine, q_part, zero), jnp.where(mine, s_part, zero)], 1
                )
                s = jnp.where(key_ok, mm_nt(left, key_side), -1e30)
                top = jnp.max(s, -1, keepdims=True)
                p = jnp.exp2((s - top) * scale).astype(BF)
                p_ref[pair * 2 + h, rows, :] = p
                acc = mm(p, value_side)
                inv = 1.0 / acc[:, 128:]
                outs.append((acc[:, :128] * inv, inv))
            first_head = lane < 64
            attn_ref[rows, cols] = jnp.where(first_head, outs[0][0], outs[1][0]).astype(BF)
            linv_ref[rows, cols] = jnp.where(first_head, outs[0][1], outs[1][1])
        return carry

    lax.fori_loop(0, 2, one_pair, 0)


def attend(sc, x, wq, wk, wv, bd, cosines, sines, feat):
    slot, width = x.shape
    half = slot // 2
    groups = width // 256
    heads = width // 64
    by_group = lambda rows: pl.BlockSpec((rows, 256), lambda g, s: (0, g))
    return call(
        functools.partial(attend_body, heads),
        (groups,),
        [
            full((slot, width)),
            by_group(width),
            by_group(width),
            by_group(width),
            pl.BlockSpec((1, 256, 256), lambda g, s: (g, 0, 0)),
            full((half, 128)),
            full((half, 128)),
            full((slot, 128)),
        ],
        [
            by_group(half),
            by_group(half),
            pl.BlockSpec((4, half, slot), lambda g, s: (g, 0, 0)),
            by_group(half),
            by_group(slot),
            by_group(slot),
            full((half, width)),
            full((width, slot)),
            full((width, half)),
        ],
        [
            sds((half, width), BF),
            sds((half, width), F32),
            sds((heads, half, slot), BF),
            sds((half, width), BF),
            sds((slot, width), BF),
            sds((slot, width), BF),
            sds((half, width), F32),
            sds((width, slot), BF),
            sds((width, half), BF),
        ],
        [pltpu.VMEM((half, 256), BF)],
        12_000_000_000,
        30_000_000,
    )(sc, x, wq, wk, wv, bd, cosines, sines, feat)


def norm_parts(rows):
    centered = rows - jnp.mean(rows, -1, keepdims=True)
    rstd = lax.rsqrt(jnp.mean(centered * centered, -1, keepdims=True) + EPS)
    return centered * rstd, rstd


def norm_back(grad, unit, rstd, gain):
    scaled = grad * gain
    return rstd * (
        scaled
        - jnp.mean(scaled, -1, keepdims=True)
        - unit * jnp.mean(scaled * unit, -1, keepdims=True)
    )


def feed_body(
    count, sc, attn_ref, pooled_ref, wo_ref, win_ref, wout_ref, g1_ref, g2_ref, *refs
):
    cots = refs[:count]
    (rows_ref, act_ref, slope_ref, gouter_ref, gtwo_ref, unit_ref, rstd_ref, mt_ref, dgain_ref) = (
        refs[count : count + 9]
    )
    mixed_s, acc_s, cot_s = refs[count + 9 :]
    step = pl.program_id(0)
    me = sc[0]
    half = attn_ref.shape[0]
    block = half // count

    @pl.when(step == 0)
    def first():
        unit, rstd = norm_parts(pooled_ref[...] + mm(attn_ref[...], wo_ref[...]))
        mixed = unit * g1_ref[...]
        unit_ref[...] = unit
        rstd_ref[...] = jnp.broadcast_to(rstd, rstd_ref.shape)
        mixed_s[...] = mixed.astype(BF)
        mt_ref[...] = mixed.astype(BF).T
        acc_s[...] = mixed
        for k in range(count):
            start = pl.multiple_of((me ^ k) * block, block)
            cot_s[pl.ds(start, block), :] = cots[k][...]

    pre = mm(mixed_s[...], win_ref[...])
    cdf = 0.5 * (1.0 + lax.erf(pre * 0.7071067811865476))
    act = (pre * cdf).astype(BF)
    act_ref[...] = act
    slope_ref[...] = (cdf + pre * (jnp.exp(pre * pre * -0.5) * 0.3989422804014327)).astype(BF)
    acc_s[...] += mm(act, wout_ref[...])

    @pl.when(step == pl.num_programs(0) - 1)
    def last():
        unit, rstd = norm_parts(acc_s[...])
        row = lax.broadcasted_iota(I32, (half, 1), 0)
        valid = 2 * row < sc[1]
        rows_ref[...] = jnp.where(valid, unit * g2_ref[...], 0.0).astype(BF)
        grad = jnp.where(valid, cot_s[...].astype(F32), 0.0)
        dgain_ref[...] = jnp.sum(grad * unit, 0, keepdims=True)
        two = norm_back(grad, unit, rstd, g2_ref[...])
        gtwo_ref[...] = two
        gouter_ref[...] = two.astype(BF)


def feed(sc, attn, pooled, wo, win, wout, g1, g2, cots):
    half, width = attn.shape
    inner = win.shape[1]
    count = len(cots)
    block = half // count
    return call(
        functools.partial(feed_body, count),
        (inner // FFC,),
        [
            full((half, width)),
            full((half, width)),
            full((width, width)),
            pl.BlockSpec((width, FFC), lambda j, s: (0, j)),
            pl.BlockSpec((FFC, width), lambda j, s: (j, 0)),
            full((1, width)),
            full((1, width)),
        ]
        + [full((block, width))] * count,
        [
            full((half, width)),
            pl.BlockSpec((half, FFC), lambda j, s: (0, j)),
            pl.BlockSpec((half, FFC), lambda j, s: (0, j)),
            full((half, width)),
            full((half, width)),
            full((half, width)),
            full((half, 128)),
            full((width, half)),
            full((1, width)),
        ],
        [
            sds((half, width), BF),
            sds((half, inner), BF),
            sds((half, inner), BF),
            sds((half, width), BF),
            sds((half, width), F32),
            sds((half, width), F32),
            sds((half, 128), F32),
            sds((width, half), BF),
            sds((1, width), F32),
        ],
        [
            pltpu.VMEM((half, width), BF),
            pltpu.VMEM((half, width), F32),
            pltpu.VMEM((half, width), BF),
        ],
        5_500_000_000,
        24_000_000,
    )(sc, attn, pooled, wo, win, wout, g1, g2, *cots)


def wouter_body(count, sc, act_ref, gouter_ref, keep_ref, send_ref):
    val = mm_tn(act_ref[...], gouter_ref[...]).astype(BF)
    pos = pl.program_id(0)

    @pl.when(pos < count // 2)
    def near():
        keep_ref[0] = val

    @pl.when(pos >= count // 2)
    def far():
        send_ref[0] = val


def wouter(sc, act, gouter, order):
    half, inner = act.shape
    width = gouter.shape[1]
    count = 2 ** len(order)
    rows = inner // count
    mid = count // 2

    def column(pos, s):
        rel = 0
        for i, mask in enumerate(order):
            rel = rel + ((pos >> (len(order) - 1 - i)) & 1) * mask
        return (0, s[0] ^ rel)

    return call(
        functools.partial(wouter_body, count),
        (count,),
        [pl.BlockSpec((half, rows), column), full((half, width))],
        [
            pl.BlockSpec((1, rows, width), lambda p, s: (jnp.minimum(p, mid - 1), 0, 0)),
            pl.BlockSpec((1, rows, width), lambda p, s: (jnp.maximum(p - mid, 0), 0, 0)),
        ],
        [sds((mid, rows, width), BF)] * 2,
        [],
        2_500_000_000,
        9_000_000,
    )(sc, act, gouter)


def loop(count, body):
    def step(i, carry):
        body(i)
        return carry

    lax.fori_loop(0, count, step, 0)


def masks_of(size):
    return [1 << i for i in range(size.bit_length() - 1)]


def moved(rank, rel, size):
    total = 0
    for mask in masks_of(size):
        bit = lax.rem(lax.div(rank, mask), 2)
        total = total + mask * ((1 - bit) if rel & mask else bit)
    return total


def wide(value):
    return value.astype(F32)


class Chunk:
    def __init__(self, env, index, order, early, keep, send, recv, zbuf, recvz, out):
        self.env, self.index, self.order, self.early = env, index, order, early
        self.keep, self.send, self.recv = keep, send, recv
        self.zbuf, self.recvz, self.out = zbuf, recvz, out

    def remote(self, slot, src, dst, device):
        return pltpu.make_async_remote_copy(
            src_ref=src,
            dst_ref=dst,
            send_sem=self.env.ssem.at[self.index, slot],
            recv_sem=self.env.rsem.at[self.index, slot],
            device_id=device,
            device_id_type=MESH,
        )

    def seq_copy(self, stage):
        device = {"seq": moved(self.env.me, self.order[stage], self.env.seq)}
        if stage == 0:
            src = self.send
        else:
            half = 4 >> stage
            src = (self.zbuf if self.early else self.recv[0]).at[pl.ds(half, half)]
        return self.remote(stage, src, self.recv[stage], device)

    def z_copies(self):
        grp, z = self.env.grp, self.env.z
        copies = []
        for d in range(1, grp):
            peer = lax.rem(z + d, grp)
            src = self.recv[0].at[:, peer] if self.early else self.zbuf.at[peer]
            copies.append(self.remote(2 + d, src, self.recvz.at[d - 1], {"grp": peer}))
        return copies

    def step(self, n):
        keep, (recv0, recv1, recv2) = self.keep, self.recv
        zbuf, recvz, grp, z = self.zbuf, self.recvz, self.env.grp, self.env.z
        if n == 0:
            self.seq_copy(0).start()
        elif n == 1 and self.early:
            self.seq_copy(0).wait()

            def add(i):
                p, g = lax.div(i, grp), lax.rem(i, grp)
                recv0[p, g] = (wide(keep[p, g]) + wide(recv0[p, g])).astype(BF)

            loop(4 * grp, add)
            for copy in self.z_copies():
                copy.start()
        elif n == 2 and self.early:
            for copy in self.z_copies():
                copy.wait()

            def add(p):
                total = wide(recv0[p, z])
                for d in range(grp - 1):
                    total = total + wide(recvz[d, p])
                zbuf[p] = total.astype(BF)

            loop(4, add)
            self.seq_copy(1).start()
        elif n == 3 and self.early:
            self.seq_copy(1).wait()
            zbuf[1] = (wide(zbuf[1]) + wide(recv1[1])).astype(BF)
            self.seq_copy(2).start()
        elif n == 4 and self.early:
            self.seq_copy(2).wait()
            self.out(wide(zbuf[0]) + wide(recv1[0]) + wide(recv2[0]))
        elif n == 1:
            self.seq_copy(0).wait()
            parts = keep.shape[1] // 48

            def add(i):
                p, rows = 2 + lax.div(i, parts), pl.ds(pl.multiple_of(48 * lax.rem(i, parts), 48), 48)
                recv0[p, rows] = (wide(keep[p, rows]) + wide(recv0[p, rows])).astype(BF)

            loop(2 * parts, add)
            self.seq_copy(1).start()
        elif n == 2:
            self.seq_copy(1).wait()

            def add(i):
                rows = pl.ds(pl.multiple_of(48 * i, 48), 48)
                recv0[1, rows] = (
                    wide(keep[1, rows]) + wide(recv0[1, rows]) + wide(recv1[1, rows])
                ).astype(BF)

            loop(keep.shape[1] // 48, add)
            self.seq_copy(2).start()
        elif n == 3:
            self.seq_copy(2).wait()
            share = keep.shape[1] // grp
            for start in range(0, keep.shape[1], 48):
                rows = slice(start, start + 48)
                total = (
                    wide(keep[0, rows]) + wide(recv0[0, rows])
                    + wide(recv1[0, rows]) + wide(recv2[0, rows])
                )
                size = min(share, 48)
                for low in range(start, start + 48, size):
                    g, inside = low // share, low % share
                    zbuf[g, inside : inside + size] = total[low - start : low - start + size].astype(BF)
            for copy in self.z_copies():
                copy.start()
        else:
            for copy in self.z_copies():
                copy.wait()
            total = wide(zbuf[z])
            for d in range(grp - 1):
                total = total + wide(recvz[d])
            self.out(total)


BACK_INPUTS = list(
    dict(
        gouter=0, slope=0, wout=0, win=0, mixed=0, gtwo=0, unit=0, rstd=0, g1=0, wo=0, attn=0,
        p=0, q=0, k=0, v=0, linv=0, xt=0, pt=0, bd=0, cos=0, sin=0, feat=0, wq=0, wk=0, wv=0,
        okeep=0, osend=0, okeep3=0, osend3=0, rows=0, dgain2=0,
    )
)
BACK_OUTPUTS = list(
    dict(hidden=0, pooled=0, inner=0, outer=0, out=0, query=0, key=0, value=0, small=0)
)
POINTS = {
    ("B", 1): [("O1", 1), ("O2", 1), ("O0", 1), ("I0", 0)],
    ("B", 2): [("I0", 1)],
    ("B", 3): [("I1", 0)],
    ("B", 4): [("I1", 1)],
    ("B", 5): [("I2", 0)],
    ("L", 0): [("I2", 1), ("W", 0)],
    ("U", 0): [("W", 1)],
    ("U", 1): [("G0", 0), ("O0", 2), ("I0", 2)],
    ("U", 2): [("G0", 1), ("O0", 3), ("O1", 2)],
    ("U", 3): [("G1", 0), ("I1", 2), ("I0", 3), ("O2", 2)],
    ("U", 4): [("G1", 1), ("I2", 2)],
    ("U", 5): [("G2", 0), ("O0", 4), ("S", 0)],
    ("T", 0): [("H", 0), ("G2", 1), ("S", 1)],
    ("E", 0): [
        ("I1", 3), ("W", 2), ("O1", 3), ("S", 2), ("I2", 3), ("O2", 3), ("I0", 4), ("S", 3),
        ("G0", 2), ("W", 3), ("I1", 4), ("O1", 4), ("S", 4), ("G1", 2), ("O2", 4), ("I2", 4),
        ("S", 5), ("G0", 3), ("W", 4), ("G2", 2), ("G1", 3), ("G0", 4), ("G2", 3), ("G1", 4),
        ("G2", 4), ("H", 1),
    ],
}


def back_body(names, sizes, *refs):
    every = dict(zip(BACK_INPUTS + BACK_OUTPUTS + names, refs))
    ref = types.SimpleNamespace(**every)
    seq, grp = sizes
    me = lax.axis_index("seq")
    z = lax.axis_index("grp")
    env = types.SimpleNamespace(me=me, z=z, seq=seq, grp=grp, ssem=ref.ssem, rsem=ref.rsem)
    half, width = ref.vgo.shape
    slot = 2 * half
    inner = ref.slope.shape[1]
    steps = inner // FFC
    pairs = width // 128
    groups = width // 256
    lsem = ref.lsem

    plain = [
        (ref.gouter, ref.vgo), (ref.mixed, ref.vmt), (ref.gtwo, ref.vacc),
        (ref.unit, ref.vun), (ref.rstd, ref.vrs), (ref.wo, ref.vwo), (ref.attn, ref.vat),
        (ref.linv, ref.vlinv),
        (ref.q, ref.vq), (ref.k, ref.vk), (ref.v, ref.vv), (ref.feat, ref.vfeat),
        (ref.cos, ref.vcos), (ref.sin, ref.vsin), (ref.bd, ref.vbd), (ref.xt, ref.vxt),
        (ref.wq, ref.vwq), (ref.wk, ref.vwk), (ref.wv, ref.vwv), (ref.pt, ref.vmt),
    ]
    local = [pltpu.make_async_copy(*pair, lsem.at[i]) for i, pair in enumerate(plain)]
    base = len(plain)

    def weights(j, buf):
        cols = pl.ds(pl.multiple_of(j * FFC, FFC), FFC)
        return [
            pltpu.make_async_copy(ref.slope.at[:, cols], ref.vslope.at[buf], ref.wsem.at[0, buf]),
            pltpu.make_async_copy(ref.wout.at[cols, :], ref.vwout.at[buf], ref.wsem.at[1, buf]),
            pltpu.make_async_copy(ref.win.at[:, cols], ref.vwin.at[buf], ref.wsem.at[2, buf]),
        ]

    def probs(i, buf):
        return pltpu.make_async_copy(
            ref.p.at[pl.ds(2 * i, 2)], ref.vp.at[buf], ref.wsem.at[3, buf]
        )

    chunks = {}
    orders = {
        "O0": (1, 2, 4), "O1": (1, 2, 4), "O2": (1, 2, 4), "I0": (1, 4, 2), "I1": (1, 2, 4),
        "I2": (1, 4, 2), "W": (1, 4, 2), "G0": (1, 2, 4), "G1": (1, 4, 2), "G2": (1, 2, 4),
    }

    def out_cols(name, start, stop):
        def put(value):
            every[name][:, start:stop] = value

        return put

    def out_three(g):
        def put(value):
            for i, name in enumerate(("query", "key", "value")):
                every[name][:, 256 * g : 256 * (g + 1)] = value[:, 256 * i : 256 * (i + 1)]

        return put

    kept = []
    for index, (name, order) in enumerate(orders.items()):
        early = name in ("O1", "O2")
        kind = name[0]
        n = int(name[1]) if len(name) > 1 else 0
        recv = [every[name + "r0"], every[name + "r1"], every[name + "r2"]]
        if kind == "O":
            cols = pl.ds(256 * n, 256)
            keep_hbm = ref.okeep.at[:, :, :, cols] if early else ref.okeep3.at[:, :, cols]
            send = ref.osend.at[:, :, :, cols] if early else ref.osend3.at[:, :, cols]
            keep = every[name + "k"]
            kept.append(pltpu.make_async_copy(keep_hbm, keep, lsem.at[base + n]))
            out = out_cols("outer", 256 * n, 256 * (n + 1))
        elif kind == "I":
            keep, send = ref.ikeep.at[n], ref.isend.at[n]
            out = out_cols("inner", 1024 * n, 1024 * (n + 1))
        elif kind == "W":
            keep, send = ref.wkeep, ref.wsend
            out = out_cols("out", 0, width)
        else:
            keep, send = ref.gkeep.at[n], ref.gsend.at[n]
            out = out_three(n)
        chunks[name] = Chunk(
            env, index, order, early, keep, send, recv, every[name + "z"], every[name + "rz"], out
        )

    def spread(src, dst, sem):
        size = dst.shape[1]
        block = lambda b: src.at[pl.ds(pl.multiple_of(b * size, size), size)]
        copies = [pltpu.make_async_copy(block(me), dst.at[me], ref.dsem.at[sem])]
        for k in range(1, seq):
            peer = lax.rem(me + k, seq)
            copies.append(
                pltpu.make_async_remote_copy(
                    src_ref=block(peer),
                    dst_ref=dst.at[me],
                    send_sem=ref.asend.at[sem, k],
                    recv_sem=ref.arecv.at[sem, k],
                    device_id={"seq": peer},
                    device_id_type=MESH,
                )
            )
        return copies

    doubling = [("seq", m) for m in masks_of(seq)] + [("grp", m) for m in masks_of(grp)]

    def small_copy(n):
        axis, mask = doubling[n]
        rank, size = (me, seq) if axis == "seq" else (z, grp)
        return pltpu.make_async_remote_copy(
            src_ref=ref.small,
            dst_ref=ref.vsmall.at[n],
            send_sem=ref.msend.at[n],
            recv_sem=ref.mrecv.at[n],
            device_id={axis: moved(rank, mask, size)},
            device_id_type=MESH,
        )

    def small_step(n):
        if 0 < n <= len(doubling):
            small_copy(n - 1).wait()
            ref.small[...] += ref.vsmall[n - 1]
        if n < len(doubling):
            small_copy(n).start()

    def event(name, n):
        if name == "H":
            for copy in spread(ref.vk, ref.hidden, 1):
                copy.start() if n == 0 else copy.wait()
        elif name == "S":
            small_step(n)
            if n == 5:
                for more in range(6, len(doubling) + 1):
                    small_step(more)
        else:
            chunks[name].step(n)

    def point(kind, index, dynamic=None):
        todo = POINTS.get((kind, index), [])
        if not todo:
            return
        if dynamic is None:
            for name, n in todo:
                event(name, n)
        else:

            @pl.when(dynamic == index)
            def run():
                for name, n in todo:
                    event(name, n)

    barrier = pltpu.get_barrier_semaphore()
    for k in range(1, seq):
        pl.semaphore_signal(
            barrier, inc=1, device_id={"seq": lax.rem(me + k, seq)}, device_id_type=MESH
        )
    for k in range(1, grp):
        pl.semaphore_signal(
            barrier, inc=1, device_id={"grp": lax.rem(z + k, grp)}, device_id_type=MESH
        )
    for copy in local[:3]:
        copy.start()
    for copy in weights(0, 0):
        copy.start()
    pl.semaphore_wait(barrier, seq + grp - 2)
    for name in ("O0", "O1", "O2"):
        chunks[name].step(0)
    for copy in spread(ref.rows, ref.pooled, 0):
        copy.start()
    for copy in kept:
        copy.start()
    for copy in local[:3]:
        copy.wait()

    def rows_of(count, rel):
        step = width // seq
        return pl.ds(pl.multiple_of(moved(me, rel, seq) * step, step), step)

    def split(order, cols, keep, send):
        for pos in range(seq):
            block = ref.vval[rows_of(width, rel_of(pos, order)), cols]
            (keep if pos < seq // 2 else send)(pos % (seq // 2), block)

    def feed_step(j):
        buf = lax.rem(j, 2)
        for copy in weights(j, buf):
            copy.wait()

        @pl.when(j + 1 < steps)
        def more():
            for copy in weights(j + 1, 1 - buf):
                copy.start()

        @pl.when(j == 1)
        def rest():
            for copy in local[3:-1]:
                copy.start()
            probs(0, 0).start()
            for copy in kept:
                copy.wait()

        grad = mm_nt(ref.vgo[...], ref.vwout[buf])
        hid = (wide(ref.vslope[buf]) * grad).astype(BF)
        ref.vacc[...] += mm_nt(hid, ref.vwin[buf])
        ref.vval[:, :FFC] = mm(ref.vmt[...], hid).astype(BF)
        c = lax.div(j, 2)
        cols = pl.ds(pl.multiple_of(lax.rem(j, 2) * FFC, FFC), FFC)

        for parity, order in ((0, orders["I0"]), (1, orders["I1"])):

            @pl.when(lax.rem(c, 2) == parity)
            def place():
                def keep(pos, block):
                    ref.ikeep[c, pos, :, cols] = block

                def send(pos, block):
                    ref.isend[c, pos, :, cols] = block

                split(order, slice(0, FFC), keep, send)

        for t in range(steps):
            point("B", t, j)

    loop(steps, feed_step)

    local[-1].start()
    for copy in local[3:8]:
        copy.wait()
    grad = ref.vacc[...]
    unit = ref.vun[...]
    small = ref.small
    dgain = jnp.sum(grad * unit, 0, keepdims=True)
    for i in range(pairs):
        small[64 * pairs + i, :] = dgain[0, 128 * i : 128 * (i + 1)]
        small[64 * pairs + pairs + i, :] = ref.dgain2[0, 128 * i : 128 * (i + 1)]
    for i in range(64 * pairs + 2 * pairs, small.shape[0]):
        small[i, :] = jnp.zeros((128,), F32)
    one = norm_back(grad, unit, ref.vrs[:, :1], ref.g1[...])
    ref.vun[...] = one
    branch = one.astype(BF)
    attn = ref.vat[...]
    ref.vval[...] = mm_tn(attn, branch).astype(BF)

    def keep_w(pos, block):
        ref.wkeep[pos] = block

    def send_w(pos, block):
        ref.wsend[pos] = block

    split(orders["W"], slice(0, width), keep_w, send_w)
    scaled = mm_nt(branch, ref.vwo[...]) * ref.vlinv[...]
    ref.vgo[...] = scaled.astype(BF)
    ref.vacc[...] = scaled * wide(attn)
    for copy in local[8:]:
        copy.wait()
    point("L", 0)

    lane = lax.broadcasted_iota(I32, (1, 128), 1)
    low = lax.rem(lane, 64) < 32
    first_head = lane < 64
    ones = jnp.broadcast_to(jnp.where(lane < 2, 1.0, 0.0).astype(BF), (slot, 128))

    def attention_step(i):
        buf = lax.rem(i, 2)
        g = lax.div(i, 2)
        probs(i, buf).wait()

        @pl.when(i + 1 < pairs)
        def more():
            probs(i + 1, 1 - buf).start()

        cols = pl.ds(pl.multiple_of(i * 128, 128), 128)
        part = pl.ds(pl.multiple_of(buf * 128, 128), 128)
        ref.vqt[...] = ref.vq[:, cols].T
        ref.vgt[...] = ref.vgo[:, cols].T
        key_side = jnp.concatenate([ref.vk[:, cols], ref.vfeat[...]], 1)
        value_side = jnp.concatenate([ref.vv[:, cols], ones], 1)
        outs = [[], []]
        for h in range(2):
            mine = first_head if h == 0 else jnp.logical_not(first_head)
            for t in range(half // QT):
                rows = slice(QT * t, QT * (t + 1))
                g_part = ref.vgo[rows, cols]
                delta = jnp.sum(jnp.where(mine, ref.vacc[rows, cols], 0.0), -1, keepdims=True)
                coarse = wide(delta.astype(BF))
                tail = jnp.where(lane == 0, coarse, jnp.where(lane == 1, delta - coarse, 0.0))
                left = jnp.concatenate(
                    [jnp.where(mine, g_part, jnp.zeros_like(g_part)), (-tail).astype(BF)], 1
                )
                ds = (wide(ref.vp[buf, h, rows, :]) * mm_nt(left, value_side)).astype(BF)
                ref.vds[rows, :] = ds
                outs[h].append(mm(ds, key_side))
            lines = slice(64 * h, 64 * (h + 1))
            ref.vkt[lines, :] = (mm(ref.vqt[lines, :], ref.vds[...]) * 0.125).astype(BF)
            ref.vvt[lines, :] = mm(ref.vgt[lines, :], ref.vp[buf, h]).astype(BF)
        for t in range(half // QT):
            rows = slice(QT * t, QT * (t + 1))
            a, b = outs[0][t], outs[1][t]
            ref.vgqf[rows, part] = jnp.where(first_head, a[:, :128], b[:, :128]) * 0.125
            shift = jnp.where(first_head, a[:, 128:], b[:, 128:]) * 0.125
            other = jnp.where(low, -pltpu.roll(shift, 96, 1), pltpu.roll(shift, 32, 1))
            ref.vrel[rows, part] = (
                shift * ref.vcos[rows, :] + other * ref.vsin[rows, :]
            ).astype(BF)
        ref.vk[:, cols] = ref.vkt[...].T
        ref.vv[:, cols] = ref.vvt[...].T
        both = mm(ref.vqt[...], ref.vrel[:, part])
        small[pl.ds(pl.multiple_of(64 * i, 64), 64), :] = jnp.where(first_head, both[:64], both[64:])

        @pl.when(buf == 1)
        def tail():
            wide_cols = pl.ds(pl.multiple_of(g * 256, 256), 256)
            gq = (ref.vgqf[...] + mm_nt(ref.vrel[...], ref.vbd[g])).astype(BF)
            ref.vq[:, wide_cols] = gq
            dk = ref.vk[:, wide_cols]
            dv = ref.vv[:, wide_cols]
            ref.vval[:, 0:256] = mm(ref.vmt[...], gq).astype(BF)
            ref.vval[:, 256:512] = mm(ref.vxt[...], dk).astype(BF)
            ref.vval[:, 512:768] = mm(ref.vxt[...], dv).astype(BF)

            def keep(pos, block):
                ref.gkeep[g, pos] = block

            def send(pos, block):
                ref.gsend[g, pos] = block

            for parity, order in ((0, orders["G0"]), (1, orders["G1"])):

                @pl.when(lax.rem(g, 2) == parity)
                def place():
                    split(order, slice(0, 768), keep, send)

        for t in range(pairs):
            point("U", t, i)

    loop(pairs, attention_step)

    spread_m = wide(pool_matrix(128)).T.astype(BF)

    def token_step(t):
        small_rows = pl.ds(pl.multiple_of(128 * t, 128), 128)
        rows = pl.ds(pl.multiple_of(256 * t, 256), 256)
        pooled = ref.vun[small_rows, :] + mm_nt(ref.vq[small_rows, :], ref.vwq[...])
        high = pooled.astype(BF)
        rest = (pooled - wide(high)).astype(BF)
        acc = mm(spread_m, high) + mm(spread_m, rest)
        acc = acc + mm_nt(ref.vk[rows, :], ref.vwk[...])
        acc = (acc + mm_nt(ref.vv[rows, :], ref.vwv[...])).astype(BF)
        ref.vk[rows, :] = acc

    loop(slot // 256, token_step)
    point("T", 0)
    point("E", 0)
    for copy in spread(ref.rows, ref.pooled, 0):
        copy.wait()


def backward(args, seq, grp):
    half, width = args["gouter"].shape
    slot = 2 * half
    inner = args["slope"].shape[1]
    part = slot // seq
    share = width // seq
    steps = seq.bit_length() - 1 + grp.bit_length() - 1
    small_rows = (64 * (width // 128) + 2 * (width // 128) + 7) // 8 * 8
    vm = pltpu.VMEM
    scratch = dict(
        vgo=vm((half, width), BF),
        vmt=vm((width, half), BF),
        vacc=vm((half, width), F32),
        vun=vm((half, width), F32),
        vrs=vm((half, 128), F32),
        vwo=vm((width, width), BF),
        vat=vm((half, width), BF),
        vslope=vm((2, half, FFC), BF),
        vwout=vm((2, FFC, width), BF),
        vwin=vm((2, width, FFC), BF),
        vval=vm((width, 768), BF),
        vp=vm((2, 2, half, slot), BF),
        vq=vm((half, width), BF),
        vk=vm((slot, width), BF),
        vv=vm((slot, width), BF),
        vlinv=vm((half, width), F32),
        vxt=vm((width, slot), BF),
        vbd=vm(args["bd"].shape, BF),
        vcos=vm((half, 128), F32),
        vsin=vm((half, 128), F32),
        vfeat=vm((slot, 128), BF),
        vqt=vm((128, half), BF),
        vgt=vm((128, half), BF),
        vgqf=vm((half, 256), F32),
        vrel=vm((half, 256), BF),
        vds=vm((half, slot), BF),
        vkt=vm((128, slot), BF),
        vvt=vm((128, slot), BF),
        vwq=vm((width, width), BF),
        vwk=vm((width, width), BF),
        vwv=vm((width, width), BF),
        vsmall=vm((steps, small_rows, 128), F32),
        ikeep=vm((3, 4, share, 1024), BF),
        isend=vm((3, 4, share, 1024), BF),
        wkeep=vm((4, share, width), BF),
        wsend=vm((4, share, width), BF),
        gkeep=vm((3, 4, share, 768), BF),
        gsend=vm((3, 4, share, 768), BF),
        lsem=pltpu.SemaphoreType.DMA((24,)),
        wsem=pltpu.SemaphoreType.DMA((4, 2)),
        dsem=pltpu.SemaphoreType.DMA((2,)),
        asend=pltpu.SemaphoreType.DMA((2, seq)),
        arecv=pltpu.SemaphoreType.DMA((2, seq)),
        msend=pltpu.SemaphoreType.DMA((steps,)),
        mrecv=pltpu.SemaphoreType.DMA((steps,)),
        ssem=pltpu.SemaphoreType.DMA((10, 2 + grp)),
        rsem=pltpu.SemaphoreType.DMA((10, 2 + grp)),
    )
    tall = inner // seq
    for name, rows, cols in (
        [(f"O{n}", tall, 256) for n in range(3)]
        + [(f"I{n}", share, 1024) for n in range(3)]
        + [("W", share, width)]
        + [(f"G{n}", share, 768) for n in range(3)]
    ):
        z_rows = rows // grp
        if name in ("O1", "O2"):
            scratch[name + "k"] = vm((4, grp, z_rows, cols), BF)
            scratch[name + "r0"] = vm((4, grp, z_rows, cols), BF)
            scratch[name + "r1"] = vm((2, z_rows, cols), BF)
            scratch[name + "r2"] = vm((1, z_rows, cols), BF)
            scratch[name + "z"] = vm((4, z_rows, cols), BF)
            scratch[name + "rz"] = vm((grp - 1, 4, z_rows, cols), BF)
        else:
            if name == "O0":
                scratch[name + "k"] = vm((4, rows, cols), BF)
            scratch[name + "r0"] = vm((4, rows, cols), BF)
            scratch[name + "r1"] = vm((2, rows, cols), BF)
            scratch[name + "r2"] = vm((1, rows, cols), BF)
            scratch[name + "z"] = vm((grp, z_rows, cols), BF)
            scratch[name + "rz"] = vm((grp - 1, z_rows, cols), BF)
    names = list(scratch)
    outs = [
        sds((seq, part, width), BF),
        sds((seq, part // 2, width), BF),
        sds((share // grp, inner), F32),
        sds((tall // grp, width), F32),
        sds((share // grp, width), F32),
        sds((share // grp, width), F32),
        sds((share // grp, width), F32),
        sds((share // grp, width), F32),
        sds((small_rows, 128), F32),
    ]
    hbm = pl.BlockSpec(memory_space=pl.ANY)
    vmem = pl.BlockSpec(memory_space=pltpu.VMEM)
    in_vmem = ("g1", "dgain2")
    return pl.pallas_call(
        functools.partial(back_body, names, (seq, grp)),
        out_shape=outs,
        in_specs=[vmem if n in in_vmem else hbm for n in BACK_INPUTS],
        out_specs=[hbm, hbm] + [vmem] * (len(outs) - 2),
        scratch_shapes=list(scratch.values()),
        compiler_params=pltpu.CompilerParams(
            collective_id=1, has_side_effects=True, vmem_limit_bytes=63 << 20
        ),
        cost_estimate=pl.CostEstimate(
            flops=30_000_000_000, bytes_accessed=60_000_000, transcendentals=0
        ),
    )(*[args[n] for n in BACK_INPUTS])


def local(
    seq_size, grp_size, hidden, lengths, query_weight, key_weight, value_weight, w_rel,
    output_weight, gain_attn, inner_weight, outer_weight, gain_ffn, cotangent,
):
    micro, unused, seqs, part, width = hidden.shape
    count = micro * seqs
    assert count == seq_size
    slot = part * seq_size
    half = slot // 2
    me = lax.axis_index("seq")
    heads, head_dim, unused_dim = w_rel.shape
    groups = width // 256
    limit = lax.dynamic_index_in_dim(lengths.reshape(count), me, 0, False)
    sc = jnp.stack([me.astype(I32), limit])

    x = to_sequence(hidden.reshape(count, part, width)).reshape(slot, width)
    cot_blocks = cotangent.reshape(count, part // 2, width)
    cots = []
    for k in range(count):
        piece = lax.dynamic_index_in_dim(cot_blocks, me ^ k, 0, False)
        cots.append(piece if k == 0 else swap(piece, "seq", seq_size, k))

    freq = head_dim // 2
    rates = jnp.exp(-jnp.arange(freq, dtype=F32) * (math.log(10000.0) / freq))
    turn = 2.0 * jnp.arange(half, dtype=F32)[:, None] * rates[None, :]
    cosines = jnp.tile(jnp.cos(turn), (1, 4))
    sines = jnp.tile(jnp.sin(turn), (1, 4))
    angles = jnp.arange(slot, dtype=F32)[:, None] * rates[None, :]
    feat = jnp.tile(jnp.concatenate([jnp.sin(angles), jnp.cos(angles)], 1), (1, 2)).astype(BF)
    eye = jnp.eye(4, dtype=BF)
    bd = (
        w_rel.reshape(groups, 4, head_dim, 1, head_dim) * eye[None, :, None, :, None]
    ).reshape(groups, 256, 256)

    attn, linv, p, q, k, v, pooled, xt, pt = attend(
        sc, x, query_weight, key_weight, value_weight, bd, cosines, sines, feat
    )
    g1 = gain_attn.astype(F32).reshape(1, width)
    g2 = gain_ffn.astype(F32).reshape(1, width)
    fed = feed(sc, attn, pooled, output_weight, inner_weight, outer_weight, g1, g2, cots)
    rows, act, slope, gouter, gtwo, unit, rstd, mixed, dgain_ffn = fed
    okeep, osend = wouter(sc, act, gouter, (1, 2, 4))
    tall = inner_weight.shape[0] * 4 // seq_size
    split = (seq_size // 2, grp_size, tall // grp_size, width)
    args = dict(
        gouter=gouter, slope=slope, wout=outer_weight, win=inner_weight, mixed=mixed, gtwo=gtwo,
        unit=unit, rstd=rstd, g1=g1, wo=output_weight, attn=attn, p=p, q=q, k=k, v=v, linv=linv,
        xt=xt, pt=pt, bd=bd, cos=cosines, sin=sines, feat=feat, wq=query_weight, wk=key_weight,
        wv=value_weight, okeep=okeep.reshape(split), osend=osend.reshape(split), okeep3=okeep,
        osend3=osend, rows=rows, dgain2=dgain_ffn,
    )
    grad_hidden, pooled_out, d_inner, d_outer, d_out, d_query, d_key, d_value, small = backward(
        args, seq_size, grp_size
    )
    pairs = width // 128
    d_rel = small[: 64 * pairs].reshape(pairs, 64, 2, 64).transpose(0, 2, 1, 3)
    d_attn = small[64 * pairs : 64 * pairs + pairs].reshape(width)
    d_ffn = small[64 * pairs + pairs : 64 * pairs + 2 * pairs].reshape(width)
    return (
        pooled_out.reshape(cotangent.shape),
        grad_hidden.reshape(hidden.shape),
        d_query,
        d_key,
        d_value,
        d_rel.reshape(w_rel.shape),
        d_out,
        d_attn,
        d_inner,
        d_outer,
        d_ffn,
    )


def solution(mesh):
    rows = P(None, "grp", None, "seq", None)
    spread = P(("seq", "grp"), None)
    sizes = dict(mesh.shape)
    return jax.shard_map(
        functools.partial(local, sizes["seq"], sizes["grp"]),
        mesh=mesh,
        in_specs=(rows, P(None, "grp", None)) + (P(),) * 9 + (rows,),
        out_specs=(
            rows, rows, spread, spread, spread, P(), spread, P(), spread, spread, P()
        ),
        check_vma=False,
    )
```

```python
import functools
import math
import types

import jax
import jax.numpy as jnp
from jax import lax
from jax.experimental import pallas as pl
from jax.experimental.pallas import tpu as pltpu
from jax.sharding import PartitionSpec as P

BF = jnp.bfloat16
F32 = jnp.float32
I32 = jnp.int32
MESH = pl.DeviceIdType.MESH
EPS = 1e-05
FFC = 512
QT = 256
OCHUNKS = 3
EARLY = ("O0", "O1")
ORDERS = {
    "O0": (1, 4, 2), "O1": (1, 4, 2), "O2": (1, 2, 4), "I0": (1, 2, 4), "I1": (1, 4, 2),
    "I2": (1, 4, 2), "W": (1, 2, 4), "G0": (1, 4, 2), "G1": (1, 2, 4), "G2": (1, 2, 4),
}


def sds(shape, dtype):
    return jax.ShapeDtypeStruct(shape, dtype)


def mm(a, b):
    return lax.dot_general(a, b, (((1,), (0,)), ((), ())), preferred_element_type=F32)


def mm_nt(a, b):
    return lax.dot_general(a, b, (((1,), (1,)), ((), ())), preferred_element_type=F32)


def mm_tn(a, b):
    return lax.dot_general(a, b, (((0,), (0,)), ((), ())), preferred_element_type=F32)


def rel_of(pos, order):
    bits = len(order)
    rel = 0
    for i, mask in enumerate(order):
        if (pos >> (bits - 1 - i)) & 1:
            rel |= mask
    return rel


def loop(count, body):
    def step(i, carry):
        body(i)
        return carry

    lax.fori_loop(0, count, step, 0)


def masks_of(size):
    return [1 << i for i in range(size.bit_length() - 1)]


def xor(rank, rel, size):
    total = 0
    for mask in masks_of(size):
        a = lax.rem(lax.div(rank, mask), 2)
        if isinstance(rel, int):
            total = total + mask * ((1 - a) if rel & mask else a)
        else:
            b = lax.rem(lax.div(rel, mask), 2)
            total = total + mask * (a + b - 2 * a * b)
    return total


def wide(value):
    return value.astype(F32)


def pool_matrix(rows):
    row = lax.broadcasted_iota(I32, (rows, 2 * rows), 0)
    col = lax.broadcasted_iota(I32, (rows, 2 * rows), 1)
    return jnp.where((col == 2 * row) | (col == 2 * row + 1), 0.5, 0.0).astype(BF)


def norm_parts(rows):
    centered = rows - jnp.mean(rows, -1, keepdims=True)
    rstd = lax.rsqrt(jnp.mean(centered * centered, -1, keepdims=True) + EPS)
    return centered * rstd, rstd


def norm_back(grad, unit, rstd, gain):
    scaled = grad * gain
    return rstd * (
        scaled
        - jnp.mean(scaled, -1, keepdims=True)
        - unit * jnp.mean(scaled * unit, -1, keepdims=True)
    )


FORE_INPUTS = list(
    dict(hidden=0, cot=0, lengths=0, wq=0, wk=0, wv=0, w_rel=0, wo=0, win=0, wout=0, g1=0, g2=0)
)
FORE_OUTPUTS = list(
    dict(
        attn=0, linv=0, p=0, q=0, k=0, v=0, xt=0, pt=0, bd=0, cos=0, sin=0, feat=0, rows=0,
        slope=0, gouter=0, gtwo=0, unit=0, rstd=0, mixed=0, outer=0, dgain=0,
    )
)


def fore_body(names, sizes, *refs):
    ref = types.SimpleNamespace(**dict(zip(FORE_INPUTS + FORE_OUTPUTS + names, refs)))
    seq, grp = sizes
    me = lax.axis_index("seq")
    half, width = ref.vq.shape
    slot = 2 * half
    part = slot // seq
    inner = ref.wout.shape[0]
    pairs = width // 128
    groups = width // 256
    steps = inner // FFC
    chips = seq // 2
    chip, core = lax.div(me, 2), lax.rem(me, 2)

    early = [(ref.wk, ref.vwk), (ref.wv, ref.vwv), (ref.wq, ref.vwq), (ref.w_rel, ref.vrel)]
    loads = [
        pltpu.make_async_copy(src, dst, ref.lsem.at[i])
        for i, (src, dst) in enumerate(early + [(ref.wo, ref.vwo)])
    ]

    def weights(j, buf):
        cols = pl.ds(pl.multiple_of(j * FFC, FFC), FFC)
        return [
            pltpu.make_async_copy(ref.win.at[:, cols], ref.vwin.at[buf], ref.wsem.at[0, buf]),
            pltpu.make_async_copy(ref.wout.at[cols, :], ref.vwout.at[buf], ref.wsem.at[1, buf]),
        ]

    stores = []

    def store(src, dst):
        copy = pltpu.make_async_copy(src, dst, ref.ssem.at[len(stores)])
        copy.start()
        stores.append(copy)

    def rows_of(rank, size):
        return pl.ds(pl.multiple_of(rank * size, size), size)

    def blocks(src, dst, size, bank, rel):
        copies = []
        for c in range(2):
            rank = 2 * xor(chip, rel, chips) + c
            copies.append(
                pltpu.make_async_remote_copy(
                    src_ref=src.at[rank],
                    dst_ref=dst.at[rows_of(me, size)],
                    send_sem=ref.asend.at[bank, 2 * rel + c],
                    recv_sem=ref.arecv.at[bank, 2 * rel + core],
                    device_id={"seq": rank},
                    device_id_type=MESH,
                )
            )
        return copies

    def arrivals(src, dst, size, bank, rel):
        copies = []
        for c in range(2):
            rank = 2 * xor(chip, rel, chips) + c
            copies.append(
                pltpu.make_async_remote_copy(
                    src_ref=src.at[rank],
                    dst_ref=dst.at[rows_of(rank, size)],
                    send_sem=ref.asend.at[bank, 2 * rel + c],
                    recv_sem=ref.arecv.at[bank, 2 * rel + c],
                    device_id={"seq": rank},
                    device_id_type=MESH,
                )
            )
        return copies

    def mate(src, dst, size, bank, receive):
        rank = 2 * chip + 1 - core
        spot = rank if receive else me
        return pltpu.make_async_remote_copy(
            src_ref=src.at[rank],
            dst_ref=dst.at[rows_of(spot, size)],
            send_sem=ref.asend.at[bank, 0],
            recv_sem=ref.arecv.at[bank, 0],
            device_id={"seq": rank},
            device_id_type=MESH,
        )

    hid = (ref.hidden, ref.vx, part, 0)
    cot = (ref.cot, ref.vcot, part // 2, 1)
    own = [
        pltpu.make_async_copy(src.at[me], dst.at[rows_of(me, size)], ref.osem.at[bank])
        for src, dst, size, bank in (hid, cot)
    ]

    barrier = pltpu.get_barrier_semaphore()
    for k in range(1, seq):
        pl.semaphore_signal(
            barrier, inc=1, device_id={"seq": lax.rem(me + k, seq)}, device_id_type=MESH
        )
    own[0].start()
    for copy in loads[:4]:
        copy.start()
    pl.semaphore_wait(barrier, seq - 1)
    mate(*hid, False).start()
    near, far = list(range(1, chips - 1)), [chips - 1]
    for rel in near:
        for copy in blocks(*hid, rel):
            copy.start()

    lane_row = lax.broadcasted_iota(I32, (1, 128), 1)
    freq = wide(lax.rem(lane_row, 32))
    rate = jnp.exp(freq * (-math.log(10000.0) / 32))
    pos = wide(lax.broadcasted_iota(I32, (half, 1), 0))
    turn = (2.0 * pos) * rate
    ref.vcos[...] = jnp.cos(turn)
    ref.vsin[...] = jnp.sin(turn)
    first_half = lax.rem(lane_row, 64) < 32
    for t in range(2):
        angle = (pos + float(half * t)) * rate
        ref.vfeat[half * t : half * (t + 1), :] = jnp.where(
            first_half, jnp.sin(angle), jnp.cos(angle)
        ).astype(BF)
    store(ref.vcos, ref.cos)
    store(ref.vsin, ref.sin)
    store(ref.vfeat, ref.feat)
    for copy in loads[:4]:
        copy.wait()
    ref.vbd[...] = jnp.zeros_like(ref.vbd)
    for h in range(2 * pairs):
        ref.vbd[h // 4, 64 * (h % 4) : 64 * (h % 4) + 64, 64 * (h % 4) : 64 * (h % 4) + 64] = (
            ref.vrel[h]
        )
    store(ref.vbd, ref.bd)

    pool = pool_matrix(part)

    def project(index):
        rows = rows_of(index, 2 * part)
        small = rows_of(index, part)
        tile = ref.vx[rows, :]
        ref.vk[rows, :] = mm(tile, ref.vwk[...]).astype(BF)
        ref.vv[rows, :] = mm(tile, ref.vwv[...]).astype(BF)
        pooled = mm(pool, tile)
        ref.vpool[small, :] = pooled
        short = pooled.astype(BF)
        ref.vq[small, :] = mm(short, ref.vwq[...]).astype(BF)
        ref.vxt[:, rows] = tile.T
        ref.vpt[:, small] = short.T

    mate(*hid, True).wait_recv()
    own[0].wait()
    project(chip)
    for rel in near:
        for copy in arrivals(*hid, rel):
            copy.wait_recv()
    for rel in far:
        for copy in blocks(*hid, rel):
            copy.start()
    for rel in near:
        project(xor(chip, rel, chips))
    for rel in far:
        for copy in arrivals(*hid, rel):
            copy.wait_recv()
    own[1].start()
    mate(*cot, False).start()
    for rel in near + far:
        for copy in blocks(*cot, rel):
            copy.start()
    for rel in far:
        project(xor(chip, rel, chips))
    store(ref.vk, ref.k)
    store(ref.vv, ref.v)
    store(ref.vq, ref.q)
    store(ref.vxt, ref.xt)
    store(ref.vpt, ref.pt)
    loads[4].start()
    for copy in weights(0, 0):
        copy.start()

    scale = 0.125 * 1.4426950408889634
    low = lax.rem(lane_row, 64) < 32
    first_head = lane_row < 64
    seqs, micro = ref.lengths.shape
    mine_row = lax.broadcasted_iota(I32, (seqs, micro), 0) == lax.rem(me, seqs)
    mine_col = lax.broadcasted_iota(I32, (seqs, micro), 1) == lax.div(me, seqs)
    limit = jnp.where(mine_row & mine_col, wide(ref.lengths[...]), 0.0)
    limit = jnp.sum(jnp.sum(limit, 1, keepdims=True), 0, keepdims=True)
    key_ok = wide(lax.broadcasted_iota(I32, (1, slot), 1)) < limit
    ones = jnp.ones((slot, 128), BF)

    def probs(i, buf):
        return pltpu.make_async_copy(
            ref.vp.at[buf], ref.p.at[pl.ds(2 * i, 2)], ref.wsem.at[2, buf]
        )

    def attention_step(i):
        buf = lax.rem(i, 2)

        @pl.when(i >= 2)
        def free():
            probs(i - 2, buf).wait()

        cols = pl.ds(pl.multiple_of(i * 128, 128), 128)
        part_bd = pl.ds(pl.multiple_of(buf * 128, 128), 128)
        rel = mm(ref.vq[:, cols], ref.vbd[lax.div(i, 2), part_bd, part_bd])
        other = jnp.where(low, pltpu.roll(rel, 96, 1), -pltpu.roll(rel, 32, 1))
        ref.vsh[...] = (rel * ref.vcos[...] + other * ref.vsin[...]).astype(BF)
        key_side = jnp.concatenate([ref.vk[:, cols], ref.vfeat[...]], 1)
        value_side = jnp.concatenate([ref.vv[:, cols], ones], 1)
        for t in range(half // QT):
            rows = slice(QT * t, QT * (t + 1))
            q_part = ref.vq[rows, cols]
            s_part = ref.vsh[rows, :]
            outs = []
            for h in range(2):
                mine = first_head if h == 0 else jnp.logical_not(first_head)
                zero = jnp.zeros_like(q_part)
                left = jnp.concatenate(
                    [jnp.where(mine, q_part, zero), jnp.where(mine, s_part, zero)], 1
                )
                s = jnp.where(key_ok, mm_nt(left, key_side), -1e30)
                top = jnp.max(s, -1, keepdims=True)
                p = jnp.exp2((s - top) * scale).astype(BF)
                ref.vp[buf, h, rows, :] = p
                acc = mm(p, value_side)
                inv = 1.0 / acc[:, 128:]
                outs.append((acc[:, :128] * inv, inv))
            ref.vattn[rows, cols] = jnp.where(first_head, outs[0][0], outs[1][0]).astype(BF)
            ref.vlinv[rows, cols] = jnp.where(first_head, outs[0][1], outs[1][1])
        probs(i, buf).start()

    loop(pairs, attention_step)
    store(ref.vattn, ref.attn)
    store(ref.vlinv, ref.linv)

    loads[4].wait()
    unit, rstd = norm_parts(ref.vpool[...] + mm(ref.vattn[...], ref.vwo[...]))
    mixed = unit * wide(ref.g1[...]).reshape(1, width)
    ref.vunit[...] = unit
    ref.vrstd[...] = jnp.broadcast_to(rstd, ref.vrstd.shape)
    ref.vacc[...] = mixed
    short = mixed.astype(BF)
    ref.vmix[...] = short
    ref.vmt[...] = short.T
    store(ref.vunit, ref.unit)
    store(ref.vrstd, ref.rstd)
    store(ref.vmt, ref.mixed)

    def slopes(j, buf):
        cols = pl.ds(pl.multiple_of(j * FFC, FFC), FFC)
        return pltpu.make_async_copy(
            ref.vslope.at[buf], ref.slope.at[:, cols], ref.wsem.at[3, buf]
        )

    def feed_step(j):
        buf = lax.rem(j, 2)
        for copy in weights(j, buf):
            copy.wait()

        @pl.when(j + 1 < steps)
        def more():
            for copy in weights(j + 1, 1 - buf):
                copy.start()

        @pl.when(j >= 2)
        def free():
            slopes(j - 2, buf).wait()

        pre = mm(ref.vmix[...], ref.vwin[buf])
        cdf = 0.5 * (1.0 + lax.erf(pre * 0.7071067811865476))
        act = (pre * cdf).astype(BF)
        ref.vslope[buf] = (
            cdf + pre * (jnp.exp(pre * pre * -0.5) * 0.3989422804014327)
        ).astype(BF)
        ref.vacc[...] += mm(act, ref.vwout[buf])
        ref.vactt[pl.ds(pl.multiple_of(j * FFC, FFC), FFC), :] = act.T
        slopes(j, buf).start()

    loop(steps, feed_step)
    mate(*cot, True).wait_recv()
    own[1].wait()
    for rel in near + far:
        for copy in arrivals(*cot, rel):
            copy.wait_recv()
    unit, rstd = norm_parts(ref.vacc[...])
    valid = wide(2 * lax.broadcasted_iota(I32, (half, 1), 0)) < limit
    g2 = wide(ref.g2[...]).reshape(1, width)
    ref.vrows[...] = jnp.where(valid, unit * g2, 0.0).astype(BF)
    store(ref.vrows, ref.rows)
    grad = jnp.where(valid, wide(ref.vcot[...]), 0.0)
    ref.dgain[...] = jnp.sum(grad * unit, 0, keepdims=True)
    two = norm_back(grad, unit, rstd, g2)
    ref.vacc[...] = two
    ref.vgo[...] = two.astype(BF)
    store(ref.vacc, ref.gtwo)
    store(ref.vgo, ref.gouter)

    tall = inner // seq
    count = ref.outer.shape[1]
    span = width // count

    def outer_step(pos):
        bits = [lax.div(pos, 4), lax.rem(lax.div(pos, 2), 2), lax.rem(pos, 2)]
        rel = bits[0] + 2 * bits[1] + 4 * bits[2]
        value = mm(ref.vactt[rows_of(xor(me, rel, seq), tall), :], ref.vgo[...]).astype(BF)
        for n in range(count):
            order = ORDERS["O" + str(n)]
            spot = 2 * bits[1] + bits[2] if order[1] == 2 else 2 * bits[2] + bits[1]
            ref.vouter[bits[0], n, spot] = value[:, span * n : span * (n + 1)]

    loop(seq, outer_step)
    store(ref.vouter, ref.outer)
    for i in (pairs - 2, pairs - 1):
        probs(i, i % 2).wait()
    for j in (steps - 2, steps - 1):
        slopes(j, j % 2).wait()
    for copy in stores:
        copy.wait()
    for bank in (hid, cot):
        mate(*bank, False).wait_send()
        for rel in near + far:
            for copy in blocks(*bank, rel):
                copy.wait_send()


def forward(args, seq, grp):
    count, part, width = args["hidden"].shape
    slot = part * seq
    half = slot // 2
    inner = args["wout"].shape[0]
    heads = width // 64
    outer = (2, OCHUNKS, 4, inner // seq, width // OCHUNKS)
    vm = pltpu.VMEM
    scratch = dict(
        vx=vm((slot, width), BF),
        vcot=vm((half, width), BF),
        vwq=vm((width, width), BF),
        vwk=vm((width, width), BF),
        vwv=vm((width, width), BF),
        vrel=vm((heads, 64, 64), BF),
        vwo=vm((width, width), BF),
        vwin=vm((2, width, FFC), BF),
        vwout=vm((2, FFC, width), BF),
        vcos=vm((half, 128), F32),
        vsin=vm((half, 128), F32),
        vfeat=vm((slot, 128), BF),
        vbd=vm((width // 256, 256, 256), BF),
        vq=vm((half, width), BF),
        vk=vm((slot, width), BF),
        vv=vm((slot, width), BF),
        vpool=vm((half, width), F32),
        vxt=vm((width, slot), BF),
        vpt=vm((width, half), BF),
        vsh=vm((half, 128), BF),
        vp=vm((2, 2, half, slot), BF),
        vattn=vm((half, width), BF),
        vlinv=vm((half, width), F32),
        vunit=vm((half, width), F32),
        vrstd=vm((half, 128), F32),
        vacc=vm((half, width), F32),
        vmix=vm((half, width), BF),
        vmt=vm((width, half), BF),
        vslope=vm((2, half, FFC), BF),
        vactt=vm((inner, half), BF),
        vrows=vm((half, width), BF),
        vgo=vm((half, width), BF),
        vouter=vm(outer, BF),
        lsem=pltpu.SemaphoreType.DMA((5,)),
        wsem=pltpu.SemaphoreType.DMA((4, 2)),
        ssem=pltpu.SemaphoreType.DMA((24,)),
        osem=pltpu.SemaphoreType.DMA((2,)),
        asend=pltpu.SemaphoreType.DMA((2, seq)),
        arecv=pltpu.SemaphoreType.DMA((2, seq)),
    )
    names = list(scratch)
    shapes = dict(
        attn=sds((half, width), BF),
        linv=sds((half, width), F32),
        p=sds((heads, half, slot), BF),
        q=sds((half, width), BF),
        k=sds((slot, width), BF),
        v=sds((slot, width), BF),
        xt=sds((width, slot), BF),
        pt=sds((width, half), BF),
        bd=sds((width // 256, 256, 256), BF),
        cos=sds((half, 128), F32),
        sin=sds((half, 128), F32),
        feat=sds((slot, 128), BF),
        rows=sds((half, width), BF),
        slope=sds((half, inner), BF),
        gouter=sds((half, width), BF),
        gtwo=sds((half, width), F32),
        unit=sds((half, width), F32),
        rstd=sds((half, 128), F32),
        mixed=sds((width, half), BF),
        outer=sds(outer, BF),
        dgain=sds((1, width), F32),
    )
    hbm = pl.BlockSpec(memory_space=pl.ANY)
    vmem = pl.BlockSpec(memory_space=pltpu.VMEM)
    spots = dict(g1=vmem, g2=vmem, lengths=vmem)
    outs = pl.pallas_call(
        functools.partial(fore_body, names, (seq, grp)),
        out_shape=[shapes[n] for n in FORE_OUTPUTS],
        in_specs=[spots.get(n, hbm) for n in FORE_INPUTS],
        out_specs=[hbm] * (len(FORE_OUTPUTS) - 1) + [vmem],
        scratch_shapes=list(scratch.values()),
        compiler_params=pltpu.CompilerParams(
            collective_id=0, has_side_effects=True, vmem_limit_bytes=63 << 20
        ),
        cost_estimate=pl.CostEstimate(
            flops=20_000_000_000, bytes_accessed=60_000_000, transcendentals=0
        ),
    )(*[args[n] for n in FORE_INPUTS])
    return dict(zip(FORE_OUTPUTS, outs))


class Chunk:
    def __init__(self, env, index, order, early, keep, send, recv, zbuf, recvz, out):
        self.env, self.index, self.order, self.early = env, index, order, early
        self.keep, self.send, self.recv = keep, send, recv
        self.zbuf, self.recvz, self.out = zbuf, recvz, out

    def remote(self, slot, src, dst, device):
        return pltpu.make_async_remote_copy(
            src_ref=src,
            dst_ref=dst,
            send_sem=self.env.ssem.at[self.index, slot],
            recv_sem=self.env.rsem.at[self.index, slot],
            device_id=device,
            device_id_type=MESH,
        )

    def seq_copy(self, stage):
        device = {"seq": xor(self.env.me, self.order[stage], self.env.seq)}
        if stage == 0:
            src = self.send
        else:
            half = 4 >> stage
            src = (self.zbuf if self.early else self.recv[0]).at[pl.ds(half, half)]
        return self.remote(stage, src, self.recv[stage], device)

    def z_copies(self):
        grp, z = self.env.grp, self.env.z
        copies = []
        for d in range(1, grp):
            peer = lax.rem(z + d, grp)
            src = self.recv[0].at[:, peer] if self.early else self.zbuf.at[peer]
            copies.append(self.remote(2 + d, src, self.recvz.at[d - 1], {"grp": peer}))
        return copies

    def step(self, n):
        keep, (recv0, recv1, recv2) = self.keep, self.recv
        zbuf, recvz, grp, z = self.zbuf, self.recvz, self.env.grp, self.env.z
        if n == 0:
            self.seq_copy(0).start()
        elif n == 1 and self.early:
            self.seq_copy(0).wait()

            def add(i):
                p, g = lax.div(i, grp), lax.rem(i, grp)
                recv0[p, g] = (wide(keep[p, g]) + wide(recv0[p, g])).astype(BF)

            loop(4 * grp, add)
            for copy in self.z_copies():
                copy.start()
        elif n == 2 and self.early:
            for copy in self.z_copies():
                copy.wait()

            def add(p):
                total = wide(recv0[p, z])
                for d in range(grp - 1):
                    total = total + wide(recvz[d, p])
                zbuf[p] = total.astype(BF)

            loop(4, add)
            self.seq_copy(1).start()
        elif n == 3 and self.early:
            self.seq_copy(1).wait()
            zbuf[1] = (wide(zbuf[1]) + wide(recv1[1])).astype(BF)
            self.seq_copy(2).start()
        elif n == 4 and self.early:
            self.seq_copy(2).wait()
            self.out(wide(zbuf[0]) + wide(recv1[0]) + wide(recv2[0]))
        elif n == 1:
            self.seq_copy(0).wait()
            parts = keep.shape[1] // 48

            def add(i):
                p, rows = 2 + lax.div(i, parts), pl.ds(pl.multiple_of(48 * lax.rem(i, parts), 48), 48)
                recv0[p, rows] = (wide(keep[p, rows]) + wide(recv0[p, rows])).astype(BF)

            loop(2 * parts, add)
            self.seq_copy(1).start()
        elif n == 2:
            self.seq_copy(1).wait()

            def add(i):
                rows = pl.ds(pl.multiple_of(48 * i, 48), 48)
                recv0[1, rows] = (
                    wide(keep[1, rows]) + wide(recv0[1, rows]) + wide(recv1[1, rows])
                ).astype(BF)

            loop(keep.shape[1] // 48, add)
            self.seq_copy(2).start()
        elif n == 3:
            self.seq_copy(2).wait()
            share = keep.shape[1] // grp
            for start in range(0, keep.shape[1], 48):
                rows = slice(start, start + 48)
                total = (
                    wide(keep[0, rows]) + wide(recv0[0, rows])
                    + wide(recv1[0, rows]) + wide(recv2[0, rows])
                )
                size = min(share, 48)
                for low in range(start, start + 48, size):
                    g, inside = low // share, low % share
                    piece = total[low - start : low - start + size].astype(BF)
                    if zbuf.shape[1] == share:
                        zbuf[g, inside : inside + size] = piece
                    else:
                        mid = zbuf.shape[2]
                        zbuf[g, :share] = piece[:, :mid]
                        zbuf[g, share:] = piece[:, mid:]
            for copy in self.z_copies():
                copy.start()
        else:
            for copy in self.z_copies():
                copy.wait()
            total = wide(zbuf[z])
            for d in range(grp - 1):
                total = total + wide(recvz[d])
            share = keep.shape[1] // grp
            if zbuf.shape[1] != share:
                total = jnp.concatenate([total[:share], total[share:]], 1)
            self.out(total)


BACK_INPUTS = list(
    dict(
        gouter=0, slope=0, wout=0, win=0, mixed=0, gtwo=0, unit=0, rstd=0, g1=0, wo=0, attn=0,
        p=0, q=0, k=0, v=0, linv=0, xt=0, pt=0, bd=0, cos=0, sin=0, feat=0, wq=0, wk=0, wv=0,
        outer3=0, outer4=0, rows=0, dgain2=0,
    )
)
BACK_OUTPUTS = list(
    dict(hidden=0, pooled=0, inner=0, outer=0, out=0, query=0, key=0, value=0, small=0)
)
POINTS = {
    ("B", 2): [("O1", 1)],
    ("B", 3): [("I1", 0)],
    ("B", 4): [("O2", 1), ("I0", 0), ("I1", 1)],
    ("B", 5): [("I2", 0)],
    ("L", 0): [("W", 0), ("I0", 1), ("O0", 1), ("I2", 1)],
    ("U", 1): [("G0", 0), ("I1", 2), ("W", 1), ("O2", 2), ("O1", 2), ("I0", 2)],
    ("U", 3): [("I2", 2), ("I1", 3), ("G1", 0), ("G0", 1)],
    ("U", 4): [("G1", 1), ("O1", 3), ("O2", 3)],
    ("U", 5): [("S", 0), ("I2", 3), ("W", 2), ("I0", 3), ("O0", 2), ("G2", 0), ("S", 1)],
    ("T", 0): [
        ("G1", 2), ("G0", 2), ("G2", 1), ("S", 2), ("I1", 4), ("W", 3), ("I2", 4), ("G1", 3),
        ("W", 4), ("H", 0), ("S", 3), ("G2", 2), ("G0", 3), ("O0", 3), ("I0", 4), ("S", 4),
        ("O0", 4), ("G2", 3), ("O1", 4), ("G0", 4), ("H", 1), ("O2", 4), ("G1", 4), ("S", 5),
        ("G2", 4),
    ],
}


def back_body(names, sizes, *refs):
    every = dict(zip(BACK_INPUTS + BACK_OUTPUTS + names, refs))
    ref = types.SimpleNamespace(**every)
    seq, grp = sizes
    me = lax.axis_index("seq")
    z = lax.axis_index("grp")
    env = types.SimpleNamespace(me=me, z=z, seq=seq, grp=grp, ssem=ref.ssem, rsem=ref.rsem)
    half, width = ref.vgo.shape
    slot = 2 * half
    inner = ref.slope.shape[1]
    steps = inner // FFC
    pairs = width // 128
    groups = width // 256
    lsem = ref.lsem

    plain = [
        (ref.gouter, ref.vgo), (ref.mixed, ref.vmt), (ref.gtwo, ref.vacc),
        (ref.unit, ref.vun), (ref.rstd, ref.vrs), (ref.wo, ref.vwo), (ref.attn, ref.vat),
        (ref.linv, ref.vlinv),
        (ref.q, ref.vq), (ref.k, ref.vk), (ref.v, ref.vv), (ref.feat, ref.vfeat),
        (ref.cos, ref.vcos), (ref.sin, ref.vsin), (ref.bd, ref.vbd), (ref.xt, ref.vxt),
        (ref.wq, ref.vwq), (ref.wk, ref.vwk), (ref.wv, ref.vwv), (ref.pt, ref.vmt),
    ]
    local = [pltpu.make_async_copy(*pair, lsem.at[i]) for i, pair in enumerate(plain)]
    base = len(plain)

    def weights(j, buf):
        cols = pl.ds(pl.multiple_of(j * FFC, FFC), FFC)
        return [
            pltpu.make_async_copy(ref.slope.at[:, cols], ref.vslope.at[buf], ref.wsem.at[0, buf]),
            pltpu.make_async_copy(ref.wout.at[cols, :], ref.vwout.at[buf], ref.wsem.at[1, buf]),
            pltpu.make_async_copy(ref.win.at[:, cols], ref.vwin.at[buf], ref.wsem.at[2, buf]),
        ]

    def probs(i, buf):
        return pltpu.make_async_copy(
            ref.p.at[pl.ds(2 * i, 2)], ref.vp.at[buf], ref.wsem.at[3, buf]
        )

    chunks = {}
    def out_cols(name, start, stop):
        def put(value):
            every[name][:, start:stop] = value

        return put

    def out_three(g):
        def put(value):
            for i, name in enumerate(("query", "key", "value")):
                every[name][:, 256 * g : 256 * (g + 1)] = value[:, 256 * i : 256 * (i + 1)]

        return put

    kept = []
    for index, (name, order) in enumerate(ORDERS.items()):
        early = name in EARLY
        kind = name[0]
        n = int(name[1]) if len(name) > 1 else 0
        recv = [every[name + "r0"], every[name + "r1"], every[name + "r2"]]
        if kind == "O":
            side = ref.outer4 if early else ref.outer3
            keep, send = every[name + "k"], side.at[1, n]
            kept.append(pltpu.make_async_copy(side.at[0, n], keep, lsem.at[base + n]))
            span = width // OCHUNKS
            out = out_cols("outer", span * n, span * (n + 1))
        elif kind == "I":
            keep, send = ref.ikeep.at[n], ref.isend.at[n]
            out = out_cols("inner", 1024 * n, 1024 * (n + 1))
        elif kind == "W":
            keep, send = ref.wkeep, ref.wsend
            out = out_cols("out", 0, width)
        else:
            keep, send = ref.gkeep.at[n], ref.gsend.at[n]
            out = out_three(n)
        chunks[name] = Chunk(
            env, index, order, early, keep, send, recv, every[name + "z"], every[name + "rz"], out
        )

    def spread(src, dst, sem):
        size = dst.shape[1]
        block = lambda b: src.at[pl.ds(pl.multiple_of(b * size, size), size)]
        copies = [pltpu.make_async_copy(block(me), dst.at[me], ref.dsem.at[sem])]
        for k in range(1, seq):
            peer = lax.rem(me + k, seq)
            copies.append(
                pltpu.make_async_remote_copy(
                    src_ref=block(peer),
                    dst_ref=dst.at[me],
                    send_sem=ref.asend.at[sem, k],
                    recv_sem=ref.arecv.at[sem, k],
                    device_id={"seq": peer},
                    device_id_type=MESH,
                )
            )
        return copies

    doubling = [("seq", m) for m in masks_of(seq)] + [("grp", m) for m in masks_of(grp)]

    def small_copy(n):
        axis, mask = doubling[n]
        rank, size = (me, seq) if axis == "seq" else (z, grp)
        return pltpu.make_async_remote_copy(
            src_ref=ref.small,
            dst_ref=ref.vsmall.at[n],
            send_sem=ref.msend.at[n],
            recv_sem=ref.mrecv.at[n],
            device_id={axis: xor(rank, mask, size)},
            device_id_type=MESH,
        )

    def small_step(n):
        if 0 < n <= len(doubling):
            small_copy(n - 1).wait()
            ref.small[...] += ref.vsmall[n - 1]
        if n < len(doubling):
            small_copy(n).start()

    def event(name, n):
        if name == "H":
            for copy in spread(ref.vk, ref.hidden, 1):
                copy.start() if n == 0 else copy.wait()
        elif name == "S":
            small_step(n)
            if n == 5:
                for more in range(6, len(doubling) + 1):
                    small_step(more)
        else:
            chunks[name].step(n)

    def point(kind, index, dynamic=None):
        todo = POINTS.get((kind, index), [])
        if not todo:
            return
        if dynamic is None:
            for name, n in todo:
                event(name, n)
        else:

            @pl.when(dynamic == index)
            def run():
                for name, n in todo:
                    event(name, n)

    barrier = pltpu.get_barrier_semaphore()
    for k in range(1, seq):
        pl.semaphore_signal(
            barrier, inc=1, device_id={"seq": lax.rem(me + k, seq)}, device_id_type=MESH
        )
    for k in range(1, grp):
        pl.semaphore_signal(
            barrier, inc=1, device_id={"grp": lax.rem(z + k, grp)}, device_id_type=MESH
        )
    for copy in local[:3]:
        copy.start()
    for copy in weights(0, 0):
        copy.start()
    pl.semaphore_wait(barrier, seq + grp - 2)
    for n in range(OCHUNKS):
        chunks["O" + str(n)].step(0)
    for copy in spread(ref.rows, ref.pooled, 0):
        copy.start()
    for copy in kept:
        copy.start()
    for copy in local[:3]:
        copy.wait()

    def rows_of(count, rel):
        step = width // seq
        return pl.ds(pl.multiple_of(xor(me, rel, seq) * step, step), step)

    def split(order, cols, keep, send):
        for pos in range(seq):
            block = ref.vval[rows_of(width, rel_of(pos, order)), cols]
            (keep if pos < seq // 2 else send)(pos % (seq // 2), block)

    def feed_step(j):
        buf = lax.rem(j, 2)
        for copy in weights(j, buf):
            copy.wait()

        @pl.when(j + 1 < steps)
        def more():
            for copy in weights(j + 1, 1 - buf):
                copy.start()

        @pl.when(j == 1)
        def rest():
            for copy in local[3:-1]:
                copy.start()
            probs(0, 0).start()
            for copy in kept:
                copy.wait()

        grad = mm_nt(ref.vgo[...], ref.vwout[buf])
        hid = (wide(ref.vslope[buf]) * grad).astype(BF)
        ref.vacc[...] += mm_nt(hid, ref.vwin[buf])
        ref.vval[:, :FFC] = mm(ref.vmt[...], hid).astype(BF)
        c = lax.div(j, 2)
        cols = pl.ds(pl.multiple_of(lax.rem(j, 2) * FFC, FFC), FFC)

        def keep(pos, block):
            ref.ikeep[c, pos, :, cols] = block

        def send(pos, block):
            ref.isend[c, pos, :, cols] = block

        for n in range(steps // 2):

            @pl.when(c == n)
            def place():
                split(ORDERS["I" + str(n)], slice(0, FFC), keep, send)

        for t in range(steps):
            point("B", t, j)

    loop(steps, feed_step)

    local[-1].start()
    for copy in local[3:8]:
        copy.wait()
    grad = ref.vacc[...]
    unit = ref.vun[...]
    small = ref.small
    dgain = jnp.sum(grad * unit, 0, keepdims=True)
    for i in range(pairs):
        small[64 * pairs + i, :] = dgain[0, 128 * i : 128 * (i + 1)]
        small[64 * pairs + pairs + i, :] = ref.dgain2[0, 128 * i : 128 * (i + 1)]
    for i in range(64 * pairs + 2 * pairs, small.shape[0]):
        small[i, :] = jnp.zeros((128,), F32)
    one = norm_back(grad, unit, ref.vrs[:, :1], wide(ref.g1[...]).reshape(1, width))
    ref.vun[...] = one
    branch = one.astype(BF)
    attn = ref.vat[...]
    ref.vval[...] = mm_tn(attn, branch).astype(BF)

    def keep_w(pos, block):
        ref.wkeep[pos] = block

    def send_w(pos, block):
        ref.wsend[pos] = block

    split(ORDERS["W"], slice(0, width), keep_w, send_w)
    scaled = mm_nt(branch, ref.vwo[...]) * ref.vlinv[...]
    ref.vgo[...] = scaled.astype(BF)
    ref.vacc[...] = scaled * wide(attn)
    for copy in local[8:]:
        copy.wait()
    point("L", 0)

    lane = lax.broadcasted_iota(I32, (1, 128), 1)
    low = lax.rem(lane, 64) < 32
    first_head = lane < 64
    ones = jnp.broadcast_to(jnp.where(lane < 2, 1.0, 0.0).astype(BF), (slot, 128))

    def attention_step(i):
        buf = lax.rem(i, 2)
        g = lax.div(i, 2)
        probs(i, buf).wait()

        @pl.when(i + 1 < pairs)
        def more():
            probs(i + 1, 1 - buf).start()

        cols = pl.ds(pl.multiple_of(i * 128, 128), 128)
        part = pl.ds(pl.multiple_of(buf * 128, 128), 128)
        ref.vqt[...] = ref.vq[:, cols].T
        ref.vgt[...] = ref.vgo[:, cols].T
        key_side = jnp.concatenate([ref.vk[:, cols], ref.vfeat[...]], 1)
        value_side = jnp.concatenate([ref.vv[:, cols], ones], 1)
        outs = [[], []]
        for h in range(2):
            mine = first_head if h == 0 else jnp.logical_not(first_head)
            for t in range(half // QT):
                rows = slice(QT * t, QT * (t + 1))
                g_part = ref.vgo[rows, cols]
                delta = jnp.sum(jnp.where(mine, ref.vacc[rows, cols], 0.0), -1, keepdims=True)
                coarse = wide(delta.astype(BF))
                tail = jnp.where(lane == 0, coarse, jnp.where(lane == 1, delta - coarse, 0.0))
                left = jnp.concatenate(
                    [jnp.where(mine, g_part, jnp.zeros_like(g_part)), (-tail).astype(BF)], 1
                )
                ds = (wide(ref.vp[buf, h, rows, :]) * mm_nt(left, value_side)).astype(BF)
                ref.vds[rows, :] = ds
                outs[h].append(mm(ds, key_side))
            lines = slice(64 * h, 64 * (h + 1))
            ref.vkt[lines, :] = (mm(ref.vqt[lines, :], ref.vds[...]) * 0.125).astype(BF)
            ref.vvt[lines, :] = mm(ref.vgt[lines, :], ref.vp[buf, h]).astype(BF)
        for t in range(half // QT):
            rows = slice(QT * t, QT * (t + 1))
            a, b = outs[0][t], outs[1][t]
            ref.vgqf[rows, part] = jnp.where(first_head, a[:, :128], b[:, :128]) * 0.125
            shift = jnp.where(first_head, a[:, 128:], b[:, 128:]) * 0.125
            other = jnp.where(low, -pltpu.roll(shift, 96, 1), pltpu.roll(shift, 32, 1))
            ref.vrel[rows, part] = (
                shift * ref.vcos[rows, :] + other * ref.vsin[rows, :]
            ).astype(BF)
        ref.vk[:, cols] = ref.vkt[...].T
        ref.vv[:, cols] = ref.vvt[...].T
        both = mm(ref.vqt[...], ref.vrel[:, part])
        small[pl.ds(pl.multiple_of(64 * i, 64), 64), :] = jnp.where(first_head, both[:64], both[64:])

        @pl.when(buf == 1)
        def tail():
            wide_cols = pl.ds(pl.multiple_of(g * 256, 256), 256)
            gq = (ref.vgqf[...] + mm_nt(ref.vrel[...], ref.vbd[g])).astype(BF)
            ref.vq[:, wide_cols] = gq
            dk = ref.vk[:, wide_cols]
            dv = ref.vv[:, wide_cols]
            ref.vval[:, 0:256] = mm(ref.vmt[...], gq).astype(BF)
            ref.vval[:, 256:512] = mm(ref.vxt[...], dk).astype(BF)
            ref.vval[:, 512:768] = mm(ref.vxt[...], dv).astype(BF)

            def keep(pos, block):
                ref.gkeep[g, pos] = block

            def send(pos, block):
                ref.gsend[g, pos] = block

            for n in range(groups):

                @pl.when(g == n)
                def place():
                    split(ORDERS["G" + str(n)], slice(0, 768), keep, send)

        for t in range(pairs):
            point("U", t, i)

    loop(pairs, attention_step)

    spread_m = wide(pool_matrix(128)).T.astype(BF)

    def token_step(t):
        small_rows = pl.ds(pl.multiple_of(128 * t, 128), 128)
        rows = pl.ds(pl.multiple_of(256 * t, 256), 256)
        pooled = ref.vun[small_rows, :] + mm_nt(ref.vq[small_rows, :], ref.vwq[...])
        high = pooled.astype(BF)
        rest = (pooled - wide(high)).astype(BF)
        acc = mm(spread_m, high) + mm(spread_m, rest)
        acc = acc + mm_nt(ref.vk[rows, :], ref.vwk[...])
        acc = (acc + mm_nt(ref.vv[rows, :], ref.vwv[...])).astype(BF)
        ref.vk[rows, :] = acc

    loop(slot // 256, token_step)
    point("T", 0)
    for copy in spread(ref.rows, ref.pooled, 0):
        copy.wait()


def backward(args, seq, grp):
    half, width = args["gouter"].shape
    slot = 2 * half
    inner = args["slope"].shape[1]
    part = slot // seq
    share = width // seq
    steps = seq.bit_length() - 1 + grp.bit_length() - 1
    small_rows = (64 * (width // 128) + 2 * (width // 128) + 7) // 8 * 8
    vm = pltpu.VMEM
    scratch = dict(
        vgo=vm((half, width), BF),
        vmt=vm((width, half), BF),
        vacc=vm((half, width), F32),
        vun=vm((half, width), F32),
        vrs=vm((half, 128), F32),
        vwo=vm((width, width), BF),
        vat=vm((half, width), BF),
        vslope=vm((2, half, FFC), BF),
        vwout=vm((2, FFC, width), BF),
        vwin=vm((2, width, FFC), BF),
        vval=vm((width, 768), BF),
        vp=vm((2, 2, half, slot), BF),
        vq=vm((half, width), BF),
        vk=vm((slot, width), BF),
        vv=vm((slot, width), BF),
        vlinv=vm((half, width), F32),
        vxt=vm((width, slot), BF),
        vbd=vm(args["bd"].shape, BF),
        vcos=vm((half, 128), F32),
        vsin=vm((half, 128), F32),
        vfeat=vm((slot, 128), BF),
        vqt=vm((128, half), BF),
        vgt=vm((128, half), BF),
        vgqf=vm((half, 256), F32),
        vrel=vm((half, 256), BF),
        vds=vm((half, slot), BF),
        vkt=vm((128, slot), BF),
        vvt=vm((128, slot), BF),
        vwq=vm((width, width), BF),
        vwk=vm((width, width), BF),
        vwv=vm((width, width), BF),
        vsmall=vm((steps, small_rows, 128), F32),
        ikeep=vm((3, 4, share, 1024), BF),
        isend=vm((3, 4, share, 1024), BF),
        wkeep=vm((4, share, width), BF),
        wsend=vm((4, share, width), BF),
        gkeep=vm((3, 4, share, 768), BF),
        gsend=vm((3, 4, share, 768), BF),
        lsem=pltpu.SemaphoreType.DMA((20 + OCHUNKS,)),
        wsem=pltpu.SemaphoreType.DMA((4, 2)),
        dsem=pltpu.SemaphoreType.DMA((2,)),
        asend=pltpu.SemaphoreType.DMA((2, seq)),
        arecv=pltpu.SemaphoreType.DMA((2, seq)),
        msend=pltpu.SemaphoreType.DMA((steps,)),
        mrecv=pltpu.SemaphoreType.DMA((steps,)),
        ssem=pltpu.SemaphoreType.DMA((len(ORDERS), 2 + grp)),
        rsem=pltpu.SemaphoreType.DMA((len(ORDERS), 2 + grp)),
    )
    tall = inner // seq
    for name in ORDERS:
        rows, cols = share, width
        if name[0] == "O":
            rows, cols = tall, width // OCHUNKS
        elif name[0] == "I":
            cols = 1024
        z_rows = rows // grp
        if name in EARLY:
            scratch[name + "k"] = vm((4, grp, z_rows, cols), BF)
            scratch[name + "r0"] = vm((4, grp, z_rows, cols), BF)
            scratch[name + "r1"] = vm((2, z_rows, cols), BF)
            scratch[name + "r2"] = vm((1, z_rows, cols), BF)
            scratch[name + "z"] = vm((4, z_rows, cols), BF)
            scratch[name + "rz"] = vm((grp - 1, 4, z_rows, cols), BF)
        else:
            if name[0] == "O":
                scratch[name + "k"] = vm((4, rows, cols), BF)
            scratch[name + "r0"] = vm((4, rows, cols), BF)
            scratch[name + "r1"] = vm((2, rows, cols), BF)
            scratch[name + "r2"] = vm((1, rows, cols), BF)
            fold = 1 if z_rows % 16 == 0 else 2
            scratch[name + "z"] = vm((grp, z_rows * fold, cols // fold), BF)
            scratch[name + "rz"] = vm((grp - 1, z_rows * fold, cols // fold), BF)
    names = list(scratch)
    outs = [
        sds((seq, part, width), BF),
        sds((seq, part // 2, width), BF),
        sds((share // grp, inner), F32),
        sds((tall // grp, width), F32),
        sds((share // grp, width), F32),
        sds((share // grp, width), F32),
        sds((share // grp, width), F32),
        sds((share // grp, width), F32),
        sds((small_rows, 128), F32),
    ]
    hbm = pl.BlockSpec(memory_space=pl.ANY)
    vmem = pl.BlockSpec(memory_space=pltpu.VMEM)
    in_vmem = ("g1", "dgain2")
    return pl.pallas_call(
        functools.partial(back_body, names, (seq, grp)),
        out_shape=outs,
        in_specs=[vmem if n in in_vmem else hbm for n in BACK_INPUTS],
        out_specs=[hbm, hbm] + [vmem] * (len(outs) - 2),
        scratch_shapes=list(scratch.values()),
        compiler_params=pltpu.CompilerParams(
            collective_id=1, has_side_effects=True, vmem_limit_bytes=63 << 20
        ),
        cost_estimate=pl.CostEstimate(
            flops=30_000_000_000, bytes_accessed=60_000_000, transcendentals=0
        ),
    )(*[args[n] for n in BACK_INPUTS])


def finish_body(count, *refs):
    srcs, small = refs[:count], refs[count]
    dsts = refs[count + 1 : 2 * count + 1]
    rel, attn, ffn = refs[2 * count + 1 : 2 * count + 4]
    rooms = refs[2 * count + 4 : 3 * count + 4]
    sem = refs[-1]
    loads = [pltpu.make_async_copy(s, r, sem.at[0, i]) for i, (s, r) in enumerate(zip(srcs, rooms))]
    stores = [pltpu.make_async_copy(r, d, sem.at[1, i]) for i, (r, d) in enumerate(zip(rooms, dsts))]
    for copy in loads:
        copy.start()
    pairs = attn.shape[0] // 128
    for i in range(pairs):
        both = small[64 * i : 64 * (i + 1), :]
        rel[2 * i] = both[:, :64]
        rel[2 * i + 1] = both[:, 64:]
        attn[pl.ds(128 * i, 128)] = small[64 * pairs + i, :]
        ffn[pl.ds(128 * i, 128)] = small[65 * pairs + i, :]
    for load, store in zip(loads, stores):
        load.wait()
        store.start()
    for copy in stores:
        copy.wait()


def finish(arrays, small, heads, width):
    count = len(arrays)
    hbm = pl.BlockSpec(memory_space=pltpu.HBM)
    vmem = pl.BlockSpec(memory_space=pltpu.VMEM)
    return pl.pallas_call(
        functools.partial(finish_body, count),
        out_shape=[sds(a.shape, a.dtype) for a in arrays]
        + [sds((heads, 64, 64), F32), sds((width,), F32), sds((width,), F32)],
        in_specs=[hbm] * count + [vmem],
        out_specs=[hbm] * count + [vmem] * 3,
        scratch_shapes=[pltpu.VMEM(a.shape, a.dtype) for a in arrays]
        + [pltpu.SemaphoreType.DMA((2, count))],
        compiler_params=pltpu.CompilerParams(vmem_limit_bytes=63 << 20),
    )(*arrays, small)


def local(
    seq_size, grp_size, hidden, lengths, query_weight, key_weight, value_weight, w_rel,
    output_weight, gain_attn, inner_weight, outer_weight, gain_ffn, cotangent,
):
    micro, unused, seqs, part, width = hidden.shape
    count = micro * seqs
    assert count == seq_size == 8
    weights = dict(
        wq=query_weight, wk=key_weight, wv=value_weight, wo=output_weight, win=inner_weight,
        wout=outer_weight, g1=gain_attn, g2=gain_ffn,
    )
    kept = forward(
        dict(
            weights, hidden=hidden.reshape(count, part, width), w_rel=w_rel,
            lengths=lengths.transpose(1, 2, 0).reshape(seqs, micro),
            cot=cotangent.reshape(count, part // 2, width),
        ),
        seq_size,
        grp_size,
    )
    outer = kept["outer"]
    tall = outer.shape[3]
    split = outer.shape[:3] + (grp_size, tall // grp_size, outer.shape[4])
    kept.update(weights, outer3=outer, outer4=outer.reshape(split), dgain2=kept["dgain"])
    *sums, small = backward(kept, seq_size, grp_size)
    hid, pooled, d_inner, d_outer, d_out, d_query, d_key, d_value, d_rel, d_attn, d_ffn = finish(
        sums, small, w_rel.shape[0], width
    )
    return (
        pooled.reshape(cotangent.shape),
        hid.reshape(hidden.shape),
        d_query,
        d_key,
        d_value,
        d_rel,
        d_out,
        d_attn,
        d_inner,
        d_outer,
        d_ffn,
    )


def solution(mesh):
    rows = P(None, "grp", None, "seq", None)
    spread = P(("seq", "grp"), None)
    sizes = dict(mesh.shape)
    return jax.shard_map(
        functools.partial(local, sizes["seq"], sizes["grp"]),
        mesh=mesh,
        in_specs=(rows, P(None, "grp", None)) + (P(),) * 9 + (rows,),
        out_specs=(
            rows, rows, spread, spread, spread, P(), spread, P(), spread, spread, P()
        ),
        check_vma=False,
    )
```

```python
import functools
import math
import types

import jax
import jax.numpy as jnp
from jax import lax
from jax.experimental import pallas as pl
from jax.experimental.pallas import tpu as pltpu
from jax.sharding import PartitionSpec as P

BF = jnp.bfloat16
F32 = jnp.float32
I32 = jnp.int32
MESH = pl.DeviceIdType.MESH
EPS = 1e-05
FFC = 512
QT = 256
OCHUNKS = 3
EARLY = ("O0", "O2")
ORDERS = {
    "O0": (1, 2, 4), "O1": (1, 4, 2), "O2": (1, 2, 4), "I0": (1, 2, 4), "I1": (1, 2, 4),
    "I2": (1, 2, 4), "W": (1, 4, 2), "G0": (1, 4, 2), "G1": (1, 2, 4), "G2": (1, 4, 2),
    "R": (1, 4, 2),
}


def sds(shape, dtype):
    return jax.ShapeDtypeStruct(shape, dtype)


def mm(a, b):
    return lax.dot_general(a, b, (((1,), (0,)), ((), ())), preferred_element_type=F32)


def mm_nt(a, b):
    return lax.dot_general(a, b, (((1,), (1,)), ((), ())), preferred_element_type=F32)


def mm_tn(a, b):
    return lax.dot_general(a, b, (((0,), (0,)), ((), ())), preferred_element_type=F32)


def rel_of(pos, order):
    bits = len(order)
    rel = 0
    for i, mask in enumerate(order):
        if (pos >> (bits - 1 - i)) & 1:
            rel |= mask
    return rel


def loop(count, body):
    def step(i, carry):
        body(i)
        return carry

    lax.fori_loop(0, count, step, 0)


def masks_of(size):
    return [1 << i for i in range(size.bit_length() - 1)]


def xor(rank, rel, size):
    total = 0
    for mask in masks_of(size):
        a = lax.rem(lax.div(rank, mask), 2)
        if isinstance(rel, int):
            total = total + mask * ((1 - a) if rel & mask else a)
        else:
            b = lax.rem(lax.div(rel, mask), 2)
            total = total + mask * (a + b - 2 * a * b)
    return total


def wide(value):
    return value.astype(F32)


def pool_matrix(rows):
    row = lax.broadcasted_iota(I32, (rows, 2 * rows), 0)
    col = lax.broadcasted_iota(I32, (rows, 2 * rows), 1)
    return jnp.where((col == 2 * row) | (col == 2 * row + 1), 0.5, 0.0).astype(BF)


def norm_parts(rows):
    centered = rows - jnp.mean(rows, -1, keepdims=True)
    rstd = lax.rsqrt(jnp.mean(centered * centered, -1, keepdims=True) + EPS)
    return centered * rstd, rstd


def norm_back(grad, unit, rstd, gain):
    scaled = grad * gain
    return rstd * (
        scaled
        - jnp.mean(scaled, -1, keepdims=True)
        - unit * jnp.mean(scaled * unit, -1, keepdims=True)
    )


FORE_INPUTS = list(
    dict(hidden=0, cot=0, lengths=0, wq=0, wk=0, wv=0, w_rel=0, wo=0, win=0, wout=0, g1=0, g2=0)
)
FORE_OUTPUTS = list(
    dict(
        attn=0, linv=0, p=0, q=0, k=0, v=0, xt=0, pt=0, bd=0, cos=0, sin=0, feat=0, rows=0,
        slope=0, gouter=0, gtwo=0, unit=0, rstd=0, mixed=0, outer=0, dgain=0,
    )
)


def fore_body(names, sizes, *refs):
    ref = types.SimpleNamespace(**dict(zip(FORE_INPUTS + FORE_OUTPUTS + names, refs)))
    seq, grp = sizes
    me = lax.axis_index("seq")
    half, width = ref.vq.shape
    slot = 2 * half
    part = slot // seq
    inner = ref.wout.shape[0]
    pairs = width // 128
    groups = width // 256
    steps = inner // FFC
    chips = seq // 2
    chip, core = lax.div(me, 2), lax.rem(me, 2)

    early = [(ref.wk, ref.vwk), (ref.wv, ref.vwv), (ref.wq, ref.vwq), (ref.w_rel, ref.vrel)]
    loads = [
        pltpu.make_async_copy(src, dst, ref.lsem.at[i])
        for i, (src, dst) in enumerate(early + [(ref.wo, ref.vwo)])
    ]

    def weights(j, buf):
        cols = pl.ds(pl.multiple_of(j * FFC, FFC), FFC)
        return [
            pltpu.make_async_copy(ref.win.at[:, cols], ref.vwin.at[buf], ref.wsem.at[0, buf]),
            pltpu.make_async_copy(ref.wout.at[cols, :], ref.vwout.at[buf], ref.wsem.at[1, buf]),
        ]

    stores = []

    def store(src, dst):
        copy = pltpu.make_async_copy(src, dst, ref.ssem.at[len(stores)])
        copy.start()
        stores.append(copy)

    def rows_of(rank, size):
        return pl.ds(pl.multiple_of(rank * size, size), size)

    def blocks(src, dst, size, bank, rel):
        copies = []
        for c in range(2):
            rank = 2 * xor(chip, rel, chips) + c
            copies.append(
                pltpu.make_async_remote_copy(
                    src_ref=src.at[rank],
                    dst_ref=dst.at[rows_of(me, size)],
                    send_sem=ref.asend.at[bank, 2 * rel + c],
                    recv_sem=ref.arecv.at[bank, 2 * rel + core],
                    device_id={"seq": rank},
                    device_id_type=MESH,
                )
            )
        return copies

    def arrivals(src, dst, size, bank, rel):
        copies = []
        for c in range(2):
            rank = 2 * xor(chip, rel, chips) + c
            copies.append(
                pltpu.make_async_remote_copy(
                    src_ref=src.at[rank],
                    dst_ref=dst.at[rows_of(rank, size)],
                    send_sem=ref.asend.at[bank, 2 * rel + c],
                    recv_sem=ref.arecv.at[bank, 2 * rel + c],
                    device_id={"seq": rank},
                    device_id_type=MESH,
                )
            )
        return copies

    def mate(src, dst, size, bank, receive):
        rank = 2 * chip + 1 - core
        spot = rank if receive else me
        return pltpu.make_async_remote_copy(
            src_ref=src.at[rank],
            dst_ref=dst.at[rows_of(spot, size)],
            send_sem=ref.asend.at[bank, 0],
            recv_sem=ref.arecv.at[bank, 0],
            device_id={"seq": rank},
            device_id_type=MESH,
        )

    hid = (ref.hidden, ref.vx, part, 0)
    cot = (ref.cot, ref.vcot, part // 2, 1)
    own = [
        pltpu.make_async_copy(src.at[me], dst.at[rows_of(me, size)], ref.osem.at[bank])
        for src, dst, size, bank in (hid, cot)
    ]

    barrier = pltpu.get_barrier_semaphore()
    for k in range(1, seq):
        pl.semaphore_signal(
            barrier, inc=1, device_id={"seq": lax.rem(me + k, seq)}, device_id_type=MESH
        )
    own[0].start()
    for copy in loads[:4]:
        copy.start()
    pl.semaphore_wait(barrier, seq - 1)
    mate(*hid, False).start()
    near, far = list(range(1, chips - 1)), [chips - 1]
    for rel in near:
        for copy in blocks(*hid, rel):
            copy.start()

    lane_row = lax.broadcasted_iota(I32, (1, 128), 1)
    freq = wide(lax.rem(lane_row, 32))
    rate = jnp.exp(freq * (-math.log(10000.0) / 32))
    pos = wide(lax.broadcasted_iota(I32, (half, 1), 0))
    turn = (2.0 * pos) * rate
    ref.vcos[...] = jnp.cos(turn)
    ref.vsin[...] = jnp.sin(turn)
    first_half = lax.rem(lane_row, 64) < 32
    for t in range(2):
        angle = (pos + float(half * t)) * rate
        ref.vfeat[half * t : half * (t + 1), :] = jnp.where(
            first_half, jnp.sin(angle), jnp.cos(angle)
        ).astype(BF)
    store(ref.vcos, ref.cos)
    store(ref.vsin, ref.sin)
    store(ref.vfeat, ref.feat)
    for copy in loads[:4]:
        copy.wait()
    ref.vbd[...] = jnp.zeros_like(ref.vbd)
    for h in range(2 * pairs):
        ref.vbd[h // 4, 64 * (h % 4) : 64 * (h % 4) + 64, 64 * (h % 4) : 64 * (h % 4) + 64] = (
            ref.vrel[h]
        )
    store(ref.vbd, ref.bd)

    pool = pool_matrix(part)

    def project(index):
        rows = rows_of(index, 2 * part)
        small = rows_of(index, part)
        tile = ref.vx[rows, :]
        ref.vk[rows, :] = mm(tile, ref.vwk[...]).astype(BF)
        ref.vv[rows, :] = mm(tile, ref.vwv[...]).astype(BF)
        pooled = mm(pool, tile)
        ref.vpool[small, :] = pooled
        short = pooled.astype(BF)
        ref.vq[small, :] = mm(short, ref.vwq[...]).astype(BF)
        ref.vxt[:, rows] = tile.T
        ref.vpt[:, small] = short.T

    mate(*hid, True).wait_recv()
    own[0].wait()
    project(chip)
    for rel in near:
        for copy in arrivals(*hid, rel):
            copy.wait_recv()
    for rel in far:
        for copy in blocks(*hid, rel):
            copy.start()
    for rel in near:
        project(xor(chip, rel, chips))
    for rel in far:
        for copy in arrivals(*hid, rel):
            copy.wait_recv()
    own[1].start()
    mate(*cot, False).start()
    for rel in near + far:
        for copy in blocks(*cot, rel):
            copy.start()
    for rel in far:
        project(xor(chip, rel, chips))
    store(ref.vk, ref.k)
    store(ref.vv, ref.v)
    store(ref.vq, ref.q)
    store(ref.vxt, ref.xt)
    store(ref.vpt, ref.pt)
    loads[4].start()
    for copy in weights(0, 0):
        copy.start()

    scale = 0.125 * 1.4426950408889634
    low = lax.rem(lane_row, 64) < 32
    first_head = lane_row < 64
    seqs, micro = ref.lengths.shape
    mine_row = lax.broadcasted_iota(I32, (seqs, micro), 0) == lax.rem(me, seqs)
    mine_col = lax.broadcasted_iota(I32, (seqs, micro), 1) == lax.div(me, seqs)
    limit = jnp.where(mine_row & mine_col, wide(ref.lengths[...]), 0.0)
    limit = jnp.sum(jnp.sum(limit, 1, keepdims=True), 0, keepdims=True)
    key_ok = wide(lax.broadcasted_iota(I32, (1, slot), 1)) < limit
    ones = jnp.ones((slot, 128), BF)

    def probs(i, buf):
        return pltpu.make_async_copy(
            ref.vp.at[buf], ref.p.at[pl.ds(2 * i, 2)], ref.wsem.at[2, buf]
        )

    def attention_step(i):
        buf = lax.rem(i, 2)

        @pl.when(i >= 2)
        def free():
            probs(i - 2, buf).wait()

        cols = pl.ds(pl.multiple_of(i * 128, 128), 128)
        part_bd = pl.ds(pl.multiple_of(buf * 128, 128), 128)
        rel = mm(ref.vq[:, cols], ref.vbd[lax.div(i, 2), part_bd, part_bd])
        other = jnp.where(low, pltpu.roll(rel, 96, 1), -pltpu.roll(rel, 32, 1))
        ref.vsh[...] = (rel * ref.vcos[...] + other * ref.vsin[...]).astype(BF)
        key_side = jnp.concatenate([ref.vk[:, cols], ref.vfeat[...]], 1)
        value_side = jnp.concatenate([ref.vv[:, cols], ones], 1)
        for t in range(half // QT):
            rows = slice(QT * t, QT * (t + 1))
            q_part = ref.vq[rows, cols]
            s_part = ref.vsh[rows, :]
            outs = []
            for h in range(2):
                mine = first_head if h == 0 else jnp.logical_not(first_head)
                zero = jnp.zeros_like(q_part)
                left = jnp.concatenate(
                    [jnp.where(mine, q_part, zero), jnp.where(mine, s_part, zero)], 1
                )
                s = jnp.where(key_ok, mm_nt(left, key_side), -1e30)
                top = jnp.max(s, -1, keepdims=True)
                p = jnp.exp2((s - top) * scale).astype(BF)
                ref.vp[buf, h, rows, :] = p
                acc = mm(p, value_side)
                inv = 1.0 / acc[:, 128:]
                outs.append((acc[:, :128] * inv, inv))
            ref.vattn[rows, cols] = jnp.where(first_head, outs[0][0], outs[1][0]).astype(BF)
            ref.vlinv[rows, cols] = jnp.where(first_head, outs[0][1], outs[1][1])
        probs(i, buf).start()

    loop(pairs, attention_step)
    store(ref.vattn, ref.attn)
    store(ref.vlinv, ref.linv)

    loads[4].wait()
    unit, rstd = norm_parts(ref.vpool[...] + mm(ref.vattn[...], ref.vwo[...]))
    mixed = unit * wide(ref.g1[...]).reshape(1, width)
    ref.vunit[...] = unit
    ref.vrstd[...] = jnp.broadcast_to(rstd, ref.vrstd.shape)
    ref.vacc[...] = mixed
    short = mixed.astype(BF)
    ref.vmix[...] = short
    ref.vmt[...] = short.T
    store(ref.vunit, ref.unit)
    store(ref.vrstd, ref.rstd)
    store(ref.vmt, ref.mixed)

    def slopes(j, buf):
        cols = pl.ds(pl.multiple_of(j * FFC, FFC), FFC)
        return pltpu.make_async_copy(
            ref.vslope.at[buf], ref.slope.at[:, cols], ref.wsem.at[3, buf]
        )

    def feed_step(j):
        buf = lax.rem(j, 2)
        for copy in weights(j, buf):
            copy.wait()

        @pl.when(j + 1 < steps)
        def more():
            for copy in weights(j + 1, 1 - buf):
                copy.start()

        @pl.when(j >= 2)
        def free():
            slopes(j - 2, buf).wait()

        pre = mm(ref.vmix[...], ref.vwin[buf])
        cdf = 0.5 * (1.0 + lax.erf(pre * 0.7071067811865476))
        act = (pre * cdf).astype(BF)
        ref.vslope[buf] = (
            cdf + pre * (jnp.exp(pre * pre * -0.5) * 0.3989422804014327)
        ).astype(BF)
        ref.vacc[...] += mm(act, ref.vwout[buf])
        ref.vactt[pl.ds(pl.multiple_of(j * FFC, FFC), FFC), :] = act.T
        slopes(j, buf).start()

    loop(steps, feed_step)
    mate(*cot, True).wait_recv()
    own[1].wait()
    for rel in near + far:
        for copy in arrivals(*cot, rel):
            copy.wait_recv()
    unit, rstd = norm_parts(ref.vacc[...])
    valid = wide(2 * lax.broadcasted_iota(I32, (half, 1), 0)) < limit
    g2 = wide(ref.g2[...]).reshape(1, width)
    ref.vrows[...] = jnp.where(valid, unit * g2, 0.0).astype(BF)
    store(ref.vrows, ref.rows)
    grad = jnp.where(valid, wide(ref.vcot[...]), 0.0)
    ref.dgain[...] = jnp.sum(grad * unit, 0, keepdims=True)
    two = norm_back(grad, unit, rstd, g2)
    ref.vacc[...] = two
    ref.vgo[...] = two.astype(BF)
    store(ref.vacc, ref.gtwo)
    store(ref.vgo, ref.gouter)

    tall = inner // seq
    count = ref.outer.shape[1]
    span = width // count

    def outer_step(pos):
        bits = [lax.div(pos, 4), lax.rem(lax.div(pos, 2), 2), lax.rem(pos, 2)]
        rel = bits[0] + 2 * bits[1] + 4 * bits[2]
        value = mm(ref.vactt[rows_of(xor(me, rel, seq), tall), :], ref.vgo[...]).astype(BF)
        for n in range(count):
            order = ORDERS["O" + str(n)]
            spot = 2 * bits[1] + bits[2] if order[1] == 2 else 2 * bits[2] + bits[1]
            ref.vouter[bits[0], n, spot] = value[:, span * n : span * (n + 1)]

    loop(seq, outer_step)
    store(ref.vouter, ref.outer)
    for i in (pairs - 2, pairs - 1):
        probs(i, i % 2).wait()
    for j in (steps - 2, steps - 1):
        slopes(j, j % 2).wait()
    for copy in stores:
        copy.wait()
    for bank in (hid, cot):
        mate(*bank, False).wait_send()
        for rel in near + far:
            for copy in blocks(*bank, rel):
                copy.wait_send()


def forward(args, seq, grp):
    count, part, width = args["hidden"].shape
    slot = part * seq
    half = slot // 2
    inner = args["wout"].shape[0]
    heads = width // 64
    outer = (2, OCHUNKS, 4, inner // seq, width // OCHUNKS)
    vm = pltpu.VMEM
    scratch = dict(
        vx=vm((slot, width), BF),
        vcot=vm((half, width), BF),
        vwq=vm((width, width), BF),
        vwk=vm((width, width), BF),
        vwv=vm((width, width), BF),
        vrel=vm((heads, 64, 64), BF),
        vwo=vm((width, width), BF),
        vwin=vm((2, width, FFC), BF),
        vwout=vm((2, FFC, width), BF),
        vcos=vm((half, 128), F32),
        vsin=vm((half, 128), F32),
        vfeat=vm((slot, 128), BF),
        vbd=vm((width // 256, 256, 256), BF),
        vq=vm((half, width), BF),
        vk=vm((slot, width), BF),
        vv=vm((slot, width), BF),
        vpool=vm((half, width), F32),
        vxt=vm((width, slot), BF),
        vpt=vm((width, half), BF),
        vsh=vm((half, 128), BF),
        vp=vm((2, 2, half, slot), BF),
        vattn=vm((half, width), BF),
        vlinv=vm((half, width), F32),
        vunit=vm((half, width), F32),
        vrstd=vm((half, 128), F32),
        vacc=vm((half, width), F32),
        vmix=vm((half, width), BF),
        vmt=vm((width, half), BF),
        vslope=vm((2, half, FFC), BF),
        vactt=vm((inner, half), BF),
        vrows=vm((half, width), BF),
        vgo=vm((half, width), BF),
        vouter=vm(outer, BF),
        lsem=pltpu.SemaphoreType.DMA((5,)),
        wsem=pltpu.SemaphoreType.DMA((4, 2)),
        ssem=pltpu.SemaphoreType.DMA((24,)),
        osem=pltpu.SemaphoreType.DMA((2,)),
        asend=pltpu.SemaphoreType.DMA((2, seq)),
        arecv=pltpu.SemaphoreType.DMA((2, seq)),
    )
    names = list(scratch)
    shapes = dict(
        attn=sds((half, width), BF),
        linv=sds((half, width), F32),
        p=sds((heads, half, slot), BF),
        q=sds((half, width), BF),
        k=sds((slot, width), BF),
        v=sds((slot, width), BF),
        xt=sds((width, slot), BF),
        pt=sds((width, half), BF),
        bd=sds((width // 256, 256, 256), BF),
        cos=sds((half, 128), F32),
        sin=sds((half, 128), F32),
        feat=sds((slot, 128), BF),
        rows=sds((half, width), BF),
        slope=sds((half, inner), BF),
        gouter=sds((half, width), BF),
        gtwo=sds((half, width), F32),
        unit=sds((half, width), F32),
        rstd=sds((half, 128), F32),
        mixed=sds((width, half), BF),
        outer=sds(outer, BF),
        dgain=sds((1, width), F32),
    )
    hbm = pl.BlockSpec(memory_space=pl.ANY)
    vmem = pl.BlockSpec(memory_space=pltpu.VMEM)
    spots = dict(g1=vmem, g2=vmem, lengths=vmem)
    outs = pl.pallas_call(
        functools.partial(fore_body, names, (seq, grp)),
        out_shape=[shapes[n] for n in FORE_OUTPUTS],
        in_specs=[spots.get(n, hbm) for n in FORE_INPUTS],
        out_specs=[hbm] * (len(FORE_OUTPUTS) - 1) + [vmem],
        scratch_shapes=list(scratch.values()),
        compiler_params=pltpu.CompilerParams(
            collective_id=0, has_side_effects=True, vmem_limit_bytes=63 << 20
        ),
        cost_estimate=pl.CostEstimate(
            flops=20_000_000_000, bytes_accessed=60_000_000, transcendentals=0
        ),
    )(*[args[n] for n in FORE_INPUTS])
    return dict(zip(FORE_OUTPUTS, outs))


class Chunk:
    def __init__(self, env, index, order, early, keep, send, recv, zbuf, recvz, out):
        self.env, self.index, self.order, self.early = env, index, order, early
        self.keep, self.send, self.recv = keep, send, recv
        self.zbuf, self.recvz, self.out = zbuf, recvz, out

    def remote(self, slot, src, dst, device):
        return pltpu.make_async_remote_copy(
            src_ref=src,
            dst_ref=dst,
            send_sem=self.env.ssem.at[self.index, slot],
            recv_sem=self.env.rsem.at[self.index, slot],
            device_id=device,
            device_id_type=MESH,
        )

    def seq_copy(self, stage):
        device = {"seq": xor(self.env.me, self.order[stage], self.env.seq)}
        if stage == 0:
            src = self.send
        else:
            half = 4 >> stage
            src = (self.zbuf if self.early else self.recv[0]).at[pl.ds(half, half)]
        return self.remote(stage, src, self.recv[stage], device)

    def z_copies(self):
        grp, z = self.env.grp, self.env.z
        copies = []
        for d in range(1, grp):
            peer = lax.rem(z + d, grp)
            src = self.recv[0].at[:, peer] if self.early else self.zbuf.at[peer]
            copies.append(self.remote(2 + d, src, self.recvz.at[d - 1], {"grp": peer}))
        return copies

    def unit(self):
        return 48 if self.keep.shape[1] % 48 == 0 else 64

    def step(self, n):
        keep, (recv0, recv1, recv2) = self.keep, self.recv
        zbuf, recvz, grp, z = self.zbuf, self.recvz, self.env.grp, self.env.z
        if n == 0:
            self.seq_copy(0).start()
        elif n == 1 and self.early:
            self.seq_copy(0).wait()

            def add(i):
                p, g = lax.div(i, grp), lax.rem(i, grp)
                recv0[p, g] = (wide(keep[p, g]) + wide(recv0[p, g])).astype(BF)

            loop(4 * grp, add)
            for copy in self.z_copies():
                copy.start()
        elif n == 2 and self.early:
            for copy in self.z_copies():
                copy.wait()

            def add(p):
                total = wide(recv0[p, z])
                for d in range(grp - 1):
                    total = total + wide(recvz[d, p])
                zbuf[p] = total.astype(BF)

            loop(4, add)
            self.seq_copy(1).start()
        elif n == 3 and self.early:
            self.seq_copy(1).wait()
            zbuf[1] = (wide(zbuf[1]) + wide(recv1[1])).astype(BF)
            self.seq_copy(2).start()
        elif n == 4 and self.early:
            self.seq_copy(2).wait()
            self.out(wide(zbuf[0]) + wide(recv1[0]) + wide(recv2[0]))
        elif n == 1:
            self.seq_copy(0).wait()
            unit = self.unit()
            parts = keep.shape[1] // unit

            def add(i):
                start = pl.multiple_of(unit * lax.rem(i, parts), unit)
                p, rows = 2 + lax.div(i, parts), pl.ds(start, unit)
                recv0[p, rows] = (wide(keep[p, rows]) + wide(recv0[p, rows])).astype(BF)

            loop(2 * parts, add)
            self.seq_copy(1).start()
        elif n == 2:
            self.seq_copy(1).wait()

            unit = self.unit()

            def add(i):
                rows = pl.ds(pl.multiple_of(unit * i, unit), unit)
                recv0[1, rows] = (
                    wide(keep[1, rows]) + wide(recv0[1, rows]) + wide(recv1[1, rows])
                ).astype(BF)

            loop(keep.shape[1] // unit, add)
            self.seq_copy(2).start()
        elif n == 3:
            self.seq_copy(2).wait()
            share = keep.shape[1] // grp
            unit = self.unit()
            for start in range(0, keep.shape[1], unit):
                rows = slice(start, start + unit)
                total = (
                    wide(keep[0, rows]) + wide(recv0[0, rows])
                    + wide(recv1[0, rows]) + wide(recv2[0, rows])
                )
                size = min(share, unit)
                for low in range(start, start + unit, size):
                    g, inside = low // share, low % share
                    piece = total[low - start : low - start + size].astype(BF)
                    if zbuf.shape[1] == share:
                        zbuf[g, inside : inside + size] = piece
                    else:
                        mid = zbuf.shape[2]
                        zbuf[g, :share] = piece[:, :mid]
                        zbuf[g, share:] = piece[:, mid:]
            for copy in self.z_copies():
                copy.start()
        else:
            for copy in self.z_copies():
                copy.wait()
            total = wide(zbuf[z])
            for d in range(grp - 1):
                total = total + wide(recvz[d])
            share = keep.shape[1] // grp
            if zbuf.shape[1] != share:
                total = jnp.concatenate([total[:share], total[share:]], 1)
            self.out(total)


BACK_INPUTS = list(
    dict(
        gouter=0, slope=0, wout=0, win=0, mixed=0, gtwo=0, unit=0, rstd=0, g1=0, wo=0, attn=0,
        p=0, q=0, k=0, v=0, linv=0, xt=0, pt=0, bd=0, cos=0, sin=0, feat=0, wq=0, wk=0, wv=0,
        outer3=0, outer4=0, rows=0, dgain2=0,
    )
)
BACK_OUTPUTS = list(
    dict(hidden=0, pooled=0, inner=0, outer=0, out=0, query=0, key=0, value=0, small=0)
)
POINTS = {
    ("X", 0): [("P", 0)],
    ("B", 1): [("O1", 1), ("I0", 0)],
    ("B", 2): [("I0", 1), ("O0", 1)],
    ("B", 3): [("I1", 0)],
    ("B", 5): [("I1", 1), ("I2", 0)],
    ("L", 0): [("W", 0), ("I2", 1), ("I0", 2)],
    ("U", 0): [("O2", 1), ("W", 1)],
    ("U", 1): [("G0", 0), ("I1", 2)],
    ("U", 2): [("O1", 2), ("G0", 1), ("O0", 2)],
    ("U", 3): [("G1", 0)],
    ("U", 4): [("G1", 1), ("I2", 2)],
    ("U", 5): [
        ("I0", 3), ("R", 0), ("G2", 0), ("O2", 2), ("R", 1), ("P", 1), ("G0", 2), ("G2", 1),
        ("I2", 3), ("G1", 2), ("R", 2), ("O0", 3), ("W", 2), ("O1", 3),
    ],
    ("T", 0): [
        ("G2", 2), ("R", 3), ("G0", 3), ("H", 0), ("G1", 3), ("I1", 3), ("R", 4), ("W", 3),
        ("I0", 4), ("A", 0), ("O1", 4), ("O0", 4), ("O2", 3), ("G1", 4), ("I2", 4), ("G2", 3),
        ("I1", 4), ("A", 1), ("G0", 4), ("W", 4), ("G2", 4), ("O2", 4), ("H", 1), ("A", 2),
    ],
}


def back_body(names, sizes, *refs):
    every = dict(zip(BACK_INPUTS + BACK_OUTPUTS + names, refs))
    ref = types.SimpleNamespace(**every)
    seq, grp = sizes
    me = lax.axis_index("seq")
    z = lax.axis_index("grp")
    env = types.SimpleNamespace(me=me, z=z, seq=seq, grp=grp, ssem=ref.ssem, rsem=ref.rsem)
    half, width = ref.vgo.shape
    slot = 2 * half
    inner = ref.slope.shape[1]
    steps = inner // FFC
    pairs = width // 128
    groups = width // 256
    lsem = ref.lsem

    plain = [
        (ref.gouter, ref.vgo), (ref.mixed, ref.vmt), (ref.gtwo, ref.vacc),
        (ref.unit, ref.vun), (ref.rstd, ref.vrs), (ref.wo, ref.vwo), (ref.attn, ref.vat),
        (ref.linv, ref.vlinv),
        (ref.q, ref.vq), (ref.k, ref.vk), (ref.v, ref.vv), (ref.feat, ref.vfeat),
        (ref.cos, ref.vcos), (ref.sin, ref.vsin), (ref.bd, ref.vbd), (ref.xt, ref.vxt),
        (ref.wq, ref.vwq), (ref.wk, ref.vwk), (ref.wv, ref.vwv), (ref.pt, ref.vmt),
    ]
    local = [pltpu.make_async_copy(*pair, lsem.at[i]) for i, pair in enumerate(plain)]
    base = len(plain)

    def weights(j, buf):
        cols = pl.ds(pl.multiple_of(j * FFC, FFC), FFC)
        return [
            pltpu.make_async_copy(ref.slope.at[:, cols], ref.vslope.at[buf], ref.wsem.at[0, buf]),
            pltpu.make_async_copy(ref.wout.at[cols, :], ref.vwout.at[buf], ref.wsem.at[1, buf]),
            pltpu.make_async_copy(ref.win.at[:, cols], ref.vwin.at[buf], ref.wsem.at[2, buf]),
        ]

    def probs(i, buf):
        return pltpu.make_async_copy(
            ref.p.at[pl.ds(2 * i, 2)], ref.vp.at[buf], ref.wsem.at[3, buf]
        )

    chunks = {}
    def out_cols(name, start, stop):
        def put(value):
            every[name][:, start:stop] = value

        return put

    def out_three(g):
        def put(value):
            for i, name in enumerate(("query", "key", "value")):
                every[name][:, 256 * g : 256 * (g + 1)] = value[:, 256 * i : 256 * (i + 1)]

        return put

    def out_small(value):
        ref.vres[...] = value

    kept = []
    for index, (name, order) in enumerate(ORDERS.items()):
        early = name in EARLY
        kind = name[0]
        n = int(name[1]) if len(name) > 1 else 0
        recv = [every[name + "r0"], every[name + "r1"], every[name + "r2"]]
        if kind == "O":
            side = ref.outer4 if early else ref.outer3
            keep, send = every[name + "k"], side.at[1, n]
            kept.append(pltpu.make_async_copy(side.at[0, n], keep, lsem.at[base + n]))
            span = width // OCHUNKS
            out = out_cols("outer", span * n, span * (n + 1))
        elif kind == "I":
            keep, send = ref.ikeep.at[n], ref.isend.at[n]
            out = out_cols("inner", 1024 * n, 1024 * (n + 1))
        elif kind == "W":
            keep, send = ref.wkeep, ref.wsend
            out = out_cols("out", 0, width)
        elif kind == "R":
            keep, send = ref.rkeep, ref.rsend
            out = out_small
        else:
            keep, send = ref.gkeep.at[n], ref.gsend.at[n]
            out = out_three(n)
        chunks[name] = Chunk(
            env, index, order, early, keep, send, recv, every[name + "z"], every[name + "rz"], out
        )

    def spread(src, dst, sem):
        size = dst.shape[1]
        block = lambda b: src.at[pl.ds(pl.multiple_of(b * size, size), size)]
        copies = [pltpu.make_async_copy(block(me), dst.at[me], ref.dsem.at[sem])]
        for k in range(1, seq):
            peer = lax.rem(me + k, seq)
            copies.append(
                pltpu.make_async_remote_copy(
                    src_ref=block(peer),
                    dst_ref=dst.at[me],
                    send_sem=ref.asend.at[sem, k],
                    recv_sem=ref.arecv.at[sem, k],
                    device_id={"seq": peer},
                    device_id_type=MESH,
                )
            )
        return copies

    def gather(stage):
        copies = []
        if stage == 0:
            pairs_of = [(lax.rem(z + k, grp), "grp", grp, z) for k in range(1, grp)]
            src, dst = ref.vres, ref.vag.at[z]
        else:
            pairs_of = [(lax.rem(me + k, seq), "seq", seq, me) for k in range(1, seq)]
            src, dst = ref.vag, ref.vall.at[me]
        for k, (peer, axis, size, rank) in enumerate(pairs_of):
            copies.append(
                pltpu.make_async_remote_copy(
                    src_ref=src,
                    dst_ref=dst,
                    send_sem=ref.msend.at[stage, k],
                    recv_sem=ref.mrecv.at[stage, k],
                    device_id={axis: peer},
                    device_id_type=MESH,
                )
            )
        return copies

    def gather_step(n):
        if n > 0:
            for copy in gather(n - 1):
                copy.wait()
        if n == 0:
            ref.vag[z] = ref.vres[...]
        elif n == 1:
            ref.vall[me] = ref.vag[...]
        if n < 2:
            for copy in gather(n):
                copy.start()
        else:
            ref.small[...] = ref.vall[...].reshape(ref.small.shape)

    def place_small():
        size = ref.vsm.shape[0] // seq
        for pos in range(seq):
            block = ref.vsm[pl.ds(pl.multiple_of(xor(me, rel_of(pos, ORDERS["R"]), seq) * size, size), size), :]
            (ref.rkeep if pos < seq // 2 else ref.rsend)[pos % (seq // 2)] = block.astype(BF)

    def event(name, n):
        if name in ("H", "P"):
            places = (ref.vk, ref.hidden, 1) if name == "H" else (ref.rows, ref.pooled, 0)
            for copy in spread(*places):
                copy.start() if n == 0 else copy.wait()
        elif name == "A":
            gather_step(n)
        else:
            if name == "R" and n == 0:
                place_small()
            chunks[name].step(n)

    def point(kind, index, dynamic=None):
        todo = POINTS.get((kind, index), [])
        if not todo:
            return
        if dynamic is None:
            for name, n in todo:
                event(name, n)
        else:

            @pl.when(dynamic == index)
            def run():
                for name, n in todo:
                    event(name, n)

    barrier = pltpu.get_barrier_semaphore()
    for k in range(1, seq):
        pl.semaphore_signal(
            barrier, inc=1, device_id={"seq": lax.rem(me + k, seq)}, device_id_type=MESH
        )
    for k in range(1, grp):
        pl.semaphore_signal(
            barrier, inc=1, device_id={"grp": lax.rem(z + k, grp)}, device_id_type=MESH
        )
    for copy in local[:3]:
        copy.start()
    for copy in weights(0, 0):
        copy.start()
    pl.semaphore_wait(barrier, seq + grp - 2)
    for n in range(OCHUNKS):
        chunks["O" + str(n)].step(0)
    for copy in kept:
        copy.start()
    point("X", 0)
    for copy in local[:3]:
        copy.wait()

    def rows_of(count, rel):
        step = width // seq
        return pl.ds(pl.multiple_of(xor(me, rel, seq) * step, step), step)

    def split(order, cols, keep, send):
        for pos in range(seq):
            block = ref.vval[rows_of(width, rel_of(pos, order)), cols]
            (keep if pos < seq // 2 else send)(pos % (seq // 2), block)

    def feed_step(j):
        buf = lax.rem(j, 2)
        for copy in weights(j, buf):
            copy.wait()

        @pl.when(j + 1 < steps)
        def more():
            for copy in weights(j + 1, 1 - buf):
                copy.start()

        @pl.when(j == 1)
        def rest():
            for copy in local[3:-1]:
                copy.start()
            probs(0, 0).start()
            for copy in kept:
                copy.wait()

        grad = mm_nt(ref.vgo[...], ref.vwout[buf])
        hid = (wide(ref.vslope[buf]) * grad).astype(BF)
        ref.vacc[...] += mm_nt(hid, ref.vwin[buf])
        ref.vval[:, :FFC] = mm(ref.vmt[...], hid).astype(BF)
        c = lax.div(j, 2)
        cols = pl.ds(pl.multiple_of(lax.rem(j, 2) * FFC, FFC), FFC)

        def keep(pos, block):
            ref.ikeep[c, pos, :, cols] = block

        def send(pos, block):
            ref.isend[c, pos, :, cols] = block

        for n in range(steps // 2):

            @pl.when(c == n)
            def place():
                split(ORDERS["I" + str(n)], slice(0, FFC), keep, send)

        for t in range(steps):
            point("B", t, j)

    loop(steps, feed_step)

    local[-1].start()
    for copy in local[3:8]:
        copy.wait()
    grad = ref.vacc[...]
    unit = ref.vun[...]
    small = ref.vsm
    dgain = jnp.sum(grad * unit, 0, keepdims=True)
    for i in range(pairs):
        small[64 * pairs + i, :] = dgain[0, 128 * i : 128 * (i + 1)]
        small[64 * pairs + pairs + i, :] = ref.dgain2[0, 128 * i : 128 * (i + 1)]
    used = 66 * pairs
    small[used:, :] = jnp.zeros((small.shape[0] - used, 128), F32)
    one = norm_back(grad, unit, ref.vrs[:, :1], wide(ref.g1[...]).reshape(1, width))
    ref.vun[...] = one
    branch = one.astype(BF)
    attn = ref.vat[...]
    ref.vval[...] = mm_tn(attn, branch).astype(BF)

    def keep_w(pos, block):
        ref.wkeep[pos] = block

    def send_w(pos, block):
        ref.wsend[pos] = block

    split(ORDERS["W"], slice(0, width), keep_w, send_w)
    scaled = mm_nt(branch, ref.vwo[...]) * ref.vlinv[...]
    ref.vgo[...] = scaled.astype(BF)
    ref.vacc[...] = scaled * wide(attn)
    for copy in local[8:]:
        copy.wait()
    point("L", 0)

    lane = lax.broadcasted_iota(I32, (1, 128), 1)
    low = lax.rem(lane, 64) < 32
    first_head = lane < 64
    ones = jnp.broadcast_to(jnp.where(lane < 2, 1.0, 0.0).astype(BF), (slot, 128))

    def attention_step(i):
        buf = lax.rem(i, 2)
        g = lax.div(i, 2)
        probs(i, buf).wait()

        @pl.when(i + 1 < pairs)
        def more():
            probs(i + 1, 1 - buf).start()

        cols = pl.ds(pl.multiple_of(i * 128, 128), 128)
        part = pl.ds(pl.multiple_of(buf * 128, 128), 128)
        ref.vqt[...] = ref.vq[:, cols].T
        ref.vgt[...] = ref.vgo[:, cols].T
        key_side = jnp.concatenate([ref.vk[:, cols], ref.vfeat[...]], 1)
        value_side = jnp.concatenate([ref.vv[:, cols], ones], 1)
        outs = [[], []]
        for h in range(2):
            mine = first_head if h == 0 else jnp.logical_not(first_head)
            for t in range(half // QT):
                rows = slice(QT * t, QT * (t + 1))
                g_part = ref.vgo[rows, cols]
                delta = jnp.sum(jnp.where(mine, ref.vacc[rows, cols], 0.0), -1, keepdims=True)
                coarse = wide(delta.astype(BF))
                tail = jnp.where(lane == 0, coarse, jnp.where(lane == 1, delta - coarse, 0.0))
                left = jnp.concatenate(
                    [jnp.where(mine, g_part, jnp.zeros_like(g_part)), (-tail).astype(BF)], 1
                )
                ds = (wide(ref.vp[buf, h, rows, :]) * mm_nt(left, value_side)).astype(BF)
                ref.vds[rows, :] = ds
                outs[h].append(mm(ds, key_side))
            lines = slice(64 * h, 64 * (h + 1))
            ref.vkt[lines, :] = (mm(ref.vqt[lines, :], ref.vds[...]) * 0.125).astype(BF)
            ref.vvt[lines, :] = mm(ref.vgt[lines, :], ref.vp[buf, h]).astype(BF)
        for t in range(half // QT):
            rows = slice(QT * t, QT * (t + 1))
            a, b = outs[0][t], outs[1][t]
            ref.vgqf[rows, part] = jnp.where(first_head, a[:, :128], b[:, :128]) * 0.125
            shift = jnp.where(first_head, a[:, 128:], b[:, 128:]) * 0.125
            other = jnp.where(low, -pltpu.roll(shift, 96, 1), pltpu.roll(shift, 32, 1))
            ref.vrel[rows, part] = (
                shift * ref.vcos[rows, :] + other * ref.vsin[rows, :]
            ).astype(BF)
        ref.vk[:, cols] = ref.vkt[...].T
        ref.vv[:, cols] = ref.vvt[...].T
        both = mm(ref.vqt[...], ref.vrel[:, part])
        small[pl.ds(pl.multiple_of(64 * i, 64), 64), :] = jnp.where(first_head, both[:64], both[64:])

        @pl.when(buf == 1)
        def tail():
            wide_cols = pl.ds(pl.multiple_of(g * 256, 256), 256)
            gq = (ref.vgqf[...] + mm_nt(ref.vrel[...], ref.vbd[g])).astype(BF)
            ref.vq[:, wide_cols] = gq
            dk = ref.vk[:, wide_cols]
            dv = ref.vv[:, wide_cols]
            ref.vval[:, 0:256] = mm(ref.vmt[...], gq).astype(BF)
            ref.vval[:, 256:512] = mm(ref.vxt[...], dk).astype(BF)
            ref.vval[:, 512:768] = mm(ref.vxt[...], dv).astype(BF)

            def keep(pos, block):
                ref.gkeep[g, pos] = block

            def send(pos, block):
                ref.gsend[g, pos] = block

            for n in range(groups):

                @pl.when(g == n)
                def place():
                    split(ORDERS["G" + str(n)], slice(0, 768), keep, send)

        for t in range(pairs):
            point("U", t, i)

    loop(pairs, attention_step)

    spread_m = wide(pool_matrix(128)).T.astype(BF)

    def token_step(t):
        small_rows = pl.ds(pl.multiple_of(128 * t, 128), 128)
        rows = pl.ds(pl.multiple_of(256 * t, 256), 256)
        pooled = ref.vun[small_rows, :] + mm_nt(ref.vq[small_rows, :], ref.vwq[...])
        high = pooled.astype(BF)
        rest = (pooled - wide(high)).astype(BF)
        acc = mm(spread_m, high) + mm(spread_m, rest)
        acc = acc + mm_nt(ref.vk[rows, :], ref.vwk[...])
        acc = (acc + mm_nt(ref.vv[rows, :], ref.vwv[...])).astype(BF)
        ref.vk[rows, :] = acc

    loop(slot // 256, token_step)
    point("T", 0)


def backward(args, seq, grp):
    half, width = args["gouter"].shape
    slot = 2 * half
    inner = args["slope"].shape[1]
    part = slot // seq
    share = width // seq
    small_rows = seq * 64 * -(-66 * (width // 128) // (seq * 64))
    assert small_rows % (seq * grp) == 0
    vm = pltpu.VMEM
    scratch = dict(
        vgo=vm((half, width), BF),
        vmt=vm((width, half), BF),
        vacc=vm((half, width), F32),
        vun=vm((half, width), F32),
        vrs=vm((half, 128), F32),
        vwo=vm((width, width), BF),
        vat=vm((half, width), BF),
        vslope=vm((2, half, FFC), BF),
        vwout=vm((2, FFC, width), BF),
        vwin=vm((2, width, FFC), BF),
        vval=vm((width, 768), BF),
        vp=vm((2, 2, half, slot), BF),
        vq=vm((half, width), BF),
        vk=vm((slot, width), BF),
        vv=vm((slot, width), BF),
        vlinv=vm((half, width), F32),
        vxt=vm((width, slot), BF),
        vbd=vm(args["bd"].shape, BF),
        vcos=vm((half, 128), F32),
        vsin=vm((half, 128), F32),
        vfeat=vm((slot, 128), BF),
        vqt=vm((128, half), BF),
        vgt=vm((128, half), BF),
        vgqf=vm((half, 256), F32),
        vrel=vm((half, 256), BF),
        vds=vm((half, slot), BF),
        vkt=vm((128, slot), BF),
        vvt=vm((128, slot), BF),
        vwq=vm((width, width), BF),
        vwk=vm((width, width), BF),
        vwv=vm((width, width), BF),
        vsm=vm((small_rows, 128), F32),
        vres=vm((small_rows // (seq * grp), 128), F32),
        vag=vm((grp, small_rows // (seq * grp), 128), F32),
        vall=vm((seq, grp, small_rows // (seq * grp), 128), F32),
        rkeep=vm((4, small_rows // seq, 128), BF),
        rsend=vm((4, small_rows // seq, 128), BF),
        ikeep=vm((3, 4, share, 1024), BF),
        isend=vm((3, 4, share, 1024), BF),
        wkeep=vm((4, share, width), BF),
        wsend=vm((4, share, width), BF),
        gkeep=vm((3, 4, share, 768), BF),
        gsend=vm((3, 4, share, 768), BF),
        lsem=pltpu.SemaphoreType.DMA((20 + OCHUNKS,)),
        wsem=pltpu.SemaphoreType.DMA((4, 2)),
        dsem=pltpu.SemaphoreType.DMA((2,)),
        asend=pltpu.SemaphoreType.DMA((2, seq)),
        arecv=pltpu.SemaphoreType.DMA((2, seq)),
        msend=pltpu.SemaphoreType.DMA((2, max(seq, grp))),
        mrecv=pltpu.SemaphoreType.DMA((2, max(seq, grp))),
        ssem=pltpu.SemaphoreType.DMA((len(ORDERS), 2 + grp)),
        rsem=pltpu.SemaphoreType.DMA((len(ORDERS), 2 + grp)),
    )
    tall = inner // seq
    for name in ORDERS:
        rows, cols = share, width
        if name[0] == "O":
            rows, cols = tall, width // OCHUNKS
        elif name[0] == "I":
            cols = 1024
        elif name == "R":
            rows, cols = small_rows // seq, 128
        z_rows = rows // grp
        if name in EARLY:
            scratch[name + "k"] = vm((4, grp, z_rows, cols), BF)
            scratch[name + "r0"] = vm((4, grp, z_rows, cols), BF)
            scratch[name + "r1"] = vm((2, z_rows, cols), BF)
            scratch[name + "r2"] = vm((1, z_rows, cols), BF)
            scratch[name + "z"] = vm((4, z_rows, cols), BF)
            scratch[name + "rz"] = vm((grp - 1, 4, z_rows, cols), BF)
        else:
            if name[0] == "O":
                scratch[name + "k"] = vm((4, rows, cols), BF)
            scratch[name + "r0"] = vm((4, rows, cols), BF)
            scratch[name + "r1"] = vm((2, rows, cols), BF)
            scratch[name + "r2"] = vm((1, rows, cols), BF)
            fold = 1 if z_rows % 16 == 0 else 2
            scratch[name + "z"] = vm((grp, z_rows * fold, cols // fold), BF)
            scratch[name + "rz"] = vm((grp - 1, z_rows * fold, cols // fold), BF)
    names = list(scratch)
    outs = [
        sds((seq, part, width), BF),
        sds((seq, part // 2, width), BF),
        sds((share // grp, inner), F32),
        sds((tall // grp, width), F32),
        sds((share // grp, width), F32),
        sds((share // grp, width), F32),
        sds((share // grp, width), F32),
        sds((share // grp, width), F32),
        sds((small_rows, 128), F32),
    ]
    hbm = pl.BlockSpec(memory_space=pl.ANY)
    vmem = pl.BlockSpec(memory_space=pltpu.VMEM)
    in_vmem = ("g1", "dgain2")
    return pl.pallas_call(
        functools.partial(back_body, names, (seq, grp)),
        out_shape=outs,
        in_specs=[vmem if n in in_vmem else hbm for n in BACK_INPUTS],
        out_specs=[hbm, hbm] + [vmem] * (len(outs) - 2),
        scratch_shapes=list(scratch.values()),
        compiler_params=pltpu.CompilerParams(
            collective_id=1, has_side_effects=True, vmem_limit_bytes=63 << 20
        ),
        cost_estimate=pl.CostEstimate(
            flops=30_000_000_000, bytes_accessed=60_000_000, transcendentals=0
        ),
    )(*[args[n] for n in BACK_INPUTS])


def finish_body(count, *refs):
    srcs, small = refs[:count], refs[count]
    dsts = refs[count + 1 : 2 * count + 1]
    rel, attn, ffn = refs[2 * count + 1 : 2 * count + 4]
    rooms = refs[2 * count + 4 : 3 * count + 4]
    sem = refs[-1]
    loads = [pltpu.make_async_copy(s, r, sem.at[0, i]) for i, (s, r) in enumerate(zip(srcs, rooms))]
    stores = [pltpu.make_async_copy(r, d, sem.at[1, i]) for i, (r, d) in enumerate(zip(rooms, dsts))]
    for copy in loads:
        copy.start()
    pairs = attn.shape[0] // 128
    for i in range(pairs):
        both = small[64 * i : 64 * (i + 1), :]
        rel[2 * i] = both[:, :64]
        rel[2 * i + 1] = both[:, 64:]
        attn[pl.ds(128 * i, 128)] = small[64 * pairs + i, :]
        ffn[pl.ds(128 * i, 128)] = small[65 * pairs + i, :]
    for load, store in zip(loads, stores):
        load.wait()
        store.start()
    for copy in stores:
        copy.wait()


def finish(arrays, small, heads, width):
    count = len(arrays)
    hbm = pl.BlockSpec(memory_space=pltpu.HBM)
    vmem = pl.BlockSpec(memory_space=pltpu.VMEM)
    return pl.pallas_call(
        functools.partial(finish_body, count),
        out_shape=[sds(a.shape, a.dtype) for a in arrays]
        + [sds((heads, 64, 64), F32), sds((width,), F32), sds((width,), F32)],
        in_specs=[hbm] * count + [vmem],
        out_specs=[hbm] * count + [vmem] * 3,
        scratch_shapes=[pltpu.VMEM(a.shape, a.dtype) for a in arrays]
        + [pltpu.SemaphoreType.DMA((2, count))],
        compiler_params=pltpu.CompilerParams(vmem_limit_bytes=63 << 20),
    )(*arrays, small)


def local(
    seq_size, grp_size, hidden, lengths, query_weight, key_weight, value_weight, w_rel,
    output_weight, gain_attn, inner_weight, outer_weight, gain_ffn, cotangent,
):
    micro, unused, seqs, part, width = hidden.shape
    count = micro * seqs
    assert count == seq_size == 8
    weights = dict(
        wq=query_weight, wk=key_weight, wv=value_weight, wo=output_weight, win=inner_weight,
        wout=outer_weight, g1=gain_attn, g2=gain_ffn,
    )
    kept = forward(
        dict(
            weights, hidden=hidden.reshape(count, part, width), w_rel=w_rel,
            lengths=lengths.transpose(1, 2, 0).reshape(seqs, micro),
            cot=cotangent.reshape(count, part // 2, width),
        ),
        seq_size,
        grp_size,
    )
    outer = kept["outer"]
    tall = outer.shape[3]
    split = outer.shape[:3] + (grp_size, tall // grp_size, outer.shape[4])
    kept.update(weights, outer3=outer, outer4=outer.reshape(split), dgain2=kept["dgain"])
    *sums, small = backward(kept, seq_size, grp_size)
    hid, pooled, d_inner, d_outer, d_out, d_query, d_key, d_value, d_rel, d_attn, d_ffn = finish(
        sums, small, w_rel.shape[0], width
    )
    return (
        pooled.reshape(cotangent.shape),
        hid.reshape(hidden.shape),
        d_query,
        d_key,
        d_value,
        d_rel,
        d_out,
        d_attn,
        d_inner,
        d_outer,
        d_ffn,
    )


def solution(mesh):
    rows = P(None, "grp", None, "seq", None)
    spread = P(("seq", "grp"), None)
    sizes = dict(mesh.shape)
    return jax.shard_map(
        functools.partial(local, sizes["seq"], sizes["grp"]),
        mesh=mesh,
        in_specs=(rows, P(None, "grp", None)) + (P(),) * 9 + (rows,),
        out_specs=(
            rows, rows, spread, spread, spread, P(), spread, P(), spread, spread, P()
        ),
        check_vma=False,
    )
```

```python
import functools
import math
import types

import jax
import jax.numpy as jnp
from jax import lax
from jax.experimental import pallas as pl
from jax.experimental.pallas import tpu as pltpu
from jax.sharding import PartitionSpec as P

BF = jnp.bfloat16
F32 = jnp.float32
I32 = jnp.int32
MESH = pl.DeviceIdType.MESH
EPS = 1e-05
FFC = 512
QT = 256
OCHUNKS = 3
EARLY = ("O0", "O1")
ORDERS = {
    "O0": (1, 2, 4), "O1": (1, 2, 4), "O2": (1, 2, 4), "I0": (1, 4, 2), "I1": (1, 2, 4),
    "I2": (1, 2, 4), "W": (1, 4, 2), "G0": (1, 2, 4), "G1": (1, 4, 2), "G2": (1, 4, 2),
    "R": (1, 2, 4),
}


def sds(shape, dtype):
    return jax.ShapeDtypeStruct(shape, dtype)


def mm(a, b):
    return lax.dot_general(a, b, (((1,), (0,)), ((), ())), preferred_element_type=F32)


def mm_nt(a, b):
    return lax.dot_general(a, b, (((1,), (1,)), ((), ())), preferred_element_type=F32)


def mm_tn(a, b):
    return lax.dot_general(a, b, (((0,), (0,)), ((), ())), preferred_element_type=F32)


def rel_of(pos, order):
    bits = len(order)
    rel = 0
    for i, mask in enumerate(order):
        if (pos >> (bits - 1 - i)) & 1:
            rel |= mask
    return rel


def loop(count, body):
    def step(i, carry):
        body(i)
        return carry

    lax.fori_loop(0, count, step, 0)


def masks_of(size):
    return [1 << i for i in range(size.bit_length() - 1)]


def xor(rank, rel, size):
    total = 0
    for mask in masks_of(size):
        a = lax.rem(lax.div(rank, mask), 2)
        if isinstance(rel, int):
            total = total + mask * ((1 - a) if rel & mask else a)
        else:
            b = lax.rem(lax.div(rel, mask), 2)
            total = total + mask * (a + b - 2 * a * b)
    return total


def wide(value):
    return value.astype(F32)


def pool_matrix(rows):
    row = lax.broadcasted_iota(I32, (rows, 2 * rows), 0)
    col = lax.broadcasted_iota(I32, (rows, 2 * rows), 1)
    return jnp.where((col == 2 * row) | (col == 2 * row + 1), 0.5, 0.0).astype(BF)


def norm_parts(rows):
    centered = rows - jnp.mean(rows, -1, keepdims=True)
    rstd = lax.rsqrt(jnp.mean(centered * centered, -1, keepdims=True) + EPS)
    return centered * rstd, rstd


def norm_back(grad, unit, rstd, gain):
    scaled = grad * gain
    return rstd * (
        scaled
        - jnp.mean(scaled, -1, keepdims=True)
        - unit * jnp.mean(scaled * unit, -1, keepdims=True)
    )


FORE_INPUTS = list(
    dict(hidden=0, cot=0, lengths=0, wq=0, wk=0, wv=0, w_rel=0, wo=0, win=0, wout=0, g1=0, g2=0)
)
FORE_OUTPUTS = list(
    dict(
        attn=0, linv=0, p=0, q=0, k=0, v=0, xt=0, pt=0, bd=0, cos=0, sin=0, feat=0, rows=0,
        slope=0, gouter=0, unit=0, rstd=0, mixed=0, actt=0, dgain=0,
    )
)


def fore_body(names, sizes, *refs):
    ref = types.SimpleNamespace(**dict(zip(FORE_INPUTS + FORE_OUTPUTS + names, refs)))
    seq, grp = sizes
    me = lax.axis_index("seq")
    half, width = ref.vq.shape
    slot = 2 * half
    part = slot // seq
    inner = ref.wout.shape[0]
    pairs = width // 128
    groups = width // 256
    steps = inner // FFC
    chips = seq // 2
    chip, core = lax.div(me, 2), lax.rem(me, 2)

    early = [(ref.wk, ref.vwk), (ref.wv, ref.vwv), (ref.wq, ref.vwq), (ref.w_rel, ref.vrel)]
    loads = [
        pltpu.make_async_copy(src, dst, ref.lsem.at[i])
        for i, (src, dst) in enumerate(
            early + [(ref.wo, ref.vwo), (ref.win, ref.vwin), (ref.wout, ref.vwout)]
        )
    ]

    stores = []

    def store(src, dst):
        copy = pltpu.make_async_copy(src, dst, ref.ssem.at[len(stores)])
        copy.start()
        stores.append(copy)

    def rows_of(rank, size):
        return pl.ds(pl.multiple_of(rank * size, size), size)

    def blocks(src, dst, size, bank, rel):
        copies = []
        for c in range(2):
            rank = 2 * xor(chip, rel, chips) + c
            copies.append(
                pltpu.make_async_remote_copy(
                    src_ref=src.at[rank],
                    dst_ref=dst.at[rows_of(me, size)],
                    send_sem=ref.asend.at[bank, 2 * rel + c],
                    recv_sem=ref.arecv.at[bank, 2 * rel + core],
                    device_id={"seq": rank},
                    device_id_type=MESH,
                )
            )
        return copies

    def arrivals(src, dst, size, bank, rel):
        copies = []
        for c in range(2):
            rank = 2 * xor(chip, rel, chips) + c
            copies.append(
                pltpu.make_async_remote_copy(
                    src_ref=src.at[rank],
                    dst_ref=dst.at[rows_of(rank, size)],
                    send_sem=ref.asend.at[bank, 2 * rel + c],
                    recv_sem=ref.arecv.at[bank, 2 * rel + c],
                    device_id={"seq": rank},
                    device_id_type=MESH,
                )
            )
        return copies

    def mate(src, dst, size, bank, receive):
        rank = 2 * chip + 1 - core
        spot = rank if receive else me
        return pltpu.make_async_remote_copy(
            src_ref=src.at[rank],
            dst_ref=dst.at[rows_of(spot, size)],
            send_sem=ref.asend.at[bank, 0],
            recv_sem=ref.arecv.at[bank, 0],
            device_id={"seq": rank},
            device_id_type=MESH,
        )

    hid = (ref.hidden, ref.vx, part, 0)
    cot = (ref.cot, ref.vcot, part // 2, 1)
    own = [
        pltpu.make_async_copy(src.at[me], dst.at[rows_of(me, size)], ref.osem.at[bank])
        for src, dst, size, bank in (hid, cot)
    ]

    barrier = pltpu.get_barrier_semaphore()
    for k in range(1, seq):
        pl.semaphore_signal(
            barrier, inc=1, device_id={"seq": lax.rem(me + k, seq)}, device_id_type=MESH
        )
    own[0].start()
    for copy in loads:
        copy.start()
    pl.semaphore_wait(barrier, seq - 1)
    mate(*hid, False).start()
    near, far = list(range(1, chips - 1)), [chips - 1]
    for rel in near:
        for copy in blocks(*hid, rel):
            copy.start()

    lane_row = lax.broadcasted_iota(I32, (1, 128), 1)
    freq = wide(lax.rem(lane_row, 32))
    rate = jnp.exp(freq * (-math.log(10000.0) / 32))
    pos = wide(lax.broadcasted_iota(I32, (half, 1), 0))
    turn = (2.0 * pos) * rate
    ref.vcos[...] = jnp.cos(turn)
    ref.vsin[...] = jnp.sin(turn)
    first_half = lax.rem(lane_row, 64) < 32
    for t in range(2):
        angle = (pos + float(half * t)) * rate
        ref.vfeat[half * t : half * (t + 1), :] = jnp.where(
            first_half, jnp.sin(angle), jnp.cos(angle)
        ).astype(BF)
    store(ref.vcos, ref.cos)
    store(ref.vsin, ref.sin)
    store(ref.vfeat, ref.feat)
    for copy in loads[:4]:
        copy.wait()
    ref.vbd[...] = jnp.zeros_like(ref.vbd)
    for h in range(2 * pairs):
        ref.vbd[h // 4, 64 * (h % 4) : 64 * (h % 4) + 64, 64 * (h % 4) : 64 * (h % 4) + 64] = (
            ref.vrel[h]
        )
    store(ref.vbd, ref.bd)

    pool = pool_matrix(part)

    def project(index):
        rows = rows_of(index, 2 * part)
        small = rows_of(index, part)
        tile = ref.vx[rows, :]
        ref.vk[rows, :] = mm(tile, ref.vwk[...]).astype(BF)
        ref.vv[rows, :] = mm(tile, ref.vwv[...]).astype(BF)
        pooled = mm(pool, tile)
        ref.vpool[small, :] = pooled
        short = pooled.astype(BF)
        ref.vq[small, :] = mm(short, ref.vwq[...]).astype(BF)
        ref.vxt[:, rows] = tile.T
        ref.vpt[:, small] = short.T

    mate(*hid, True).wait_recv()
    own[0].wait()
    project(chip)
    for rel in near:
        for copy in arrivals(*hid, rel):
            copy.wait_recv()
    for rel in far:
        for copy in blocks(*hid, rel):
            copy.start()
    for rel in near:
        project(xor(chip, rel, chips))
    for rel in far:
        for copy in arrivals(*hid, rel):
            copy.wait_recv()
    own[1].start()
    mate(*cot, False).start()
    for rel in near + far:
        for copy in blocks(*cot, rel):
            copy.start()
    for rel in far:
        project(xor(chip, rel, chips))
    store(ref.vk, ref.k)
    store(ref.vv, ref.v)
    store(ref.vq, ref.q)
    store(ref.vxt, ref.xt)
    store(ref.vpt, ref.pt)

    scale = 0.125 * 1.4426950408889634
    low = lax.rem(lane_row, 64) < 32
    first_head = lane_row < 64
    seqs, micro = ref.lengths.shape
    mine_row = lax.broadcasted_iota(I32, (seqs, micro), 0) == lax.rem(me, seqs)
    mine_col = lax.broadcasted_iota(I32, (seqs, micro), 1) == lax.div(me, seqs)
    limit = jnp.where(mine_row & mine_col, wide(ref.lengths[...]), 0.0)
    limit = jnp.sum(jnp.sum(limit, 1, keepdims=True), 0, keepdims=True)
    key_ok = wide(lax.broadcasted_iota(I32, (1, slot), 1)) < limit
    ones = jnp.ones((slot, 128), BF)

    def probs(i, buf):
        return pltpu.make_async_copy(
            ref.vp.at[buf], ref.p.at[pl.ds(2 * i, 2)], ref.wsem.at[2, buf]
        )

    def attention_step(i):
        buf = lax.rem(i, 2)

        @pl.when(i >= 2)
        def free():
            probs(i - 2, buf).wait()

        cols = pl.ds(pl.multiple_of(i * 128, 128), 128)
        part_bd = pl.ds(pl.multiple_of(buf * 128, 128), 128)
        rel = mm(ref.vq[:, cols], ref.vbd[lax.div(i, 2), part_bd, part_bd])
        other = jnp.where(low, pltpu.roll(rel, 96, 1), -pltpu.roll(rel, 32, 1))
        ref.vsh[...] = (rel * ref.vcos[...] + other * ref.vsin[...]).astype(BF)
        key_side = jnp.concatenate([ref.vk[:, cols], ref.vfeat[...]], 1)
        value_side = jnp.concatenate([ref.vv[:, cols], ones], 1)
        for t in range(half // QT):
            rows = slice(QT * t, QT * (t + 1))
            q_part = ref.vq[rows, cols]
            s_part = ref.vsh[rows, :]
            outs = []
            for h in range(2):
                mine = first_head if h == 0 else jnp.logical_not(first_head)
                zero = jnp.zeros_like(q_part)
                left = jnp.concatenate(
                    [jnp.where(mine, q_part, zero), jnp.where(mine, s_part, zero)], 1
                )
                s = jnp.where(key_ok, mm_nt(left, key_side), -1e30)
                top = jnp.max(s, -1, keepdims=True)
                p = jnp.exp2((s - top) * scale).astype(BF)
                ref.vp[buf, h, rows, :] = p
                acc = mm(p, value_side)
                inv = 1.0 / acc[:, 128:]
                outs.append((acc[:, :128] * inv, inv))
            ref.vattn[rows, cols] = jnp.where(first_head, outs[0][0], outs[1][0]).astype(BF)
            ref.vlinv[rows, cols] = jnp.where(first_head, outs[0][1], outs[1][1])
        probs(i, buf).start()

    loop(pairs, attention_step)
    store(ref.vattn, ref.attn)
    store(ref.vlinv, ref.linv)

    for copy in loads[4:]:
        copy.wait()
    unit, rstd = norm_parts(ref.vpool[...] + mm(ref.vattn[...], ref.vwo[...]))
    mixed = unit * wide(ref.g1[...]).reshape(1, width)
    ref.vunit[...] = unit.astype(BF)
    ref.vrstd[...] = jnp.broadcast_to(rstd, ref.vrstd.shape)
    ref.vacc[...] = mixed
    short = mixed.astype(BF)
    ref.vmix[...] = short
    ref.vmt[...] = short.T
    store(ref.vunit, ref.unit)
    store(ref.vrstd, ref.rstd)
    store(ref.vmt, ref.mixed)

    def slopes(j, buf):
        cols = pl.ds(pl.multiple_of(j * FFC, FFC), FFC)
        return [
            pltpu.make_async_copy(ref.vslope.at[buf], ref.slope.at[:, cols], ref.wsem.at[3, buf]),
            pltpu.make_async_copy(ref.vactt.at[buf], ref.actt.at[cols, :], ref.wsem.at[1, buf]),
        ]

    def feed_step(j):
        buf = lax.rem(j, 2)
        cols = pl.ds(pl.multiple_of(j * FFC, FFC), FFC)

        @pl.when(j >= 2)
        def free():
            for copy in slopes(j - 2, buf):
                copy.wait()

        pre = mm(ref.vmix[...], ref.vwin[:, cols])
        cdf = 0.5 * (1.0 + lax.erf(pre * 0.7071067811865476))
        act = (pre * cdf).astype(BF)
        ref.vslope[buf] = (
            cdf + pre * (jnp.exp(pre * pre * -0.5) * 0.3989422804014327)
        ).astype(BF)
        ref.vacc[...] += mm(act, ref.vwout[cols, :])
        ref.vactt[buf] = act.T
        for copy in slopes(j, buf):
            copy.start()

    loop(steps, feed_step)
    mate(*cot, True).wait_recv()
    own[1].wait()
    for rel in near + far:
        for copy in arrivals(*cot, rel):
            copy.wait_recv()
    unit, rstd = norm_parts(ref.vacc[...])
    valid = wide(2 * lax.broadcasted_iota(I32, (half, 1), 0)) < limit
    g2 = wide(ref.g2[...]).reshape(1, width)
    ref.vrows[...] = jnp.where(valid, unit * g2, 0.0).astype(BF)
    store(ref.vrows, ref.rows)
    grad = jnp.where(valid, wide(ref.vcot[...]), 0.0)
    ref.dgain[...] = jnp.sum(grad * unit, 0, keepdims=True)
    two = norm_back(grad, unit, rstd, g2)
    ref.vgo[...] = two.astype(BF)
    store(ref.vgo, ref.gouter)

    for i in (pairs - 2, pairs - 1):
        probs(i, i % 2).wait()
    for j in (steps - 2, steps - 1):
        for copy in slopes(j, j % 2):
            copy.wait()
    for copy in stores:
        copy.wait()
    for bank in (hid, cot):
        mate(*bank, False).wait_send()
        for rel in near + far:
            for copy in blocks(*bank, rel):
                copy.wait_send()


def forward(args, seq, grp):
    count, part, width = args["hidden"].shape
    slot = part * seq
    half = slot // 2
    inner = args["wout"].shape[0]
    heads = width // 64
    vm = pltpu.VMEM
    scratch = dict(
        vx=vm((slot, width), BF),
        vcot=vm((half, width), BF),
        vwq=vm((width, width), BF),
        vwk=vm((width, width), BF),
        vwv=vm((width, width), BF),
        vrel=vm((heads, 64, 64), BF),
        vwo=vm((width, width), BF),
        vwin=vm((width, inner), BF),
        vwout=vm((inner, width), BF),
        vcos=vm((half, 128), F32),
        vsin=vm((half, 128), F32),
        vfeat=vm((slot, 128), BF),
        vbd=vm((width // 256, 256, 256), BF),
        vq=vm((half, width), BF),
        vk=vm((slot, width), BF),
        vv=vm((slot, width), BF),
        vpool=vm((half, width), F32),
        vxt=vm((width, slot), BF),
        vpt=vm((width, half), BF),
        vsh=vm((half, 128), BF),
        vp=vm((2, 2, half, slot), BF),
        vattn=vm((half, width), BF),
        vlinv=vm((half, width), F32),
        vunit=vm((half, width), BF),
        vrstd=vm((half, 128), F32),
        vacc=vm((half, width), F32),
        vmix=vm((half, width), BF),
        vmt=vm((width, half), BF),
        vslope=vm((2, half, FFC), BF),
        vactt=vm((2, FFC, half), BF),
        vrows=vm((half, width), BF),
        vgo=vm((half, width), BF),
        lsem=pltpu.SemaphoreType.DMA((7,)),
        wsem=pltpu.SemaphoreType.DMA((4, 2)),
        ssem=pltpu.SemaphoreType.DMA((24,)),
        osem=pltpu.SemaphoreType.DMA((2,)),
        asend=pltpu.SemaphoreType.DMA((2, seq)),
        arecv=pltpu.SemaphoreType.DMA((2, seq)),
    )
    names = list(scratch)
    shapes = dict(
        attn=sds((half, width), BF),
        linv=sds((half, width), F32),
        p=sds((heads, half, slot), BF),
        q=sds((half, width), BF),
        k=sds((slot, width), BF),
        v=sds((slot, width), BF),
        xt=sds((width, slot), BF),
        pt=sds((width, half), BF),
        bd=sds((width // 256, 256, 256), BF),
        cos=sds((half, 128), F32),
        sin=sds((half, 128), F32),
        feat=sds((slot, 128), BF),
        rows=sds((half, width), BF),
        slope=sds((half, inner), BF),
        gouter=sds((half, width), BF),
        unit=sds((half, width), BF),
        rstd=sds((half, 128), F32),
        mixed=sds((width, half), BF),
        actt=sds((inner, half), BF),
        dgain=sds((1, width), F32),
    )
    hbm = pl.BlockSpec(memory_space=pl.ANY)
    vmem = pl.BlockSpec(memory_space=pltpu.VMEM)
    spots = dict(g1=vmem, g2=vmem, lengths=vmem)
    outs = pl.pallas_call(
        functools.partial(fore_body, names, (seq, grp)),
        out_shape=[shapes[n] for n in FORE_OUTPUTS],
        in_specs=[spots.get(n, hbm) for n in FORE_INPUTS],
        out_specs=[hbm] * (len(FORE_OUTPUTS) - 1) + [vmem],
        scratch_shapes=list(scratch.values()),
        compiler_params=pltpu.CompilerParams(
            collective_id=0, has_side_effects=True, vmem_limit_bytes=63 << 20
        ),
        cost_estimate=pl.CostEstimate(
            flops=20_000_000_000, bytes_accessed=60_000_000, transcendentals=0
        ),
    )(*[args[n] for n in FORE_INPUTS])
    return dict(zip(FORE_OUTPUTS, outs))


def is_early(name, rows, grp):
    return name in EARLY and (rows // grp) % 16 == 0


class Chunk:
    def __init__(self, env, index, order, early, keep, send, recv, zbuf, recvz, out):
        self.env, self.index, self.order, self.early = env, index, order, early
        self.keep, self.send, self.recv = keep, send, recv
        self.zbuf, self.recvz, self.out = zbuf, recvz, out

    def remote(self, slot, src, dst, device):
        return pltpu.make_async_remote_copy(
            src_ref=src,
            dst_ref=dst,
            send_sem=self.env.ssem.at[self.index, slot],
            recv_sem=self.env.rsem.at[self.index, slot],
            device_id=device,
            device_id_type=MESH,
        )

    def seq_copy(self, stage):
        device = {"seq": xor(self.env.me, self.order[stage], self.env.seq)}
        if stage == 0:
            src = self.send
        else:
            half = 4 >> stage
            src = (self.zbuf if self.early else self.recv[0]).at[pl.ds(half, half)]
        return self.remote(stage, src, self.recv[stage], device)

    def z_copies(self):
        grp, z = self.env.grp, self.env.z
        copies = []
        for d in range(1, grp):
            peer = lax.rem(z + d, grp)
            src = self.recv[0].at[:, peer] if self.early else self.zbuf.at[peer]
            copies.append(self.remote(2 + d, src, self.recvz.at[d - 1], {"grp": peer}))
        return copies

    def unit(self):
        return 48 if self.keep.shape[1] % 48 == 0 else 64

    def step(self, n):
        keep, (recv0, recv1, recv2) = self.keep, self.recv
        zbuf, recvz, grp, z = self.zbuf, self.recvz, self.env.grp, self.env.z
        if n == 0:
            self.seq_copy(0).start()
        elif n == 1 and self.early:
            self.seq_copy(0).wait()

            def add(i):
                p, g = lax.div(i, grp), lax.rem(i, grp)
                recv0[p, g] = (wide(keep[p, g]) + wide(recv0[p, g])).astype(BF)

            loop(4 * grp, add)
            for copy in self.z_copies():
                copy.start()
        elif n == 2 and self.early:
            for copy in self.z_copies():
                copy.wait()

            def add(p):
                total = wide(recv0[p, z])
                for d in range(grp - 1):
                    total = total + wide(recvz[d, p])
                zbuf[p] = total.astype(BF)

            loop(4, add)
            self.seq_copy(1).start()
        elif n == 3 and self.early:
            self.seq_copy(1).wait()
            zbuf[1] = (wide(zbuf[1]) + wide(recv1[1])).astype(BF)
            self.seq_copy(2).start()
        elif n == 4 and self.early:
            self.seq_copy(2).wait()
            self.out(wide(zbuf[0]) + wide(recv1[0]) + wide(recv2[0]))
        elif n == 1:
            self.seq_copy(0).wait()
            unit = self.unit()
            parts = keep.shape[1] // unit

            def add(i):
                start = pl.multiple_of(unit * lax.rem(i, parts), unit)
                p, rows = 2 + lax.div(i, parts), pl.ds(start, unit)
                recv0[p, rows] = (wide(keep[p, rows]) + wide(recv0[p, rows])).astype(BF)

            loop(2 * parts, add)
            self.seq_copy(1).start()
        elif n == 2:
            self.seq_copy(1).wait()

            unit = self.unit()

            def add(i):
                rows = pl.ds(pl.multiple_of(unit * i, unit), unit)
                recv0[1, rows] = (
                    wide(keep[1, rows]) + wide(recv0[1, rows]) + wide(recv1[1, rows])
                ).astype(BF)

            loop(keep.shape[1] // unit, add)
            self.seq_copy(2).start()
        elif n == 3:
            self.seq_copy(2).wait()
            share = keep.shape[1] // grp
            unit = self.unit()
            for start in range(0, keep.shape[1], unit):
                rows = slice(start, start + unit)
                total = (
                    wide(keep[0, rows]) + wide(recv0[0, rows])
                    + wide(recv1[0, rows]) + wide(recv2[0, rows])
                )
                size = min(share, unit)
                for low in range(start, start + unit, size):
                    g, inside = low // share, low % share
                    piece = total[low - start : low - start + size].astype(BF)
                    if zbuf.shape[1] == share:
                        zbuf[g, inside : inside + size] = piece
                    else:
                        mid = zbuf.shape[2]
                        zbuf[g, :share] = piece[:, :mid]
                        zbuf[g, share:] = piece[:, mid:]
            for copy in self.z_copies():
                copy.start()
        else:
            for copy in self.z_copies():
                copy.wait()
            total = wide(zbuf[z])
            for d in range(grp - 1):
                total = total + wide(recvz[d])
            share = keep.shape[1] // grp
            if zbuf.shape[1] != share:
                total = jnp.concatenate([total[:share], total[share:]], 1)
            self.out(total)


BACK_INPUTS = list(
    dict(
        gouter=0, slope=0, wout=0, win=0, mixed=0, actt=0, unit=0, rstd=0, g1=0, wo=0, attn=0,
        p=0, q=0, k=0, v=0, linv=0, xt=0, pt=0, bd=0, cos=0, sin=0, feat=0, wq=0, wk=0, wv=0,
        rows=0, dgain2=0,
    )
)
BACK_OUTPUTS = list(
    dict(hidden=0, pooled=0, inner=0, outer=0, out=0, query=0, key=0, value=0, small=0)
)
POINTS = {
    ("X", 0): [("P", 0)],
    ("B", 0): [("O0", 1)],
    ("B", 1): [("I0", 0), ("O2", 1)],
    ("B", 3): [("I1", 0), ("I0", 1)],
    ("B", 4): [("I1", 1)],
    ("L", 0): [("I2", 0), ("W", 0), ("O1", 1), ("O2", 2)],
    ("U", 0): [("I2", 1), ("I0", 2), ("W", 1)],
    ("U", 1): [("G0", 0)],
    ("U", 2): [("O0", 2), ("I1", 2)],
    ("U", 3): [("G1", 0), ("I2", 2)],
    ("U", 4): [("G0", 1), ("G1", 1), ("P", 1)],
    ("U", 5): [
        ("R", 0), ("G2", 0), ("I1", 3), ("O1", 2), ("R", 1), ("O2", 3), ("W", 2), ("G2", 1),
    ],
    ("T", 0): [
        ("G1", 2), ("G0", 2), ("I0", 3), ("G2", 2), ("R", 2), ("O1", 3), ("H", 0), ("I2", 3),
        ("I1", 4), ("G1", 3), ("R", 3), ("O0", 3), ("W", 3), ("R", 4), ("I2", 4), ("A", 0),
        ("I0", 4), ("G0", 3), ("G2", 3), ("A", 1), ("O2", 4), ("O1", 4), ("O0", 4), ("G0", 4),
        ("W", 4), ("G1", 4), ("G2", 4), ("A", 2), ("H", 1),
    ],
}


def back_body(names, sizes, *refs):
    every = dict(zip(BACK_INPUTS + BACK_OUTPUTS + names, refs))
    ref = types.SimpleNamespace(**every)
    seq, grp = sizes
    me = lax.axis_index("seq")
    z = lax.axis_index("grp")
    env = types.SimpleNamespace(me=me, z=z, seq=seq, grp=grp, ssem=ref.ssem, rsem=ref.rsem)
    half, width = ref.vgo.shape
    slot = 2 * half
    inner = ref.slope.shape[1]
    steps = inner // FFC
    pairs = width // 128
    groups = width // 256
    lsem = ref.lsem

    plain = [
        (ref.gouter, ref.vgo), (ref.mixed, ref.vmt),
        (ref.unit, ref.vunit), (ref.rstd, ref.vrs), (ref.wo, ref.vwo), (ref.attn, ref.vat),
        (ref.linv, ref.vlinv),
        (ref.q, ref.vq), (ref.k, ref.vk), (ref.v, ref.vv), (ref.feat, ref.vfeat),
        (ref.cos, ref.vcos), (ref.sin, ref.vsin), (ref.bd, ref.vbd), (ref.xt, ref.vxt),
        (ref.pt, ref.vmt),
        (ref.wq, ref.vwo), (ref.wk, ref.vwout.at[0]), (ref.wv, ref.vwout.at[1]),
    ]
    local = [pltpu.make_async_copy(*pair, lsem.at[i]) for i, pair in enumerate(plain)]

    def act_room(buf):
        return ref.vds.at[pl.ds(0, inner // seq), pl.ds(pl.multiple_of(half * buf, half), half)]

    def act_rows(pos, buf):
        bits = [lax.div(pos, 4), lax.rem(lax.div(pos, 2), 2), lax.rem(pos, 2)]
        rows = inner // seq
        start = xor(me, bits[0] + 2 * bits[1] + 4 * bits[2], seq) * rows
        return pltpu.make_async_copy(
            ref.actt.at[pl.ds(pl.multiple_of(start, rows), rows)], act_room(buf),
            ref.wsem.at[0, buf],
        )

    def weights(j, buf):
        cols = pl.ds(pl.multiple_of(j * FFC, FFC), FFC)
        return [
            pltpu.make_async_copy(ref.slope.at[:, cols], ref.vslope.at[buf], ref.wsem.at[4, buf]),
            pltpu.make_async_copy(ref.wout.at[cols, :], ref.vwout.at[buf, pl.ds(0, FFC)], ref.wsem.at[1, buf]),
            pltpu.make_async_copy(ref.win.at[:, cols], ref.vwin.at[buf], ref.wsem.at[2, buf]),
        ]

    def probs(i, buf):
        return pltpu.make_async_copy(
            ref.p.at[pl.ds(2 * i, 2)], ref.vp.at[buf], ref.wsem.at[3, buf]
        )

    chunks = {}
    results = []

    def out_cols(room, dst, start, stop, first=0):
        copy = pltpu.make_async_copy(
            room.at[:, pl.ds(start, stop - start)], dst.at[:, pl.ds(start, stop - start)],
            ref.fsem.at[len(results)],
        )
        results.append(copy)

        def put(value):
            room[:, start:stop] = value[:, first : first + stop - start]
            copy.start()

        return put

    def out_three(g):
        rooms = (ref.xq, ref.query), (ref.xk, ref.key), (ref.xv, ref.value)
        puts = [
            out_cols(*pair, 256 * g, 256 * (g + 1), 256 * i) for i, pair in enumerate(rooms)
        ]

        def put(value):
            for each in puts:
                each(value)

        return put

    def out_small(value):
        ref.vres[...] = value

    for index, (name, order) in enumerate(ORDERS.items()):
        early = is_early(name, inner // seq, grp)
        kind = name[0]
        n = int(name[1]) if len(name) > 1 else 0
        recv = [every[name + "r0"], every[name + "r1"], every[name + "r2"]]
        if kind == "O":
            keep, send = every[name + "k"], every[name + "s"]
            span = width // OCHUNKS
            out = out_cols(ref.xouter, ref.outer, span * n, span * (n + 1))
        elif kind == "I":
            keep, send = ref.ikeep.at[n], ref.isend.at[n]
            out = out_cols(ref.xinner, ref.inner, 1024 * n, 1024 * (n + 1))
        elif kind == "W":
            keep, send = ref.wkeep, ref.wsend
            out = out_cols(ref.xout, ref.out, 0, width)
        elif kind == "R":
            keep, send = ref.rkeep, ref.rsend
            out = out_small
        else:
            keep, send = ref.gkeep.at[n], ref.gsend.at[n]
            out = out_three(n)
        chunks[name] = Chunk(
            env, index, order, early, keep, send, recv, every[name + "z"], every[name + "rz"], out
        )

    def spread(src, dst, sem):
        size = dst.shape[1]
        block = lambda b: src.at[pl.ds(pl.multiple_of(b * size, size), size)]
        copies = [pltpu.make_async_copy(block(me), dst.at[me], ref.dsem.at[sem])]
        for k in range(1, seq):
            peer = lax.rem(me + k, seq)
            copies.append(
                pltpu.make_async_remote_copy(
                    src_ref=block(peer),
                    dst_ref=dst.at[me],
                    send_sem=ref.asend.at[sem, k],
                    recv_sem=ref.arecv.at[sem, k],
                    device_id={"seq": peer},
                    device_id_type=MESH,
                )
            )
        return copies

    def gather(stage):
        copies = []
        if stage == 0:
            pairs_of = [(lax.rem(z + k, grp), "grp", grp, z) for k in range(1, grp)]
            src, dst = ref.vres, ref.vag.at[z]
        else:
            pairs_of = [(lax.rem(me + k, seq), "seq", seq, me) for k in range(1, seq)]
            src, dst = ref.vag, ref.vall.at[me]
        for k, (peer, axis, size, rank) in enumerate(pairs_of):
            copies.append(
                pltpu.make_async_remote_copy(
                    src_ref=src,
                    dst_ref=dst,
                    send_sem=ref.msend.at[stage, k],
                    recv_sem=ref.mrecv.at[stage, k],
                    device_id={axis: peer},
                    device_id_type=MESH,
                )
            )
        return copies

    def gather_step(n):
        if n > 0:
            for copy in gather(n - 1):
                copy.wait()
        if n == 0:
            ref.vag[z] = ref.vres[...]
        elif n == 1:
            ref.vall[me] = ref.vag[...]
        if n < 2:
            for copy in gather(n):
                copy.start()
        else:
            spot = pltpu.make_async_copy(ref.vall, ref.small, ref.dsem.at[2])
            spot.start()
            spot.wait()

    def place_small():
        size = ref.vsm.shape[0] // seq
        for pos in range(seq):
            block = ref.vsm[pl.ds(pl.multiple_of(xor(me, rel_of(pos, ORDERS["R"]), seq) * size, size), size), :]
            (ref.rkeep if pos < seq // 2 else ref.rsend)[pos % (seq // 2)] = block.astype(BF)

    def event(name, n):
        if name in ("H", "P"):
            places = (ref.vk, ref.hidden, 1) if name == "H" else (ref.rows, ref.pooled, 0)
            for copy in spread(*places):
                copy.start() if n == 0 else copy.wait()
        elif name == "A":
            gather_step(n)
        else:
            if name == "R" and n == 0:
                place_small()
            chunks[name].step(n)

    def point(kind, index, dynamic=None):
        todo = POINTS.get((kind, index), [])
        if not todo:
            return
        if dynamic is None:
            for name, n in todo:
                event(name, n)
        else:

            @pl.when(dynamic == index)
            def run():
                for name, n in todo:
                    event(name, n)

    barrier = pltpu.get_barrier_semaphore()
    for k in range(1, seq):
        pl.semaphore_signal(
            barrier, inc=1, device_id={"seq": lax.rem(me + k, seq)}, device_id_type=MESH
        )
    for k in range(1, grp):
        pl.semaphore_signal(
            barrier, inc=1, device_id={"grp": lax.rem(z + k, grp)}, device_id_type=MESH
        )
    for copy in local[:2]:
        copy.start()
    act_rows(4, 0).start()
    act_rows(5, 1).start()
    for copy in weights(0, 0):
        copy.start()
    pl.semaphore_wait(barrier, seq + grp - 2)
    point("X", 0)
    local[0].wait()

    def outer_step(i):
        pos, buf = lax.rem(i + 4, 8), lax.rem(i, 2)
        act_rows(pos, buf).wait()
        value = mm(act_room(buf)[...], ref.vgo[...])

        @pl.when(i + 2 < seq)
        def more():
            act_rows(lax.rem(i + 6, 8), buf).start()

        first, second = lax.rem(lax.div(pos, 2), 2), lax.rem(pos, 2)
        span = width // OCHUNKS
        for half_of in range(2):

            @pl.when(lax.div(pos, 4) == half_of)
            def place():
                for n in range(OCHUNKS):
                    name = "O" + str(n)
                    spot = 2 * first + second if ORDERS[name][1] == 2 else 2 * second + first
                    room = every[name + ("s" if half_of else "k")]
                    piece = value[:, span * n : span * (n + 1)]
                    if is_early(name, inner // seq, grp):
                        size = piece.shape[0] // grp
                        for g in range(grp):
                            room[spot, g] = piece[size * g : size * (g + 1)].astype(BF)
                    else:
                        room[spot] = piece.astype(BF)

        @pl.when(i == 3)
        def go():
            for n in range(OCHUNKS):
                chunks["O" + str(n)].step(0)

    loop(seq, outer_step)
    local[1].wait()
    ref.vacc[...] = wide(ref.vgo[...])
    point("Q", 0)

    def rows_of(count, rel):
        step = width // seq
        return pl.ds(pl.multiple_of(xor(me, rel, seq) * step, step), step)

    def split(order, cols, keep, send):
        for pos in range(seq):
            block = ref.vval[rows_of(width, rel_of(pos, order)), cols]
            (keep if pos < seq // 2 else send)(pos % (seq // 2), block)

    def feed_step(j):
        buf = lax.rem(j, 2)
        for copy in weights(j, buf):
            copy.wait()

        @pl.when(j + 1 < steps)
        def more():
            for copy in weights(j + 1, 1 - buf):
                copy.start()

        @pl.when(j == 1)
        def rest():
            for copy in local[2:-4]:
                copy.start()
            probs(0, 0).start()

        grad = mm_nt(ref.vgo[...], ref.vwout[buf, :FFC])
        hid = (wide(ref.vslope[buf]) * grad).astype(BF)
        ref.vacc[...] += mm_nt(hid, ref.vwin[buf])
        ref.vval[:, :FFC] = mm(ref.vmt[...], hid).astype(BF)
        c = lax.div(j, 2)
        cols = pl.ds(pl.multiple_of(lax.rem(j, 2) * FFC, FFC), FFC)

        def keep(pos, block):
            ref.ikeep[c, pos, :, cols] = block

        def send(pos, block):
            ref.isend[c, pos, :, cols] = block

        for n in range(steps // 2):

            @pl.when(c == n)
            def place():
                split(ORDERS["I" + str(n)], slice(0, FFC), keep, send)

        for t in range(steps):
            point("B", t, j)

    loop(steps, feed_step)

    for copy in (local[-4], local[-2], local[-1]):
        copy.start()
    for copy in local[2:7]:
        copy.wait()
    grad = ref.vacc[...]
    unit = wide(ref.vunit[...])
    small = ref.vsm
    dgain = jnp.sum(grad * unit, 0, keepdims=True)
    for i in range(pairs):
        small[64 * pairs + i, :] = dgain[0, 128 * i : 128 * (i + 1)]
        small[64 * pairs + pairs + i, :] = ref.dgain2[0, 128 * i : 128 * (i + 1)]
    used = 66 * pairs
    small[used:, :] = jnp.zeros((small.shape[0] - used, 128), F32)
    one = norm_back(grad, unit, ref.vrs[:, :1], wide(ref.g1[...]).reshape(1, width))
    ref.vun[...] = one
    branch = one.astype(BF)
    attn = ref.vat[...]
    ref.vval[...] = mm_tn(attn, branch).astype(BF)

    def keep_w(pos, block):
        ref.wkeep[pos] = block

    def send_w(pos, block):
        ref.wsend[pos] = block

    split(ORDERS["W"], slice(0, width), keep_w, send_w)
    scaled = mm_nt(branch, ref.vwo[...]) * ref.vlinv[...]
    ref.vgo[...] = scaled.astype(BF)
    ref.vacc[...] = scaled * wide(attn)
    local[-3].start()
    for copy in local[7:-3]:
        copy.wait()
    point("L", 0)

    lane = lax.broadcasted_iota(I32, (1, 128), 1)
    low = lax.rem(lane, 64) < 32
    first_head = lane < 64
    ones = jnp.broadcast_to(jnp.where(lane < 2, 1.0, 0.0).astype(BF), (slot, 128))

    def attention_step(i):
        buf = lax.rem(i, 2)
        g = lax.div(i, 2)
        probs(i, buf).wait()

        @pl.when(i + 1 < pairs)
        def more():
            probs(i + 1, 1 - buf).start()

        cols = pl.ds(pl.multiple_of(i * 128, 128), 128)
        part = pl.ds(pl.multiple_of(buf * 128, 128), 128)
        ref.vqt[...] = ref.vq[:, cols].T
        ref.vgt[...] = ref.vgo[:, cols].T
        key_side = jnp.concatenate([ref.vk[:, cols], ref.vfeat[...]], 1)
        value_side = jnp.concatenate([ref.vv[:, cols], ones], 1)
        outs = [[], []]
        for h in range(2):
            mine = first_head if h == 0 else jnp.logical_not(first_head)
            for t in range(half // QT):
                rows = slice(QT * t, QT * (t + 1))
                g_part = ref.vgo[rows, cols]
                delta = jnp.sum(jnp.where(mine, ref.vacc[rows, cols], 0.0), -1, keepdims=True)
                coarse = wide(delta.astype(BF))
                tail = jnp.where(lane == 0, coarse, jnp.where(lane == 1, delta - coarse, 0.0))
                left = jnp.concatenate(
                    [jnp.where(mine, g_part, jnp.zeros_like(g_part)), (-tail).astype(BF)], 1
                )
                ds = (wide(ref.vp[buf, h, rows, :]) * mm_nt(left, value_side)).astype(BF)
                ref.vds[rows, :] = ds
                outs[h].append(mm(ds, key_side))
            lines = slice(64 * h, 64 * (h + 1))
            ref.vkt[lines, :] = (mm(ref.vqt[lines, :], ref.vds[...]) * 0.125).astype(BF)
            ref.vvt[lines, :] = mm(ref.vgt[lines, :], ref.vp[buf, h]).astype(BF)
        for t in range(half // QT):
            rows = slice(QT * t, QT * (t + 1))
            a, b = outs[0][t], outs[1][t]
            ref.vgqf[rows, part] = jnp.where(first_head, a[:, :128], b[:, :128]) * 0.125
            shift = jnp.where(first_head, a[:, 128:], b[:, 128:]) * 0.125
            other = jnp.where(low, -pltpu.roll(shift, 96, 1), pltpu.roll(shift, 32, 1))
            ref.vrel[rows, part] = (
                shift * ref.vcos[rows, :] + other * ref.vsin[rows, :]
            ).astype(BF)
        ref.vk[:, cols] = ref.vkt[...].T
        ref.vv[:, cols] = ref.vvt[...].T
        both = mm(ref.vqt[...], ref.vrel[:, part])
        small[pl.ds(pl.multiple_of(64 * i, 64), 64), :] = jnp.where(first_head, both[:64], both[64:])

        @pl.when(buf == 1)
        def tail():
            wide_cols = pl.ds(pl.multiple_of(g * 256, 256), 256)
            gq = (ref.vgqf[...] + mm_nt(ref.vrel[...], ref.vbd[g])).astype(BF)
            ref.vq[:, wide_cols] = gq
            dk = ref.vk[:, wide_cols]
            dv = ref.vv[:, wide_cols]
            ref.vval[:, 0:256] = mm(ref.vmt[...], gq).astype(BF)
            ref.vval[:, 256:512] = mm(ref.vxt[...], dk).astype(BF)
            ref.vval[:, 512:768] = mm(ref.vxt[...], dv).astype(BF)

            def keep(pos, block):
                ref.gkeep[g, pos] = block

            def send(pos, block):
                ref.gsend[g, pos] = block

            for n in range(groups):

                @pl.when(g == n)
                def place():
                    split(ORDERS["G" + str(n)], slice(0, 768), keep, send)

        for t in range(pairs):
            point("U", t, i)

    loop(pairs, attention_step)

    for copy in local[-3:]:
        copy.wait()
    spread_m = wide(pool_matrix(128)).T.astype(BF)

    def token_step(t):
        small_rows = pl.ds(pl.multiple_of(128 * t, 128), 128)
        rows = pl.ds(pl.multiple_of(256 * t, 256), 256)
        pooled = ref.vun[small_rows, :] + mm_nt(ref.vq[small_rows, :], ref.vwo[...])
        high = pooled.astype(BF)
        rest = (pooled - wide(high)).astype(BF)
        acc = mm(spread_m, high) + mm(spread_m, rest)
        acc = acc + mm_nt(ref.vk[rows, :], ref.vwout[0])
        acc = (acc + mm_nt(ref.vv[rows, :], ref.vwout[1])).astype(BF)
        ref.vk[rows, :] = acc

    loop(slot // 256, token_step)
    point("T", 0)
    for copy in results:
        copy.wait()


def backward(args, seq, grp):
    half, width = args["gouter"].shape
    slot = 2 * half
    inner = args["slope"].shape[1]
    part = slot // seq
    share = width // seq
    small_rows = seq * 64 * -(-66 * (width // 128) // (seq * 64))
    assert small_rows % (seq * grp) == 0
    vm = pltpu.VMEM
    scratch = dict(
        vgo=vm((half, width), BF),
        vmt=vm((width, half), BF),
        vacc=vm((half, width), F32),
        vun=vm((half, width), F32),
        vrs=vm((half, 128), F32),
        vwo=vm((width, width), BF),
        vat=vm((half, width), BF),
        vslope=vm((2, half, FFC), BF),
        vwout=vm((2, width, width), BF),
        vwin=vm((2, width, FFC), BF),
        vval=vm((width, 768), BF),
        vp=vm((2, 2, half, slot), BF),
        vq=vm((half, width), BF),
        vk=vm((slot, width), BF),
        vv=vm((slot, width), BF),
        vlinv=vm((half, width), F32),
        vxt=vm((width, slot), BF),
        vbd=vm(args["bd"].shape, BF),
        vcos=vm((half, 128), F32),
        vsin=vm((half, 128), F32),
        vfeat=vm((slot, 128), BF),
        vqt=vm((128, half), BF),
        vgt=vm((128, half), BF),
        vgqf=vm((half, 256), F32),
        vrel=vm((half, 256), BF),
        vds=vm((half, slot), BF),
        vkt=vm((128, slot), BF),
        vvt=vm((128, slot), BF),
        vunit=vm((half, width), BF),
        vsm=vm((small_rows, 128), F32),
        vres=vm((small_rows // (seq * grp), 128), F32),
        vag=vm((grp, small_rows // (seq * grp), 128), F32),
        vall=vm((seq, grp, small_rows // (seq * grp), 128), F32),
        rkeep=vm((4, small_rows // seq, 128), BF),
        rsend=vm((4, small_rows // seq, 128), BF),
        ikeep=vm((3, 4, share, 1024), BF),
        isend=vm((3, 4, share, 1024), BF),
        wkeep=vm((4, share, width), BF),
        wsend=vm((4, share, width), BF),
        gkeep=vm((3, 4, share, 768), BF),
        gsend=vm((3, 4, share, 768), BF),
        lsem=pltpu.SemaphoreType.DMA((24,)),
        wsem=pltpu.SemaphoreType.DMA((5, 2)),
        dsem=pltpu.SemaphoreType.DMA((3,)),
        fsem=pltpu.SemaphoreType.DMA((20,)),
        asend=pltpu.SemaphoreType.DMA((2, seq)),
        arecv=pltpu.SemaphoreType.DMA((2, seq)),
        msend=pltpu.SemaphoreType.DMA((2, max(seq, grp))),
        mrecv=pltpu.SemaphoreType.DMA((2, max(seq, grp))),
        ssem=pltpu.SemaphoreType.DMA((len(ORDERS), 2 + grp)),
        rsem=pltpu.SemaphoreType.DMA((len(ORDERS), 2 + grp)),
    )
    tall = inner // seq
    for name in ORDERS:
        rows, cols = share, width
        if name[0] == "O":
            rows, cols = tall, width // OCHUNKS
        elif name[0] == "I":
            cols = 1024
        elif name == "R":
            rows, cols = small_rows // seq, 128
        z_rows = rows // grp
        if is_early(name, tall, grp):
            scratch[name + "k"] = vm((4, grp, z_rows, cols), BF)
            scratch[name + "s"] = vm((4, grp, z_rows, cols), BF)
            scratch[name + "r0"] = vm((4, grp, z_rows, cols), BF)
            scratch[name + "r1"] = vm((2, z_rows, cols), BF)
            scratch[name + "r2"] = vm((1, z_rows, cols), BF)
            scratch[name + "z"] = vm((4, z_rows, cols), BF)
            scratch[name + "rz"] = vm((grp - 1, 4, z_rows, cols), BF)
        else:
            if name[0] == "O":
                scratch[name + "k"] = vm((4, rows, cols), BF)
                scratch[name + "s"] = vm((4, rows, cols), BF)
            scratch[name + "r0"] = vm((4, rows, cols), BF)
            scratch[name + "r1"] = vm((2, rows, cols), BF)
            scratch[name + "r2"] = vm((1, rows, cols), BF)
            fold = 1 if z_rows % 16 == 0 else 2
            scratch[name + "z"] = vm((grp, z_rows * fold, cols // fold), BF)
            scratch[name + "rz"] = vm((grp - 1, z_rows * fold, cols // fold), BF)
    scratch.update(
        xinner=vm((share // grp, inner), F32),
        xouter=vm((tall // grp, width), F32),
        xout=vm((share // grp, width), F32),
        xq=vm((share // grp, width), F32),
        xk=vm((share // grp, width), F32),
        xv=vm((share // grp, width), F32),
    )
    names = list(scratch)
    outs = [
        sds((seq, part, width), BF),
        sds((seq, part // 2, width), BF),
        sds((share // grp, inner), F32),
        sds((tall // grp, width), F32),
        sds((share // grp, width), F32),
        sds((share // grp, width), F32),
        sds((share // grp, width), F32),
        sds((share // grp, width), F32),
        sds((seq, grp, small_rows // (seq * grp), 128), F32),
    ]
    hbm = pl.BlockSpec(memory_space=pl.ANY)
    vmem = pl.BlockSpec(memory_space=pltpu.VMEM)
    in_vmem = ("g1", "dgain2")
    return pl.pallas_call(
        functools.partial(back_body, names, (seq, grp)),
        out_shape=outs,
        in_specs=[vmem if n in in_vmem else hbm for n in BACK_INPUTS],
        out_specs=[hbm] * len(outs),
        scratch_shapes=list(scratch.values()),
        compiler_params=pltpu.CompilerParams(
            collective_id=1, has_side_effects=True, vmem_limit_bytes=63 << 20
        ),
        cost_estimate=pl.CostEstimate(
            flops=30_000_000_000, bytes_accessed=60_000_000, transcendentals=0
        ),
    )(*[args[n] for n in BACK_INPUTS])


def pieces_of(shape):
    parts = 4 if len(shape) == 3 else 1
    size = shape[0] // parts
    return [pl.ds(i * size, size) for i in range(parts)]


def finish_body(count, *refs):
    srcs, small = refs[:count], refs[count]
    dsts = refs[count + 1 : 2 * count + 1]
    tails = refs[2 * count + 1 : 2 * count + 4]
    rooms = refs[2 * count + 4 : 3 * count + 4]
    held, rel, attn, ffn, sem, tail_sem = refs[3 * count + 4 :]
    head = pltpu.make_async_copy(small, held, tail_sem.at[3])
    head.start()
    loads, stores = [], []
    for src, room, dst in zip(srcs, rooms, dsts):
        for rows in pieces_of(src.shape):
            i = len(loads)
            loads.append(pltpu.make_async_copy(src.at[rows], room.at[rows], sem.at[0, i]))
            stores.append(pltpu.make_async_copy(room.at[rows], dst.at[rows], sem.at[1, i]))
            loads[-1].start()
    pairs = attn.shape[0] // 128
    head.wait()
    for i in range(pairs):
        both = held[64 * i : 64 * (i + 1), :]
        rel[2 * i] = both[:, :64]
        rel[2 * i + 1] = both[:, 64:]
        attn[pl.ds(128 * i, 128)] = held[64 * pairs + i, :]
        ffn[pl.ds(128 * i, 128)] = held[65 * pairs + i, :]
    for i, pair in enumerate(zip((rel, attn, ffn), tails)):
        stores.append(pltpu.make_async_copy(*pair, tail_sem.at[i]))
        stores[-1].start()
    for load, store in zip(loads, stores):
        load.wait()
        store.start()
    for copy in stores:
        copy.wait()


def finish(arrays, small, heads, width):
    count = len(arrays)
    hbm = pl.BlockSpec(memory_space=pltpu.HBM)
    tails = [sds((heads, 64, 64), F32), sds((width,), F32), sds((width,), F32)]
    total = sum(len(pieces_of(a.shape)) for a in arrays)
    return pl.pallas_call(
        functools.partial(finish_body, count),
        out_shape=[sds(a.shape, a.dtype) for a in arrays] + tails,
        in_specs=[hbm] * (count + 1),
        out_specs=[hbm] * (count + 3),
        scratch_shapes=[pltpu.VMEM(a.shape, a.dtype) for a in (*arrays, small, *tails)]
        + [pltpu.SemaphoreType.DMA((2, total)), pltpu.SemaphoreType.DMA((4,))],
        compiler_params=pltpu.CompilerParams(vmem_limit_bytes=63 << 20),
    )(*arrays, small)


def local(
    seq_size, grp_size, hidden, lengths, query_weight, key_weight, value_weight, w_rel,
    output_weight, gain_attn, inner_weight, outer_weight, gain_ffn, cotangent,
):
    micro, unused, seqs, part, width = hidden.shape
    count = micro * seqs
    assert count == seq_size == 8
    weights = dict(
        wq=query_weight, wk=key_weight, wv=value_weight, wo=output_weight, win=inner_weight,
        wout=outer_weight, g1=gain_attn, g2=gain_ffn,
    )
    kept = forward(
        dict(
            weights, hidden=hidden.reshape(count, part, width), w_rel=w_rel,
            lengths=lengths.transpose(1, 2, 0).reshape(seqs, micro),
            cot=cotangent.reshape(count, part // 2, width),
        ),
        seq_size,
        grp_size,
    )
    kept.update(weights, dgain2=kept["dgain"])
    *sums, small = backward(kept, seq_size, grp_size)
    small = small.reshape(-1, 128)
    hid, pooled, d_inner, d_outer, d_out, d_query, d_key, d_value, d_rel, d_attn, d_ffn = finish(
        sums, small, w_rel.shape[0], width
    )
    return (
        pooled.reshape(cotangent.shape),
        hid.reshape(hidden.shape),
        d_query,
        d_key,
        d_value,
        d_rel,
        d_out,
        d_attn,
        d_inner,
        d_outer,
        d_ffn,
    )


def solution(mesh):
    rows = P(None, "grp", None, "seq", None)
    spread = P(("seq", "grp"), None)
    sizes = dict(mesh.shape)
    return jax.shard_map(
        functools.partial(local, sizes["seq"], sizes["grp"]),
        mesh=mesh,
        in_specs=(rows, P(None, "grp", None)) + (P(),) * 9 + (rows,),
        out_specs=(
            rows, rows, spread, spread, spread, P(), spread, P(), spread, spread, P()
        ),
        check_vma=False,
    )
```

```python
import functools
import math
import types

import jax
import jax.numpy as jnp
from jax import lax
from jax.experimental import pallas as pl
from jax.experimental.pallas import tpu as pltpu
from jax.sharding import PartitionSpec as P

BF = jnp.bfloat16
F32 = jnp.float32
I32 = jnp.int32
MESH = pl.DeviceIdType.MESH
EPS = 1e-05
FFC = 512
QT = 256
OCHUNKS = 3
EARLY = ("O0", "O2")
ORDERS = {
    "O0": (1, 2, 4), "O1": (1, 2, 4), "O2": (1, 2, 4), "I0": (1, 4, 2), "I1": (1, 2, 4),
    "I2": (1, 4, 2), "W": (1, 2, 4), "G0": (1, 4, 2), "G1": (1, 2, 4), "G2": (1, 4, 2),
    "R": (1, 2, 4),
}


def sds(shape, dtype):
    return jax.ShapeDtypeStruct(shape, dtype)


def mm(a, b):
    return lax.dot_general(a, b, (((1,), (0,)), ((), ())), preferred_element_type=F32)


def mm_nt(a, b):
    return lax.dot_general(a, b, (((1,), (1,)), ((), ())), preferred_element_type=F32)


def mm_tn(a, b):
    return lax.dot_general(a, b, (((0,), (0,)), ((), ())), preferred_element_type=F32)


def rel_of(pos, order):
    bits = len(order)
    rel = 0
    for i, mask in enumerate(order):
        if (pos >> (bits - 1 - i)) & 1:
            rel |= mask
    return rel


def loop(count, body):
    def step(i, carry):
        body(i)
        return carry

    lax.fori_loop(0, count, step, 0)


def masks_of(size):
    return [1 << i for i in range(size.bit_length() - 1)]


def xor(rank, rel, size):
    total = 0
    for mask in masks_of(size):
        a = lax.rem(lax.div(rank, mask), 2)
        if isinstance(rel, int):
            total = total + mask * ((1 - a) if rel & mask else a)
        else:
            b = lax.rem(lax.div(rel, mask), 2)
            total = total + mask * (a + b - 2 * a * b)
    return total


def wide(value):
    return value.astype(F32)


def pool_matrix(rows):
    row = lax.broadcasted_iota(I32, (rows, 2 * rows), 0)
    col = lax.broadcasted_iota(I32, (rows, 2 * rows), 1)
    return jnp.where((col == 2 * row) | (col == 2 * row + 1), 0.5, 0.0).astype(BF)


def norm_parts(rows):
    centered = rows - jnp.mean(rows, -1, keepdims=True)
    rstd = lax.rsqrt(jnp.mean(centered * centered, -1, keepdims=True) + EPS)
    return centered * rstd, rstd


def norm_back(grad, unit, rstd, gain):
    scaled = grad * gain
    return rstd * (
        scaled
        - jnp.mean(scaled, -1, keepdims=True)
        - unit * jnp.mean(scaled * unit, -1, keepdims=True)
    )


FORE_INPUTS = list(
    dict(hidden=0, cot=0, lengths=0, wq=0, wk=0, wv=0, w_rel=0, wo=0, win=0, wout=0, g1=0, g2=0)
)
FORE_OUTPUTS = list(
    dict(
        attn=0, linv=0, p=0, q=0, k=0, v=0, xt=0, pt=0, bd=0, cos=0, sin=0, feat=0, rows=0,
        slope=0, gouter=0, unit=0, rstd=0, mixed=0, actt=0, dgain=0,
    )
)


def fore_body(names, sizes, *refs):
    ref = types.SimpleNamespace(**dict(zip(FORE_INPUTS + FORE_OUTPUTS + names, refs)))
    seq, grp = sizes
    me = lax.axis_index("seq")
    half, width = ref.vq.shape
    slot = 2 * half
    part = slot // seq
    inner = ref.wout.shape[0]
    pairs = width // 128
    groups = width // 256
    steps = inner // FFC
    chips = seq // 2
    chip, core = lax.div(me, 2), lax.rem(me, 2)

    early = [(ref.wk, ref.vwk), (ref.wv, ref.vwv), (ref.wq, ref.vwq), (ref.w_rel, ref.vrel)]
    loads = [
        pltpu.make_async_copy(src, dst, ref.lsem.at[i])
        for i, (src, dst) in enumerate(
            early + [(ref.wo, ref.vwo), (ref.win, ref.vwin), (ref.wout, ref.vwout)]
        )
    ]

    stores = []

    def store(src, dst):
        copy = pltpu.make_async_copy(src, dst, ref.ssem.at[len(stores)])
        copy.start()
        stores.append(copy)

    def rows_of(rank, size):
        return pl.ds(pl.multiple_of(rank * size, size), size)

    def blocks(src, dst, size, bank, rel):
        copies = []
        for c in range(2):
            rank = 2 * xor(chip, rel, chips) + c
            copies.append(
                pltpu.make_async_remote_copy(
                    src_ref=src.at[rank],
                    dst_ref=dst.at[rows_of(me, size)],
                    send_sem=ref.asend.at[bank, 2 * rel + c],
                    recv_sem=ref.arecv.at[bank, 2 * rel + core],
                    device_id={"seq": rank},
                    device_id_type=MESH,
                )
            )
        return copies

    def arrivals(src, dst, size, bank, rel):
        copies = []
        for c in range(2):
            rank = 2 * xor(chip, rel, chips) + c
            copies.append(
                pltpu.make_async_remote_copy(
                    src_ref=src.at[rank],
                    dst_ref=dst.at[rows_of(rank, size)],
                    send_sem=ref.asend.at[bank, 2 * rel + c],
                    recv_sem=ref.arecv.at[bank, 2 * rel + c],
                    device_id={"seq": rank},
                    device_id_type=MESH,
                )
            )
        return copies

    def mate(src, dst, size, bank, receive):
        rank = 2 * chip + 1 - core
        spot = rank if receive else me
        return pltpu.make_async_remote_copy(
            src_ref=src.at[rank],
            dst_ref=dst.at[rows_of(spot, size)],
            send_sem=ref.asend.at[bank, 0],
            recv_sem=ref.arecv.at[bank, 0],
            device_id={"seq": rank},
            device_id_type=MESH,
        )

    hid = (ref.hidden, ref.vx, part, 0)
    cot = (ref.cot, ref.vcot, part // 2, 1)
    own = [
        pltpu.make_async_copy(src.at[me], dst.at[rows_of(me, size)], ref.osem.at[bank])
        for src, dst, size, bank in (hid, cot)
    ]

    barrier = pltpu.get_barrier_semaphore()
    for k in range(1, seq):
        pl.semaphore_signal(
            barrier, inc=1, device_id={"seq": lax.rem(me + k, seq)}, device_id_type=MESH
        )
    own[0].start()
    for copy in loads:
        copy.start()
    pl.semaphore_wait(barrier, seq - 1)
    mate(*hid, False).start()
    near, far = list(range(1, chips - 1)), [chips - 1]
    for rel in near:
        for copy in blocks(*hid, rel):
            copy.start()

    lane_row = lax.broadcasted_iota(I32, (1, 128), 1)
    freq = wide(lax.rem(lane_row, 32))
    rate = jnp.exp(freq * (-math.log(10000.0) / 32))
    pos = wide(lax.broadcasted_iota(I32, (half, 1), 0))
    turn = (2.0 * pos) * rate
    ref.vcos[...] = jnp.cos(turn)
    ref.vsin[...] = jnp.sin(turn)
    first_half = lax.rem(lane_row, 64) < 32
    for t in range(2):
        angle = (pos + float(half * t)) * rate
        ref.vfeat[half * t : half * (t + 1), :] = jnp.where(
            first_half, jnp.sin(angle), jnp.cos(angle)
        ).astype(BF)
    store(ref.vcos, ref.cos)
    store(ref.vsin, ref.sin)
    store(ref.vfeat, ref.feat)
    for copy in loads[:4]:
        copy.wait()
    ref.vbd[...] = jnp.zeros_like(ref.vbd)
    for h in range(2 * pairs):
        ref.vbd[h // 4, 64 * (h % 4) : 64 * (h % 4) + 64, 64 * (h % 4) : 64 * (h % 4) + 64] = (
            ref.vrel[h]
        )
    store(ref.vbd, ref.bd)

    pool = pool_matrix(part)

    def project(index):
        rows = rows_of(index, 2 * part)
        small = rows_of(index, part)
        tile = ref.vx[rows, :]
        ref.vk[rows, :] = mm(tile, ref.vwk[...]).astype(BF)
        ref.vv[rows, :] = mm(tile, ref.vwv[...]).astype(BF)
        pooled = mm(pool, tile)
        ref.vpool[small, :] = pooled
        short = pooled.astype(BF)
        ref.vq[small, :] = mm(short, ref.vwq[...]).astype(BF)
        ref.vxt[:, rows] = tile.T
        ref.vpt[:, small] = short.T

    mate(*hid, True).wait_recv()
    own[0].wait()
    project(chip)
    for rel in near:
        for copy in arrivals(*hid, rel):
            copy.wait_recv()
    for rel in far:
        for copy in blocks(*hid, rel):
            copy.start()
    for rel in near:
        project(xor(chip, rel, chips))
    for rel in far:
        for copy in arrivals(*hid, rel):
            copy.wait_recv()
    own[1].start()
    mate(*cot, False).start()
    for rel in near + far:
        for copy in blocks(*cot, rel):
            copy.start()
    for rel in far:
        project(xor(chip, rel, chips))
    store(ref.vk, ref.k)
    store(ref.vv, ref.v)
    store(ref.vq, ref.q)
    store(ref.vxt, ref.xt)
    store(ref.vpt, ref.pt)

    scale = 0.125 * 1.4426950408889634
    low = lax.rem(lane_row, 64) < 32
    first_head = lane_row < 64
    seqs, micro = ref.lengths.shape
    mine_row = lax.broadcasted_iota(I32, (seqs, micro), 0) == lax.rem(me, seqs)
    mine_col = lax.broadcasted_iota(I32, (seqs, micro), 1) == lax.div(me, seqs)
    limit = jnp.where(mine_row & mine_col, wide(ref.lengths[...]), 0.0)
    limit = jnp.sum(jnp.sum(limit, 1, keepdims=True), 0, keepdims=True)
    key_ok = wide(lax.broadcasted_iota(I32, (1, slot), 1)) < limit
    ones = jnp.ones((slot, 128), BF)

    def probs(i, buf):
        return pltpu.make_async_copy(
            ref.vp.at[buf], ref.p.at[pl.ds(2 * i, 2)], ref.wsem.at[2, buf]
        )

    def attention_step(i):
        buf = lax.rem(i, 2)

        @pl.when(i >= 2)
        def free():
            probs(i - 2, buf).wait()

        cols = pl.ds(pl.multiple_of(i * 128, 128), 128)
        part_bd = pl.ds(pl.multiple_of(buf * 128, 128), 128)
        rel = mm(ref.vq[:, cols], ref.vbd[lax.div(i, 2), part_bd, part_bd])
        other = jnp.where(low, pltpu.roll(rel, 96, 1), -pltpu.roll(rel, 32, 1))
        ref.vsh[...] = (rel * ref.vcos[...] + other * ref.vsin[...]).astype(BF)
        key_side = jnp.concatenate([ref.vk[:, cols], ref.vfeat[...]], 1)
        value_side = jnp.concatenate([ref.vv[:, cols], ones], 1)
        for t in range(half // QT):
            rows = slice(QT * t, QT * (t + 1))
            q_part = ref.vq[rows, cols]
            s_part = ref.vsh[rows, :]
            outs = []
            for h in range(2):
                mine = first_head if h == 0 else jnp.logical_not(first_head)
                zero = jnp.zeros_like(q_part)
                left = jnp.concatenate(
                    [jnp.where(mine, q_part, zero), jnp.where(mine, s_part, zero)], 1
                )
                s = jnp.where(key_ok, mm_nt(left, key_side), -1e30)
                top = jnp.max(s, -1, keepdims=True)
                p = jnp.exp2((s - top) * scale).astype(BF)
                ref.vp[buf, h, rows, :] = p
                acc = mm(p, value_side)
                inv = 1.0 / acc[:, 128:]
                outs.append((acc[:, :128] * inv, inv))
            ref.vattn[rows, cols] = jnp.where(first_head, outs[0][0], outs[1][0]).astype(BF)
            ref.vlinv[rows, cols] = jnp.where(first_head, outs[0][1], outs[1][1])
        probs(i, buf).start()

    loop(pairs, attention_step)
    store(ref.vattn, ref.attn)
    store(ref.vlinv, ref.linv)

    for copy in loads[4:]:
        copy.wait()
    unit, rstd = norm_parts(ref.vpool[...] + mm(ref.vattn[...], ref.vwo[...]))
    mixed = unit * wide(ref.g1[...]).reshape(1, width)
    ref.vunit[...] = unit.astype(BF)
    ref.vrstd[...] = jnp.broadcast_to(rstd, ref.vrstd.shape)
    ref.vacc[...] = mixed
    short = mixed.astype(BF)
    ref.vmix[...] = short
    ref.vmt[...] = short.T
    store(ref.vunit, ref.unit)
    store(ref.vrstd, ref.rstd)
    store(ref.vmt, ref.mixed)

    def slopes(j, buf):
        cols = pl.ds(pl.multiple_of(j * FFC, FFC), FFC)
        return [
            pltpu.make_async_copy(ref.vslope.at[buf], ref.slope.at[:, cols], ref.wsem.at[3, buf]),
            pltpu.make_async_copy(ref.vactt.at[buf], ref.actt.at[cols, :], ref.wsem.at[1, buf]),
        ]

    def feed_step(j):
        buf = lax.rem(j, 2)
        cols = pl.ds(pl.multiple_of(j * FFC, FFC), FFC)

        @pl.when(j >= 2)
        def free():
            for copy in slopes(j - 2, buf):
                copy.wait()

        pre = mm(ref.vmix[...], ref.vwin[:, cols])
        cdf = 0.5 * (1.0 + lax.erf(pre * 0.7071067811865476))
        act = (pre * cdf).astype(BF)
        ref.vslope[buf] = (
            cdf + pre * (jnp.exp(pre * pre * -0.5) * 0.3989422804014327)
        ).astype(BF)
        ref.vacc[...] += mm(act, ref.vwout[cols, :])
        ref.vactt[buf] = act.T
        for copy in slopes(j, buf):
            copy.start()

    loop(steps, feed_step)
    mate(*cot, True).wait_recv()
    own[1].wait()
    for rel in near + far:
        for copy in arrivals(*cot, rel):
            copy.wait_recv()
    unit, rstd = norm_parts(ref.vacc[...])
    valid = wide(2 * lax.broadcasted_iota(I32, (half, 1), 0)) < limit
    g2 = wide(ref.g2[...]).reshape(1, width)
    ref.vrows[...] = jnp.where(valid, unit * g2, 0.0).astype(BF)
    store(ref.vrows, ref.rows)
    grad = jnp.where(valid, wide(ref.vcot[...]), 0.0)
    ref.dgain[...] = jnp.sum(grad * unit, 0, keepdims=True)
    two = norm_back(grad, unit, rstd, g2)
    ref.vgo[...] = two.astype(BF)
    store(ref.vgo, ref.gouter)

    for i in (pairs - 2, pairs - 1):
        probs(i, i % 2).wait()
    for j in (steps - 2, steps - 1):
        for copy in slopes(j, j % 2):
            copy.wait()
    for copy in stores:
        copy.wait()
    for bank in (hid, cot):
        mate(*bank, False).wait_send()
        for rel in near + far:
            for copy in blocks(*bank, rel):
                copy.wait_send()


def forward(args, seq, grp):
    count, part, width = args["hidden"].shape
    slot = part * seq
    half = slot // 2
    inner = args["wout"].shape[0]
    heads = width // 64
    vm = pltpu.VMEM
    scratch = dict(
        vx=vm((slot, width), BF),
        vcot=vm((half, width), BF),
        vwq=vm((width, width), BF),
        vwk=vm((width, width), BF),
        vwv=vm((width, width), BF),
        vrel=vm((heads, 64, 64), BF),
        vwo=vm((width, width), BF),
        vwin=vm((width, inner), BF),
        vwout=vm((inner, width), BF),
        vcos=vm((half, 128), F32),
        vsin=vm((half, 128), F32),
        vfeat=vm((slot, 128), BF),
        vbd=vm((width // 256, 256, 256), BF),
        vq=vm((half, width), BF),
        vk=vm((slot, width), BF),
        vv=vm((slot, width), BF),
        vpool=vm((half, width), F32),
        vxt=vm((width, slot), BF),
        vpt=vm((width, half), BF),
        vsh=vm((half, 128), BF),
        vp=vm((2, 2, half, slot), BF),
        vattn=vm((half, width), BF),
        vlinv=vm((half, width), F32),
        vunit=vm((half, width), BF),
        vrstd=vm((half, 128), F32),
        vacc=vm((half, width), F32),
        vmix=vm((half, width), BF),
        vmt=vm((width, half), BF),
        vslope=vm((2, half, FFC), BF),
        vactt=vm((2, FFC, half), BF),
        vrows=vm((half, width), BF),
        vgo=vm((half, width), BF),
        lsem=pltpu.SemaphoreType.DMA((7,)),
        wsem=pltpu.SemaphoreType.DMA((4, 2)),
        ssem=pltpu.SemaphoreType.DMA((24,)),
        osem=pltpu.SemaphoreType.DMA((2,)),
        asend=pltpu.SemaphoreType.DMA((2, seq)),
        arecv=pltpu.SemaphoreType.DMA((2, seq)),
    )
    names = list(scratch)
    shapes = dict(
        attn=sds((half, width), BF),
        linv=sds((half, width), F32),
        p=sds((heads, half, slot), BF),
        q=sds((half, width), BF),
        k=sds((slot, width), BF),
        v=sds((slot, width), BF),
        xt=sds((width, slot), BF),
        pt=sds((width, half), BF),
        bd=sds((width // 256, 256, 256), BF),
        cos=sds((half, 128), F32),
        sin=sds((half, 128), F32),
        feat=sds((slot, 128), BF),
        rows=sds((half, width), BF),
        slope=sds((half, inner), BF),
        gouter=sds((half, width), BF),
        unit=sds((half, width), BF),
        rstd=sds((half, 128), F32),
        mixed=sds((width, half), BF),
        actt=sds((inner, half), BF),
        dgain=sds((1, width), F32),
    )
    hbm = pl.BlockSpec(memory_space=pl.ANY)
    vmem = pl.BlockSpec(memory_space=pltpu.VMEM)
    spots = dict(g1=vmem, g2=vmem, lengths=vmem)
    outs = pl.pallas_call(
        functools.partial(fore_body, names, (seq, grp)),
        out_shape=[shapes[n] for n in FORE_OUTPUTS],
        in_specs=[spots.get(n, hbm) for n in FORE_INPUTS],
        out_specs=[hbm] * (len(FORE_OUTPUTS) - 1) + [vmem],
        scratch_shapes=list(scratch.values()),
        compiler_params=pltpu.CompilerParams(
            collective_id=0, has_side_effects=True, vmem_limit_bytes=63 << 20
        ),
        cost_estimate=pl.CostEstimate(
            flops=20_000_000_000, bytes_accessed=60_000_000, transcendentals=0
        ),
    )(*[args[n] for n in FORE_INPUTS])
    return dict(zip(FORE_OUTPUTS, outs))


def is_early(name, rows, grp):
    return name in EARLY and grp == 4 and (rows // grp) % 16 == 0


def place_of(z, g, grp):
    if grp != 4:
        return g
    rel = xor(z, g, 4)
    return 2 * lax.rem(rel, 2) + lax.div(rel, 2)


class Chunk:
    def __init__(self, env, index, order, early, keep, send, recv, zbuf, recvz, out):
        self.env, self.index, self.order, self.early = env, index, order, early
        self.keep, self.send, self.recv = keep, send, recv
        self.zbuf, self.recvz, self.out = zbuf, recvz, out

    def remote(self, slot, src, dst, device):
        return pltpu.make_async_remote_copy(
            src_ref=src,
            dst_ref=dst,
            send_sem=self.env.ssem.at[self.index, slot],
            recv_sem=self.env.rsem.at[self.index, slot],
            device_id=device,
            device_id_type=MESH,
        )

    def seq_copy(self, stage):
        device = {"seq": xor(self.env.me, self.order[stage], self.env.seq)}
        if stage == 0:
            src = self.send
        else:
            half = 4 >> stage
            src = (self.zbuf if self.early else self.recv[0]).at[pl.ds(half, half)]
        return self.remote(stage, src, self.recv[stage], device)

    def z_copies(self):
        grp, z = self.env.grp, self.env.z
        copies = []
        for d in range(1, grp):
            peer = lax.rem(z + d, grp)
            copies.append(
                self.remote(2 + d, self.zbuf.at[peer], self.recvz.at[d - 1], {"grp": peer})
            )
        return copies

    def z_copy(self, stage):
        half = 2 >> stage
        src = (self.recv[0] if self.early else self.zbuf).at[pl.ds(half, half)]
        dst = self.recvz.at[pl.ds(2 * stage, half)]
        return self.remote(3 + stage, src, dst, {"grp": xor(self.env.z, 1 << stage, 4)})

    def unit(self):
        return 48 if self.keep.shape[1] % 48 == 0 else 64

    def step(self, n):
        keep, (recv0, recv1, recv2) = self.keep, self.recv
        zbuf, recvz, grp, z = self.zbuf, self.recvz, self.env.grp, self.env.z
        if n == 0:
            self.seq_copy(0).start()
        elif n == 1 and self.early:
            self.seq_copy(0).wait()

            def add(i):
                s, p = 2 + lax.div(i, 4), lax.rem(i, 4)
                recv0[s, p] = (wide(keep[s, p]) + wide(recv0[s, p])).astype(BF)

            loop(8, add)
            self.z_copy(0).start()
        elif n == 2 and self.early:
            self.z_copy(0).wait()

            def add(p):
                recv0[1, p] = (wide(keep[1, p]) + wide(recv0[1, p]) + wide(recvz[1, p])).astype(BF)

            loop(4, add)
            self.z_copy(1).start()
        elif n == 3 and self.early:
            self.z_copy(1).wait()

            def add(p):
                total = wide(keep[0, p]) + wide(recv0[0, p]) + wide(recvz[0, p])
                zbuf[p] = (total + wide(recvz[2, p])).astype(BF)

            loop(4, add)
            self.seq_copy(1).start()
        elif n == 4 and self.early:
            self.seq_copy(1).wait()
            zbuf[1] = (wide(zbuf[1]) + wide(recv1[1])).astype(BF)
            self.seq_copy(2).start()
        elif n == 5 and self.early:
            self.seq_copy(2).wait()
            self.out(wide(zbuf[0]) + wide(recv1[0]) + wide(recv2[0]))
        elif n == 1:
            self.seq_copy(0).wait()
            unit = self.unit()
            parts = keep.shape[1] // unit

            def add(i):
                start = pl.multiple_of(unit * lax.rem(i, parts), unit)
                p, rows = 2 + lax.div(i, parts), pl.ds(start, unit)
                recv0[p, rows] = (wide(keep[p, rows]) + wide(recv0[p, rows])).astype(BF)

            loop(2 * parts, add)
            self.seq_copy(1).start()
        elif n == 2:
            self.seq_copy(1).wait()

            unit = self.unit()

            def add(i):
                rows = pl.ds(pl.multiple_of(unit * i, unit), unit)
                recv0[1, rows] = (
                    wide(keep[1, rows]) + wide(recv0[1, rows]) + wide(recv1[1, rows])
                ).astype(BF)

            loop(keep.shape[1] // unit, add)
            self.seq_copy(2).start()
        elif n == 3:
            self.seq_copy(2).wait()
            share = keep.shape[1] // grp
            unit = self.unit()
            for start in range(0, keep.shape[1], unit):
                rows = slice(start, start + unit)
                total = (
                    wide(keep[0, rows]) + wide(recv0[0, rows])
                    + wide(recv1[0, rows]) + wide(recv2[0, rows])
                )
                size = min(share, unit)
                for low in range(start, start + unit, size):
                    g, inside = place_of(z, low // share, grp), low % share
                    piece = total[low - start : low - start + size].astype(BF)
                    if zbuf.shape[1] == share:
                        zbuf[g, inside : inside + size] = piece
                    else:
                        mid = zbuf.shape[2]
                        zbuf[g, :share] = piece[:, :mid]
                        zbuf[g, share:] = piece[:, mid:]
            if grp == 4:
                self.z_copy(0).start()
            else:
                for copy in self.z_copies():
                    copy.start()
        elif n == 4:
            if grp == 4:
                self.z_copy(0).wait()
                zbuf[1] = (wide(zbuf[1]) + wide(recvz[1])).astype(BF)
                self.z_copy(1).start()
        else:
            if grp == 4:
                self.z_copy(1).wait()
                total = wide(zbuf[0]) + wide(recvz[0]) + wide(recvz[2])
            else:
                for copy in self.z_copies():
                    copy.wait()
                total = wide(zbuf[z])
                for d in range(grp - 1):
                    total = total + wide(recvz[d])
            share = keep.shape[1] // grp
            if zbuf.shape[1] != share:
                total = jnp.concatenate([total[:share], total[share:]], 1)
            self.out(total)


BACK_INPUTS = list(
    dict(
        gouter=0, slope=0, wout=0, win=0, mixed=0, actt=0, unit=0, rstd=0, g1=0, wo=0, attn=0,
        p=0, q=0, k=0, v=0, linv=0, xt=0, pt=0, bd=0, cos=0, sin=0, feat=0, wq=0, wk=0, wv=0,
        rows=0, dgain2=0,
    )
)
BACK_OUTPUTS = list(
    dict(hidden=0, pooled=0, inner=0, outer=0, out=0, query=0, key=0, value=0, small=0)
)
POINTS = {
    ("X", 0): [("P", 0)],
    ("B", 1): [("I0", 0), ("O1", 1)],
    ("B", 2): [("I0", 1)],
    ("B", 3): [("I1", 0)],
    ("B", 5): [("I2", 0), ("O2", 1), ("I1", 1), ("O0", 1), ("I2", 1), ("P", 1)],
    ("U", 0): [("W", 0), ("I0", 2), ("O1", 2)],
    ("U", 1): [("G0", 0), ("W", 1), ("O2", 2), ("I1", 2), ("I2", 2), ("G0", 1)],
    ("U", 3): [("G1", 0)],
    ("U", 4): [("W", 2), ("G1", 1)],
    ("U", 5): [
        ("G2", 0), ("G2", 1), ("R", 0), ("G0", 2), ("O1", 3), ("R", 1), ("O0", 2), ("W", 3),
        ("I2", 3), ("O2", 3),
    ],
    ("T", 0): [("G1", 2), ("R", 2)],
    ("T", 1): [
        ("O1", 4), ("R", 3), ("I0", 3), ("G0", 3), ("O0", 3), ("G2", 2), ("I1", 3), ("O2", 4),
        ("I2", 4),
    ],
    ("T", 2): [("G0", 4)],
    ("T", 3): [
        ("R", 4), ("G1", 3), ("W", 4), ("I2", 5), ("O0", 4), ("R", 5), ("A", 0), ("I0", 4),
        ("I1", 4), ("G0", 5), ("W", 5), ("G2", 3), ("I0", 5), ("G1", 4), ("A", 1), ("G2", 4),
        ("O0", 5), ("I1", 5), ("O2", 5), ("G1", 5), ("O1", 5), ("G2", 5), ("H", 1), ("A", 2),
    ],
}


def back_body(names, sizes, *refs):
    every = dict(zip(BACK_INPUTS + BACK_OUTPUTS + names, refs))
    ref = types.SimpleNamespace(**every)
    seq, grp = sizes
    me = lax.axis_index("seq")
    z = lax.axis_index("grp")
    env = types.SimpleNamespace(me=me, z=z, seq=seq, grp=grp, ssem=ref.ssem, rsem=ref.rsem)
    half, width = ref.vgo.shape
    slot = 2 * half
    inner = ref.slope.shape[1]
    steps = inner // FFC
    pairs = width // 128
    groups = width // 256
    lsem = ref.lsem

    plain = [
        (ref.gouter, ref.vgo), (ref.mixed, ref.vmt),
        (ref.unit, ref.vunit), (ref.rstd, ref.vrs), (ref.wo, ref.vwo), (ref.attn, ref.vat),
        (ref.linv, ref.vlinv),
        (ref.q, ref.vq), (ref.k, ref.vk), (ref.v, ref.vv), (ref.feat, ref.vfeat),
        (ref.cos, ref.vcos), (ref.sin, ref.vsin), (ref.bd, ref.vbd), (ref.xt, ref.vxt),
        (ref.pt, ref.vmt),
        (ref.wq, ref.vwo), (ref.wk, ref.vwout.at[0]), (ref.wv, ref.vwout.at[1]),
    ]
    local = [pltpu.make_async_copy(*pair, lsem.at[i]) for i, pair in enumerate(plain)]

    def act_room(buf):
        return ref.vds.at[pl.ds(0, inner // seq), pl.ds(pl.multiple_of(half * buf, half), half)]

    def act_rows(pos, buf):
        bits = [lax.div(pos, 4), lax.rem(lax.div(pos, 2), 2), lax.rem(pos, 2)]
        rows = inner // seq
        start = xor(me, bits[0] + 2 * bits[1] + 4 * bits[2], seq) * rows
        return pltpu.make_async_copy(
            ref.actt.at[pl.ds(pl.multiple_of(start, rows), rows)], act_room(buf),
            ref.wsem.at[0, buf],
        )

    def weights(j, buf):
        cols = pl.ds(pl.multiple_of(j * FFC, FFC), FFC)
        return [
            pltpu.make_async_copy(ref.slope.at[:, cols], ref.vslope.at[buf], ref.wsem.at[4, buf]),
            pltpu.make_async_copy(ref.wout.at[cols, :], ref.vwout.at[buf, pl.ds(0, FFC)], ref.wsem.at[1, buf]),
            pltpu.make_async_copy(ref.win.at[:, cols], ref.vwin.at[buf], ref.wsem.at[2, buf]),
        ]

    def probs(i, buf):
        return pltpu.make_async_copy(
            ref.p.at[pl.ds(2 * i, 2)], ref.vp.at[buf], ref.wsem.at[3, buf]
        )

    chunks = {}
    results = []

    def out_cols(room, dst, start, stop, first=0):
        copy = pltpu.make_async_copy(
            room.at[:, pl.ds(start, stop - start)], dst.at[:, pl.ds(start, stop - start)],
            ref.fsem.at[len(results)],
        )
        results.append(copy)

        def put(value):
            room[:, start:stop] = value[:, first : first + stop - start]
            copy.start()

        return put

    def out_three(g):
        rooms = (ref.xq, ref.query), (ref.xk, ref.key), (ref.xv, ref.value)
        puts = [
            out_cols(*pair, 256 * g, 256 * (g + 1), 256 * i) for i, pair in enumerate(rooms)
        ]

        def put(value):
            for each in puts:
                each(value)

        return put

    def out_small(value):
        ref.vres[...] = value

    for index, (name, order) in enumerate(ORDERS.items()):
        early = is_early(name, inner // seq, grp)
        kind = name[0]
        n = int(name[1]) if len(name) > 1 else 0
        recv = [every[name + "r0"], every[name + "r1"], every[name + "r2"]]
        if kind == "O":
            keep, send = every[name + "k"], every[name + "s"]
            span = width // OCHUNKS
            out = out_cols(ref.xouter, ref.outer, span * n, span * (n + 1))
        elif kind == "I":
            keep, send = ref.ikeep.at[n], ref.isend.at[n]
            out = out_cols(ref.xinner, ref.inner, 1024 * n, 1024 * (n + 1))
        elif kind == "W":
            keep, send = ref.wkeep, ref.wsend
            out = out_cols(ref.xout, ref.out, 0, width)
        elif kind == "R":
            keep, send = ref.rkeep, ref.rsend
            out = out_small
        else:
            keep, send = ref.gkeep.at[n], ref.gsend.at[n]
            out = out_three(n)
        chunks[name] = Chunk(
            env, index, order, early, keep, send, recv, every[name + "z"], every[name + "rz"], out
        )

    def spread(src, dst, sem):
        size = dst.shape[1]
        block = lambda b: src.at[pl.ds(pl.multiple_of(b * size, size), size)]
        copies = [pltpu.make_async_copy(block(me), dst.at[me], ref.dsem.at[sem])]
        for k in range(1, seq):
            peer = lax.rem(me + k, seq)
            copies.append(
                pltpu.make_async_remote_copy(
                    src_ref=block(peer),
                    dst_ref=dst.at[me],
                    send_sem=ref.asend.at[sem, k],
                    recv_sem=ref.arecv.at[sem, k],
                    device_id={"seq": peer},
                    device_id_type=MESH,
                )
            )
        return copies

    chip, core = lax.div(me, 2), lax.rem(me, 2)
    part = slot // seq
    rows_at = lambda rank: pl.ds(pl.multiple_of(rank * part, part), part)
    own_rows = pltpu.make_async_copy(ref.vk.at[rows_at(me)], ref.hidden.at[me], ref.dsem.at[1])

    def home(rel, receive):
        copies = []
        for c in range(2 if rel else 1):
            rank = 2 * xor(chip, rel, 4) + c
            if rel == 0:
                rank = 2 * chip + 1 - core
            copies.append(
                pltpu.make_async_remote_copy(
                    src_ref=ref.vk.at[rows_at(rank)],
                    dst_ref=ref.hidden.at[rank if receive else me],
                    send_sem=ref.asend.at[1, 2 * rel + c],
                    recv_sem=ref.arecv.at[1, 0 if rel == 0 else 2 * rel + (c if receive else core)],
                    device_id={"seq": rank},
                    device_id_type=MESH,
                )
            )
        if rel == 0:
            copies = copies[:1] if receive else [copies[0], own_rows]
        return copies

    def gather(stage):
        copies = []
        if stage == 0:
            pairs_of = [(lax.rem(z + k, grp), "grp", grp, z) for k in range(1, grp)]
            src, dst = ref.vres, ref.vag.at[z]
        else:
            pairs_of = [(lax.rem(me + k, seq), "seq", seq, me) for k in range(1, seq)]
            src, dst = ref.vag, ref.vall.at[me]
        for k, (peer, axis, size, rank) in enumerate(pairs_of):
            copies.append(
                pltpu.make_async_remote_copy(
                    src_ref=src,
                    dst_ref=dst,
                    send_sem=ref.msend.at[stage, k],
                    recv_sem=ref.mrecv.at[stage, k],
                    device_id={axis: peer},
                    device_id_type=MESH,
                )
            )
        return copies

    def gather_step(n):
        if n > 0:
            for copy in gather(n - 1):
                copy.wait()
        if n == 0:
            ref.vag[z] = ref.vres[...]
        elif n == 1:
            ref.vall[me] = ref.vag[...]
        if n < 2:
            for copy in gather(n):
                copy.start()
        else:
            spot = pltpu.make_async_copy(ref.vall, ref.small, ref.dsem.at[2])
            spot.start()
            spot.wait()

    def place_small():
        size = ref.vsm.shape[0] // seq
        for pos in range(seq):
            block = ref.vsm[pl.ds(pl.multiple_of(xor(me, rel_of(pos, ORDERS["R"]), seq) * size, size), size), :]
            (ref.rkeep if pos < seq // 2 else ref.rsend)[pos % (seq // 2)] = block.astype(BF)

    def event(name, n):
        if name == "P":
            for copy in spread(ref.rows, ref.pooled, 0):
                copy.start() if n == 0 else copy.wait()
        elif name == "H":
            for rel in range(4):
                for copy in home(rel, False):
                    copy.wait_send() if copy is not own_rows else copy.wait()
                for copy in home(rel, True):
                    copy.wait_recv()
        elif name == "A":
            gather_step(n)
        else:
            if name == "R" and n == 0:
                place_small()
            chunks[name].step(n)

    def point(kind, index, dynamic=None):
        todo = POINTS.get((kind, index), [])
        if not todo:
            return
        if dynamic is None:
            for name, n in todo:
                event(name, n)
        else:

            @pl.when(dynamic == index)
            def run():
                for name, n in todo:
                    event(name, n)

    barrier = pltpu.get_barrier_semaphore()
    for k in range(1, seq):
        pl.semaphore_signal(
            barrier, inc=1, device_id={"seq": lax.rem(me + k, seq)}, device_id_type=MESH
        )
    for k in range(1, grp):
        pl.semaphore_signal(
            barrier, inc=1, device_id={"grp": lax.rem(z + k, grp)}, device_id_type=MESH
        )
    for copy in local[:2]:
        copy.start()
    act_rows(4, 0).start()
    act_rows(5, 1).start()
    for copy in weights(0, 0):
        copy.start()
    pl.semaphore_wait(barrier, seq + grp - 2)
    point("X", 0)
    local[0].wait()

    def outer_step(i):
        pos, buf = lax.rem(i + 4, 8), lax.rem(i, 2)
        act_rows(pos, buf).wait()
        value = mm(act_room(buf)[...], ref.vgo[...])

        @pl.when(i + 2 < seq)
        def more():
            act_rows(lax.rem(i + 6, 8), buf).start()

        first, second = lax.rem(lax.div(pos, 2), 2), lax.rem(pos, 2)
        span = width // OCHUNKS
        for half_of in range(2):

            @pl.when(lax.div(pos, 4) == half_of)
            def place():
                for n in range(OCHUNKS):
                    name = "O" + str(n)
                    spot = 2 * first + second if ORDERS[name][1] == 2 else 2 * second + first
                    room = every[name + ("s" if half_of else "k")]
                    piece = value[:, span * n : span * (n + 1)]
                    if is_early(name, inner // seq, grp):
                        size = piece.shape[0] // grp
                        for g in range(grp):
                            room[place_of(z, g, grp), spot] = piece[
                                size * g : size * (g + 1)
                            ].astype(BF)
                    else:
                        room[spot] = piece.astype(BF)

        @pl.when(i == 3)
        def go():
            for n in range(OCHUNKS):
                chunks["O" + str(n)].step(0)

    loop(seq, outer_step)
    local[1].wait()
    ref.vacc[...] = wide(ref.vgo[...])
    point("Q", 0)

    def rows_of(count, rel):
        step = width // seq
        return pl.ds(pl.multiple_of(xor(me, rel, seq) * step, step), step)

    def split(order, cols, keep, send):
        for pos in range(seq):
            block = ref.vval[rows_of(width, rel_of(pos, order)), cols]
            (keep if pos < seq // 2 else send)(pos % (seq // 2), block)

    def feed_step(j):
        buf = lax.rem(j, 2)
        for copy in weights(j, buf):
            copy.wait()

        @pl.when(j + 1 < steps)
        def more():
            for copy in weights(j + 1, 1 - buf):
                copy.start()

        @pl.when(j == 1)
        def rest():
            for copy in local[2:-4]:
                copy.start()
            probs(0, 0).start()

        grad = mm_nt(ref.vgo[...], ref.vwout[buf, :FFC])
        hid = (wide(ref.vslope[buf]) * grad).astype(BF)
        ref.vacc[...] += mm_nt(hid, ref.vwin[buf])
        ref.vval[:, :FFC] = mm(ref.vmt[...], hid).astype(BF)
        c = lax.div(j, 2)
        cols = pl.ds(pl.multiple_of(lax.rem(j, 2) * FFC, FFC), FFC)

        def keep(pos, block):
            ref.ikeep[c, pos, :, cols] = block

        def send(pos, block):
            ref.isend[c, pos, :, cols] = block

        for n in range(steps // 2):

            @pl.when(c == n)
            def place():
                split(ORDERS["I" + str(n)], slice(0, FFC), keep, send)

        for t in range(steps):
            point("B", t, j)

    loop(steps, feed_step)

    for copy in (local[-4], local[-2], local[-1]):
        copy.start()
    for copy in local[2:7]:
        copy.wait()
    grad = ref.vacc[...]
    unit = wide(ref.vunit[...])
    small = ref.vsm
    dgain = jnp.sum(grad * unit, 0, keepdims=True)
    for i in range(pairs):
        small[64 * pairs + i, :] = dgain[0, 128 * i : 128 * (i + 1)]
        small[64 * pairs + pairs + i, :] = ref.dgain2[0, 128 * i : 128 * (i + 1)]
    used = 66 * pairs
    small[used:, :] = jnp.zeros((small.shape[0] - used, 128), F32)
    one = norm_back(grad, unit, ref.vrs[:, :1], wide(ref.g1[...]).reshape(1, width))
    ref.vun[...] = one
    branch = one.astype(BF)
    attn = ref.vat[...]
    ref.vval[...] = mm_tn(attn, branch).astype(BF)

    def keep_w(pos, block):
        ref.wkeep[pos] = block

    def send_w(pos, block):
        ref.wsend[pos] = block

    split(ORDERS["W"], slice(0, width), keep_w, send_w)
    scaled = mm_nt(branch, ref.vwo[...]) * ref.vlinv[...]
    ref.vgo[...] = scaled.astype(BF)
    ref.vacc[...] = scaled * wide(attn)
    local[-3].start()
    for copy in local[7:-3]:
        copy.wait()
    point("L", 0)

    lane = lax.broadcasted_iota(I32, (1, 128), 1)
    low = lax.rem(lane, 64) < 32
    first_head = lane < 64
    ones = jnp.broadcast_to(jnp.where(lane < 2, 1.0, 0.0).astype(BF), (slot, 128))

    def attention_step(i):
        buf = lax.rem(i, 2)
        g = lax.div(i, 2)
        probs(i, buf).wait()

        @pl.when(i + 1 < pairs)
        def more():
            probs(i + 1, 1 - buf).start()

        cols = pl.ds(pl.multiple_of(i * 128, 128), 128)
        part = pl.ds(pl.multiple_of(buf * 128, 128), 128)
        ref.vqt[...] = ref.vq[:, cols].T
        ref.vgt[...] = ref.vgo[:, cols].T
        key_side = jnp.concatenate([ref.vk[:, cols], ref.vfeat[...]], 1)
        value_side = jnp.concatenate([ref.vv[:, cols], ones], 1)
        outs = [[], []]
        for h in range(2):
            mine = first_head if h == 0 else jnp.logical_not(first_head)
            for t in range(half // QT):
                rows = slice(QT * t, QT * (t + 1))
                g_part = ref.vgo[rows, cols]
                delta = jnp.sum(jnp.where(mine, ref.vacc[rows, cols], 0.0), -1, keepdims=True)
                coarse = wide(delta.astype(BF))
                tail = jnp.where(lane == 0, coarse, jnp.where(lane == 1, delta - coarse, 0.0))
                left = jnp.concatenate(
                    [jnp.where(mine, g_part, jnp.zeros_like(g_part)), (-tail).astype(BF)], 1
                )
                ds = (wide(ref.vp[buf, h, rows, :]) * mm_nt(left, value_side)).astype(BF)
                ref.vds[rows, :] = ds
                outs[h].append(mm(ds, key_side))
            lines = slice(64 * h, 64 * (h + 1))
            ref.vkt[lines, :] = (mm(ref.vqt[lines, :], ref.vds[...]) * 0.125).astype(BF)
            ref.vvt[lines, :] = mm(ref.vgt[lines, :], ref.vp[buf, h]).astype(BF)
        for t in range(half // QT):
            rows = slice(QT * t, QT * (t + 1))
            a, b = outs[0][t], outs[1][t]
            ref.vgqf[rows, part] = jnp.where(first_head, a[:, :128], b[:, :128]) * 0.125
            shift = jnp.where(first_head, a[:, 128:], b[:, 128:]) * 0.125
            other = jnp.where(low, -pltpu.roll(shift, 96, 1), pltpu.roll(shift, 32, 1))
            ref.vrel[rows, part] = (
                shift * ref.vcos[rows, :] + other * ref.vsin[rows, :]
            ).astype(BF)
        ref.vk[:, cols] = ref.vkt[...].T
        ref.vv[:, cols] = ref.vvt[...].T
        both = mm(ref.vqt[...], ref.vrel[:, part])
        small[pl.ds(pl.multiple_of(64 * i, 64), 64), :] = jnp.where(first_head, both[:64], both[64:])

        @pl.when(buf == 1)
        def tail():
            wide_cols = pl.ds(pl.multiple_of(g * 256, 256), 256)
            gq = (ref.vgqf[...] + mm_nt(ref.vrel[...], ref.vbd[g])).astype(BF)
            ref.vq[:, wide_cols] = gq
            dk = ref.vk[:, wide_cols]
            dv = ref.vv[:, wide_cols]
            ref.vval[:, 0:256] = mm(ref.vmt[...], gq).astype(BF)
            ref.vval[:, 256:512] = mm(ref.vxt[...], dk).astype(BF)
            ref.vval[:, 512:768] = mm(ref.vxt[...], dv).astype(BF)

            def keep(pos, block):
                ref.gkeep[g, pos] = block

            def send(pos, block):
                ref.gsend[g, pos] = block

            for n in range(groups):

                @pl.when(g == n)
                def place():
                    split(ORDERS["G" + str(n)], slice(0, 768), keep, send)

        for t in range(pairs):
            point("U", t, i)

    loop(pairs, attention_step)

    for copy in local[-3:]:
        copy.wait()
    spread_m = wide(pool_matrix(128)).T.astype(BF)

    def token_step(t):
        small_rows = pl.ds(pl.multiple_of(128 * t, 128), 128)
        rows = pl.ds(pl.multiple_of(256 * t, 256), 256)
        pooled = ref.vun[small_rows, :] + mm_nt(ref.vq[small_rows, :], ref.vwo[...])
        high = pooled.astype(BF)
        rest = (pooled - wide(high)).astype(BF)
        acc = mm(spread_m, high) + mm(spread_m, rest)
        acc = acc + mm_nt(ref.vk[rows, :], ref.vwout[0])
        acc = (acc + mm_nt(ref.vv[rows, :], ref.vwout[1])).astype(BF)
        ref.vk[rows, :] = acc

    for i, rel in enumerate((1, 2, 3, 0)):
        token_step(xor(chip, rel, 4))
        for copy in home(rel, False):
            copy.start()
        point("T", i)
    for copy in results:
        copy.wait()


def backward(args, seq, grp):
    half, width = args["gouter"].shape
    slot = 2 * half
    inner = args["slope"].shape[1]
    part = slot // seq
    share = width // seq
    small_rows = seq * 64 * -(-66 * (width // 128) // (seq * 64))
    assert small_rows % (seq * grp) == 0
    vm = pltpu.VMEM
    scratch = dict(
        vgo=vm((half, width), BF),
        vmt=vm((width, half), BF),
        vacc=vm((half, width), F32),
        vun=vm((half, width), F32),
        vrs=vm((half, 128), F32),
        vwo=vm((width, width), BF),
        vat=vm((half, width), BF),
        vslope=vm((2, half, FFC), BF),
        vwout=vm((2, width, width), BF),
        vwin=vm((2, width, FFC), BF),
        vval=vm((width, 768), BF),
        vp=vm((2, 2, half, slot), BF),
        vq=vm((half, width), BF),
        vk=vm((slot, width), BF),
        vv=vm((slot, width), BF),
        vlinv=vm((half, width), F32),
        vxt=vm((width, slot), BF),
        vbd=vm(args["bd"].shape, BF),
        vcos=vm((half, 128), F32),
        vsin=vm((half, 128), F32),
        vfeat=vm((slot, 128), BF),
        vqt=vm((128, half), BF),
        vgt=vm((128, half), BF),
        vgqf=vm((half, 256), F32),
        vrel=vm((half, 256), BF),
        vds=vm((half, slot), BF),
        vkt=vm((128, slot), BF),
        vvt=vm((128, slot), BF),
        vunit=vm((half, width), BF),
        vsm=vm((small_rows, 128), F32),
        vres=vm((small_rows // (seq * grp), 128), F32),
        vag=vm((grp, small_rows // (seq * grp), 128), F32),
        vall=vm((seq, grp, small_rows // (seq * grp), 128), F32),
        rkeep=vm((4, small_rows // seq, 128), BF),
        rsend=vm((4, small_rows // seq, 128), BF),
        ikeep=vm((3, 4, share, 1024), BF),
        isend=vm((3, 4, share, 1024), BF),
        wkeep=vm((4, share, width), BF),
        wsend=vm((4, share, width), BF),
        gkeep=vm((3, 4, share, 768), BF),
        gsend=vm((3, 4, share, 768), BF),
        lsem=pltpu.SemaphoreType.DMA((24,)),
        wsem=pltpu.SemaphoreType.DMA((5, 2)),
        dsem=pltpu.SemaphoreType.DMA((3,)),
        fsem=pltpu.SemaphoreType.DMA((20,)),
        asend=pltpu.SemaphoreType.DMA((2, seq)),
        arecv=pltpu.SemaphoreType.DMA((2, seq)),
        msend=pltpu.SemaphoreType.DMA((2, max(seq, grp))),
        mrecv=pltpu.SemaphoreType.DMA((2, max(seq, grp))),
        ssem=pltpu.SemaphoreType.DMA((len(ORDERS), 2 + grp)),
        rsem=pltpu.SemaphoreType.DMA((len(ORDERS), 2 + grp)),
    )
    tall = inner // seq
    for name in ORDERS:
        rows, cols = share, width
        if name[0] == "O":
            rows, cols = tall, width // OCHUNKS
        elif name[0] == "I":
            cols = 1024
        elif name == "R":
            rows, cols = small_rows // seq, 128
        z_rows = rows // grp
        if is_early(name, tall, grp):
            scratch[name + "k"] = vm((4, grp, z_rows, cols), BF)
            scratch[name + "s"] = vm((4, grp, z_rows, cols), BF)
            scratch[name + "r0"] = vm((4, grp, z_rows, cols), BF)
            scratch[name + "r1"] = vm((2, z_rows, cols), BF)
            scratch[name + "r2"] = vm((1, z_rows, cols), BF)
            scratch[name + "z"] = vm((4, z_rows, cols), BF)
            scratch[name + "rz"] = vm((grp - 1, 4, z_rows, cols), BF)
        else:
            if name[0] == "O":
                scratch[name + "k"] = vm((4, rows, cols), BF)
                scratch[name + "s"] = vm((4, rows, cols), BF)
            scratch[name + "r0"] = vm((4, rows, cols), BF)
            scratch[name + "r1"] = vm((2, rows, cols), BF)
            scratch[name + "r2"] = vm((1, rows, cols), BF)
            fold = 1 if z_rows % 16 == 0 else 2
            scratch[name + "z"] = vm((grp, z_rows * fold, cols // fold), BF)
            scratch[name + "rz"] = vm((grp - 1, z_rows * fold, cols // fold), BF)
    scratch.update(
        xinner=vm((share // grp, inner), F32),
        xouter=vm((tall // grp, width), F32),
        xout=vm((share // grp, width), F32),
        xq=vm((share // grp, width), F32),
        xk=vm((share // grp, width), F32),
        xv=vm((share // grp, width), F32),
    )
    names = list(scratch)
    outs = [
        sds((seq, part, width), BF),
        sds((seq, part // 2, width), BF),
        sds((share // grp, inner), F32),
        sds((tall // grp, width), F32),
        sds((share // grp, width), F32),
        sds((share // grp, width), F32),
        sds((share // grp, width), F32),
        sds((share // grp, width), F32),
        sds((seq, grp, small_rows // (seq * grp), 128), F32),
    ]
    hbm = pl.BlockSpec(memory_space=pl.ANY)
    vmem = pl.BlockSpec(memory_space=pltpu.VMEM)
    in_vmem = ("g1", "dgain2")
    return pl.pallas_call(
        functools.partial(back_body, names, (seq, grp)),
        out_shape=outs,
        in_specs=[vmem if n in in_vmem else hbm for n in BACK_INPUTS],
        out_specs=[hbm] * len(outs),
        scratch_shapes=list(scratch.values()),
        compiler_params=pltpu.CompilerParams(
            collective_id=1, has_side_effects=True, vmem_limit_bytes=63 << 20
        ),
        cost_estimate=pl.CostEstimate(
            flops=30_000_000_000, bytes_accessed=60_000_000, transcendentals=0
        ),
    )(*[args[n] for n in BACK_INPUTS])


def pieces_of(shape):
    parts = 4 if len(shape) == 3 else 1
    size = shape[0] // parts
    return [pl.ds(i * size, size) for i in range(parts)]


def finish_body(count, *refs):
    srcs, small = refs[:count], refs[count]
    dsts = refs[count + 1 : 2 * count + 1]
    tails = refs[2 * count + 1 : 2 * count + 4]
    rooms = refs[2 * count + 4 : 3 * count + 4]
    held, rel, attn, ffn, sem, tail_sem = refs[3 * count + 4 :]
    head = pltpu.make_async_copy(small, held, tail_sem.at[3])
    head.start()
    loads, stores = [], []
    for src, room, dst in zip(srcs, rooms, dsts):
        for rows in pieces_of(src.shape):
            i = len(loads)
            loads.append(pltpu.make_async_copy(src.at[rows], room.at[rows], sem.at[0, i]))
            stores.append(pltpu.make_async_copy(room.at[rows], dst.at[rows], sem.at[1, i]))
            loads[-1].start()
    pairs = attn.shape[0] // 128
    head.wait()
    for i in range(pairs):
        both = held[64 * i : 64 * (i + 1), :]
        rel[2 * i] = both[:, :64]
        rel[2 * i + 1] = both[:, 64:]
        attn[pl.ds(128 * i, 128)] = held[64 * pairs + i, :]
        ffn[pl.ds(128 * i, 128)] = held[65 * pairs + i, :]
    for i, pair in enumerate(zip((rel, attn, ffn), tails)):
        stores.append(pltpu.make_async_copy(*pair, tail_sem.at[i]))
        stores[-1].start()
    for load, store in zip(loads, stores):
        load.wait()
        store.start()
    for copy in stores:
        copy.wait()


def finish(arrays, small, heads, width):
    count = len(arrays)
    hbm = pl.BlockSpec(memory_space=pltpu.HBM)
    tails = [sds((heads, 64, 64), F32), sds((width,), F32), sds((width,), F32)]
    total = sum(len(pieces_of(a.shape)) for a in arrays)
    return pl.pallas_call(
        functools.partial(finish_body, count),
        out_shape=[sds(a.shape, a.dtype) for a in arrays] + tails,
        in_specs=[hbm] * (count + 1),
        out_specs=[hbm] * (count + 3),
        scratch_shapes=[pltpu.VMEM(a.shape, a.dtype) for a in (*arrays, small, *tails)]
        + [pltpu.SemaphoreType.DMA((2, total)), pltpu.SemaphoreType.DMA((4,))],
        compiler_params=pltpu.CompilerParams(vmem_limit_bytes=63 << 20),
    )(*arrays, small)


def local(
    seq_size, grp_size, hidden, lengths, query_weight, key_weight, value_weight, w_rel,
    output_weight, gain_attn, inner_weight, outer_weight, gain_ffn, cotangent,
):
    micro, unused, seqs, part, width = hidden.shape
    count = micro * seqs
    assert count == seq_size == 8
    weights = dict(
        wq=query_weight, wk=key_weight, wv=value_weight, wo=output_weight, win=inner_weight,
        wout=outer_weight, g1=gain_attn, g2=gain_ffn,
    )
    kept = forward(
        dict(
            weights, hidden=hidden.reshape(count, part, width), w_rel=w_rel,
            lengths=lengths.transpose(1, 2, 0).reshape(seqs, micro),
            cot=cotangent.reshape(count, part // 2, width),
        ),
        seq_size,
        grp_size,
    )
    kept.update(weights, dgain2=kept["dgain"])
    *sums, small = backward(kept, seq_size, grp_size)
    small = small.reshape(-1, 128)
    hid, pooled, d_inner, d_outer, d_out, d_query, d_key, d_value, d_rel, d_attn, d_ffn = finish(
        sums, small, w_rel.shape[0], width
    )
    return (
        pooled.reshape(cotangent.shape),
        hid.reshape(hidden.shape),
        d_query,
        d_key,
        d_value,
        d_rel,
        d_out,
        d_attn,
        d_inner,
        d_outer,
        d_ffn,
    )


def solution(mesh):
    rows = P(None, "grp", None, "seq", None)
    spread = P(("seq", "grp"), None)
    sizes = dict(mesh.shape)
    return jax.shard_map(
        functools.partial(local, sizes["seq"], sizes["grp"]),
        mesh=mesh,
        in_specs=(rows, P(None, "grp", None)) + (P(),) * 9 + (rows,),
        out_specs=(
            rows, rows, spread, spread, spread, P(), spread, P(), spread, spread, P()
        ),
        check_vma=False,
    )
```
